32 devices in a mesh: dp: 8 (over z, x), mp: 4 (over y, core).
Axes of the slice: x: 2, y: 2, z: 4, core: 2. Of those that a mesh axis runs over, the one named last changes fastest.
Arguments:
- tokens: float32 [10240, 1024], P(('dp', 'mp')), may hold values from -6 to 6
- cotangent: float32 [10240, 1024], P(('dp', 'mp')), may hold values from -6 to 6
- segments: int32 [10240], P('dp'), may hold values from 0 to 63, as said below
- attention_weights: float32 [2, 4, 1024, 1024], P(None, None, 'dp', 'mp')
- attention_first: float32 [2, 4, 1024, 1024], P(None, None, 'dp', 'mp')
- attention_second: float32 [2, 4, 1024, 1024], P(None, None, 'dp', 'mp')
- dense_weights: float32 [2, 2, 1024, 4096], P(None, None, 'dp', 'mp')
- dense_first: float32 [2, 2, 1024, 4096], P(None, None, 'dp', 'mp')
- dense_second: float32 [2, 2, 1024, 4096], P(None, None, 'dp', 'mp')
- norm_params: float32 [2, 4, 1024], replicated
- norm_first: float32 [2, 4, 1024], replicated
- norm_second: float32 [2, 4, 1024], replicated
Outputs:
- outcome: float32 [10240, 1024], P(('dp', 'mp'))
- grad_tokens: float32 [10240, 1024], P(('dp', 'mp'))
- attention_new: float32 [2, 4, 1024, 1024], P(None, None, 'dp', 'mp')
- attention_first_new: float32 [2, 4, 1024, 1024], P(None, None, 'dp', 'mp')
- attention_second_new: float32 [2, 4, 1024, 1024], P(None, None, 'dp', 'mp')
- attention_copy: bfloat16 [2, 4, 1024, 1024], P(None, None, 'dp', 'mp')
- dense_new: float32 [2, 2, 1024, 4096], P(None, None, 'dp', 'mp')
- dense_first_new: float32 [2, 2, 1024, 4096], P(None, None, 'dp', 'mp')
- dense_second_new: float32 [2, 2, 1024, 4096], P(None, None, 'dp', 'mp')
- dense_copy: bfloat16 [2, 2, 1024, 4096], P(None, None, 'dp', 'mp')
- norm_new: float32 [2, 4, 1024], replicated
- norm_first_new: float32 [2, 4, 1024], replicated
- norm_second_new: float32 [2, 4, 1024], replicated
- norms: float32 [2, 6, 2], replicated
- second_norm_grad: float32 [2, 2, 1024], replicated
The draws below stay inside these ranges and needn't reach their ends.
Inputs may be any that keep to these rules, and one draw needn't show every extreme that they name: `segments`: in each aligned block of 1280 tokens crop numbers start at 0 and never fall; a block holds 2·8 crops of 50 tokens and 6·8 crops of 10 tokens in an order drawn from the seed.
All inputs are finite; a program needn't handle non-finite values.
Results may differ from the reference program's by a relative error of at most 0.029.
Values may be sent and summed in bfloat16 or wider, within the bound.
No kernel may reach another device: no remote copies, remote signals or barrier semaphores. Data moves between devices by JAX's collectives and lax.ppermute only.
A program may use at most 320 MiB of HBM per device.

```python
import jax
import jax.numpy as jnp
from jax import lax

D = 1024
HEADS = 16
HD = 64
FF = 4096
LAYERS = 2
GLOBAL_LEN = 50
LOCAL_LEN = 10
GLOBAL_CROPS = 2
LOCAL_CROPS = 6
STEP = 10
IMG_DEV = 8
TOK_DEV = 1280
TOKENS = 10240


def scaled_matrix(random_base, row_rise, spread):
    return random_base * spread[None, :, None, None] * row_rise[None, None, :, None]


def first_moment(key, full_shape, scale_rows):
    random_base = jnp.clip(jax.random.normal(key, full_shape, jnp.float32), -3.0, 3.0)
    return 0.11 * float(TOKENS) ** 0.5 * scale_rows * random_base


def second_moment(key, full_shape, scale_rows):
    matrix_part = jnp.exp(jax.random.uniform(jax.random.fold_in(key, 1), full_shape[:2], jnp.float32, 0.0, jnp.log(4.0)))
    entry_part = jnp.exp(jax.random.uniform(jax.random.fold_in(key, 2), full_shape, jnp.float32, jnp.log(0.5), jnp.log(2.0)))
    matrix_part = matrix_part.reshape(full_shape[:2] + (1,) * (len(full_shape) - 2))
    return 0.001 * float(TOKENS) * scale_rows * scale_rows * matrix_part * entry_part


def draw_segments(key, part):
    blocks = TOKENS // TOK_DEV
    crop_count = IMG_DEV * (GLOBAL_CROPS + LOCAL_CROPS)
    is_global = (jnp.arange(crop_count, dtype=jnp.int32) < IMG_DEV * GLOBAL_CROPS).astype(jnp.int32)
    block_keys = jax.random.split(key, blocks)

    def shuffle_one(block_key):
        return jax.random.permutation(block_key, is_global)
    shuffled = jax.vmap(shuffle_one)(block_keys)
    length = shuffled * GLOBAL_LEN + (1 - shuffled) * LOCAL_LEN
    starts = jnp.cumsum(length, axis=1) - length
    position = jnp.arange(TOK_DEV, dtype=jnp.int32)
    segment_ids = jnp.sum((starts[:, None, :] <= position[None, :, None]).astype(jnp.int32), axis=2) - 1
    return segment_ids.reshape(TOKENS).astype(jnp.int32)


def draw_attention_weights(key, part):
    full_shape = (LAYERS, 4, D, HEADS * HD)
    place = jnp.arange(D, dtype=jnp.float32) / float(max(D - 1, 1))
    random_base = jnp.clip(jax.random.normal(key, full_shape, jnp.float32), -4.0, 4.0)
    row_rise = (1.0 + 2.0 * place) / jnp.sqrt(13.0 / 3.0)
    spread = jnp.array([D ** (-0.5), D ** (-0.5), D ** (-0.5), (HEADS * HD // 16) ** (-0.5)], jnp.float32)
    return scaled_matrix(random_base, row_rise, spread)


def draw_dense_weights(key, part):
    full_shape = (LAYERS, 2, D, FF)
    place = jnp.arange(D, dtype=jnp.float32) / float(max(D - 1, 1))
    random_base = jnp.clip(jax.random.normal(key, full_shape, jnp.float32), -4.0, 4.0)
    row_rise = (1.0 + 2.0 * place) / jnp.sqrt(13.0 / 3.0)
    spread = jnp.array([D ** (-0.5), (FF / 4.0) ** (-0.5)], jnp.float32)
    return scaled_matrix(random_base, row_rise, spread)


def draw_attention_first(key, part):
    scale_rows = jnp.array([0.7, 0.7, 1.0, 0.3], jnp.float32)[None, :, None, None]
    return first_moment(key, (LAYERS, 4, D, HEADS * HD), scale_rows)


def draw_attention_second(key, part):
    scale_rows = jnp.array([0.7, 0.7, 1.0, 0.3], jnp.float32)[None, :, None, None]
    return second_moment(key, (LAYERS, 4, D, HEADS * HD), scale_rows)


def draw_dense_first(key, part):
    scale_rows = jnp.array([0.6, 0.7], jnp.float32)[None, :, None, None]
    return first_moment(key, (LAYERS, 2, D, FF), scale_rows)


def draw_dense_second(key, part):
    scale_rows = jnp.array([0.6, 0.7], jnp.float32)[None, :, None, None]
    return second_moment(key, (LAYERS, 2, D, FF), scale_rows)


def draw_norm_params(key, part):
    full_shape = (LAYERS, 4, D)
    random_base = jnp.clip(jax.random.normal(key, full_shape, jnp.float32), -4.0, 4.0)
    is_gain = jnp.array([1.0, 0.0, 1.0, 0.0], jnp.float32)[None, :, None]
    return is_gain * (1.0 + 0.15 * random_base) + (1.0 - is_gain) * 0.3 * random_base


def draw_norm_first(key, part):
    scale_rows = jnp.array([2.5, 2.5, 1.2, 1.2], jnp.float32)[None, :, None]
    return first_moment(key, (LAYERS, 4, D), scale_rows)


def draw_norm_second(key, part):
    full_shape = (LAYERS, 4, D)
    scale_rows = jnp.array([2.5, 2.5, 1.2, 1.2], jnp.float32)[None, :, None]
    multiple = jnp.array([1.5, 1.5, 4.0, 4.0], jnp.float32)[None, :, None]
    entry_part = jnp.exp(jax.random.uniform(jax.random.fold_in(key, 2), full_shape, jnp.float32, jnp.log(0.5), jnp.log(2.0)))
    return 0.001 * float(TOKENS) * scale_rows * scale_rows * multiple * entry_part


def block_scale(own_key, dims, shards, least, largest):
    def one(dim, shards_of):
        steps = jax.random.uniform(jax.random.fold_in(jax.random.fold_in(own_key, 6), dim), (shards_of,), jnp.float32, least / len(shards), largest / len(shards))
        return jnp.repeat(jnp.exp(steps), dims[dim] // shards_of).reshape((-1,) + (1,) * (len(dims) - dim - 1))

    factor_of = one(*shards[0])
    for cut in shards[1:]:
        factor_of = factor_of * one(*cut)
    return factor_of


def bell_draw(rng, dims, scale, most, shards=(), kind=jnp.bfloat16):
    values = jax.random.normal(rng, dims, jnp.float32) * scale
    if len(shards) > 0:
        values = block_scale(rng, dims, shards, -0.22, 0.18) * values
    return jnp.clip(values, min=-most, max=most).astype(kind)


def setup_inputs(seed: int = 0) -> dict:
    splits = jax.random.split(jax.random.key(seed), 13)
    return {
        "tokens": bell_draw(splits[0], (TOKENS, D), 1.0, 6.0, ((0, 32),), jnp.float32),
        "cotangent": bell_draw(splits[1], (TOKENS, D), 1.0, 6.0, ((0, 32),), jnp.float32),
        "segments": draw_segments(jax.random.fold_in(splits[12], 71), 0),
        "attention_weights": draw_attention_weights(jax.random.fold_in(splits[12], 71), 0),
        "attention_first": draw_attention_first(jax.random.fold_in(splits[12], 71), 0),
        "attention_second": draw_attention_second(jax.random.fold_in(splits[12], 71), 0),
        "dense_weights": draw_dense_weights(jax.random.fold_in(splits[12], 71), 0),
        "dense_first": draw_dense_first(jax.random.fold_in(splits[12], 71), 0),
        "dense_second": draw_dense_second(jax.random.fold_in(splits[12], 71), 0),
        "norm_params": draw_norm_params(jax.random.fold_in(splits[12], 71), 0),
        "norm_first": draw_norm_first(jax.random.fold_in(splits[12], 71), 0),
        "norm_second": draw_norm_second(jax.random.fold_in(splits[12], 71), 0),
    }


@jax.custom_vjp
def low(v):
    return lax.optimization_barrier(v.astype(jnp.bfloat16)).astype(jnp.float32)

@jax.custom_vjp
def low_back(v):
    return v

def low_keep(v):
    return (low(v), None)

def low_pass(kept, grad):
    return (grad,)

def back_keep(v):
    return (v, None)

def back_low(kept, grad):
    return (low(grad),)
low.defvjp(low_keep, low_pass)
low_back.defvjp(back_keep, back_low)
PRECISE = lax.Precision.HIGHEST
EPS_NORM = 1e-06
BETA_ONE = 0.9
BETA_TWO = 0.999
ADAM_EPS = 1e-06
WEIGHT_DECAY = 0.01
LEARN_RATE = 0.5
MASKED = -1000000000.0

def layer_norm(stream, gain, shift):
    centre = stream - lax.optimization_barrier(jnp.mean(stream, axis=-1, keepdims=True))
    spread = lax.optimization_barrier(jnp.mean(centre * centre, axis=-1, keepdims=True))
    return centre * lax.rsqrt(spread + EPS_NORM) * gain + shift

def attend_block(inputs):
    query, keys_in, values_in, segment_ids = inputs
    scores = low_back(jnp.einsum('qhe,khe->hqk', query, keys_in, precision=PRECISE) * HD ** (-0.5))
    same_crop = segment_ids[:, None] == segment_ids[None, :]
    scores = jnp.where(same_crop[None], scores, MASKED)
    shares = low(jax.nn.softmax(scores, axis=-1))
    return jnp.einsum('hqk,khe->qhe', shares, values_in, precision=PRECISE)

def run_layers(stream, weights_mixer, weights_dense, params, segments):
    token_count = stream.shape[0]
    blocks = token_count // TOK_DEV
    width_all = HEADS * HD
    segment_blocks = segments.reshape(blocks, TOK_DEV)
    for current in range(LAYERS):
        normed = low(layer_norm(stream, params[current, 0], params[current, 1]))
        projected = jnp.einsum('td,sdh->tsh', normed, weights_mixer[current, :3], precision=PRECISE)
        projected = low(low_back(projected))
        shaped = projected.reshape(blocks, TOK_DEV, 3, HEADS, HD)
        attended = lax.map(jax.checkpoint(attend_block), (shaped[:, :, 0], shaped[:, :, 1], shaped[:, :, 2], segment_blocks))
        attended = low(low_back(attended.reshape(token_count, width_all)))
        stream = stream + low_back(jnp.einsum('th,dh->td', attended, weights_mixer[current, 3], precision=PRECISE))
        normed_two = low(layer_norm(stream, params[current, 2], params[current, 3]))
        hidden = low_back(jnp.einsum('td,df->tf', normed_two, weights_dense[current, 0], precision=PRECISE))
        active = low(jax.nn.gelu(hidden, approximate=False))
        stream = stream + low_back(jnp.einsum('tf,df->td', active, weights_dense[current, 1], precision=PRECISE))
    return stream

def adam_part(gradient, weight, first, second, decay):
    first_new = BETA_ONE * first + (1.0 - BETA_ONE) * gradient
    second_new = BETA_TWO * second + (1.0 - BETA_TWO) * gradient * gradient
    step_dir = first_new / (1.0 - BETA_ONE ** STEP) / (jnp.sqrt(second_new / (1.0 - BETA_TWO ** STEP)) + ADAM_EPS) + decay * weight
    return (first_new, second_new, step_dir)

def reference(tokens, cotangent, segments, attention_weights, attention_first, attention_second, dense_weights, dense_first, dense_second, norm_params, norm_first, norm_second):

    def forward(stream, weights_mixer, weights_dense, params):
        return run_layers(stream, weights_mixer, weights_dense, params, segments)
    outcome, pull_back = jax.vjp(forward, tokens, low(attention_weights), low(dense_weights), norm_params)
    grad_tokens, grad_mixer, grad_dense, grad_params = pull_back(cotangent)
    mixer_first, mixer_second, mixer_step = adam_part(grad_mixer, attention_weights, attention_first, attention_second, WEIGHT_DECAY)
    dense_first_new, dense_second_new, dense_step = adam_part(grad_dense, dense_weights, dense_first, dense_second, WEIGHT_DECAY)
    params_first, params_second, params_step = adam_part(grad_params, norm_params, norm_first, norm_second, 0.0)
    mixer_size = jnp.sqrt(lax.optimization_barrier(jnp.sum(attention_weights * attention_weights, axis=(2, 3))))
    mixer_move = jnp.sqrt(lax.optimization_barrier(jnp.sum(mixer_step * mixer_step, axis=(2, 3))))
    mixer_new = attention_weights - LEARN_RATE * (mixer_size / mixer_move)[:, :, None, None] * mixer_step
    dense_size = jnp.sqrt(lax.optimization_barrier(jnp.sum(dense_weights * dense_weights, axis=(2, 3))))
    dense_move = jnp.sqrt(lax.optimization_barrier(jnp.sum(dense_step * dense_step, axis=(2, 3))))
    dense_new = dense_weights - LEARN_RATE * (dense_size / dense_move)[:, :, None, None] * dense_step
    params_size = jnp.sqrt(lax.optimization_barrier(jnp.sum(norm_params * norm_params, axis=-1)))
    params_move = jnp.sqrt(lax.optimization_barrier(jnp.sum(params_step * params_step, axis=-1)))
    params_new = norm_params - LEARN_RATE * (params_size / params_move)[:, :, None] * params_step
    mixer_entries = float(D * HEADS * HD) ** 0.5
    dense_entries = float(D * FF) ** 0.5
    weight_rms = jnp.concatenate([mixer_size / mixer_entries, dense_size / dense_entries], axis=1)
    update_rms = jnp.concatenate([mixer_move / mixer_entries, dense_move / dense_entries], axis=1)
    norms = jnp.stack([weight_rms, update_rms], axis=-1)
    second_norm_grad = grad_params[:, 2:4]
    return (outcome, grad_tokens, mixer_new, mixer_first, mixer_second, mixer_new.astype(jnp.bfloat16), dense_new, dense_first_new, dense_second_new, dense_new.astype(jnp.bfloat16), params_new, params_first, params_second, norms, second_norm_grad)
```

```python
import functools

import jax
import jax.numpy as jnp
from jax import lax
from jax.experimental import pallas as pl
from jax.experimental.pallas import tpu as pltpu
from jax.sharding import PartitionSpec as P

D = 1024
HEADS = 16
HD = 64
FF = 4096
STEP = 10


EPS_NORM = 1e-06
BETA_ONE = 0.9
BETA_TWO = 0.999
ADAM_EPS = 1e-06
WEIGHT_DECAY = 0.01
LEARN_RATE = 0.5
MASKED = -1000000000.0

QUERIES = 128
REACH = 64
WINDOW = QUERIES + 2 * REACH

NT = (((1,), (1,)), ((), ()))
TN = (((0,), (0,)), ((), ()))


def layer_norm(stream, gain, shift):
    centre = stream - jnp.mean(stream, axis=-1, keepdims=True)
    spread = jnp.mean(centre * centre, axis=-1, keepdims=True)
    return centre * lax.rsqrt(spread + EPS_NORM) * gain + shift


def adam_part(gradient, weight, first, second, decay):
    first_new = BETA_ONE * first + (1.0 - BETA_ONE) * gradient
    second_new = BETA_TWO * second + (1.0 - BETA_TWO) * gradient * gradient
    step_dir = (
        first_new
        / (1.0 - BETA_ONE**STEP)
        / (jnp.sqrt(second_new / (1.0 - BETA_TWO**STEP)) + ADAM_EPS)
        + decay * weight
    )
    return (first_new, second_new, step_dir)


def dot(left, right, dims=(((1,), (0,)), ((), ()))):
    return lax.dot_general(left, right, dims, preferred_element_type=jnp.float32)


def head_lanes(rows, width, value):
    lane_head = lax.broadcasted_iota(jnp.int32, (rows, width), 1) // HD
    return [
        jnp.where(lane_head == head, value, 0.0).astype(jnp.float32) for head in range(width // HD)
    ]


def block_shares(query_wide, keys_in, mask):
    heads_here = query_wide.shape[0] // QUERIES
    scores = dot(query_wide, keys_in, NT).reshape(heads_here, QUERIES, WINDOW)
    scores = jnp.where((mask > 0.5)[None], scores, MASKED)
    powered = jnp.exp(scores - jnp.max(scores, axis=-1, keepdims=True))
    shares = powered / jnp.sum(powered, axis=-1, keepdims=True)
    return shares.reshape(heads_here * QUERIES, WINDOW)


def fold_heads(wide, lanes):
    total = wide[:QUERIES] * lanes[0]
    for head in range(1, len(lanes)):
        total += wide[head * QUERIES : (head + 1) * QUERIES] * lanes[head]
    return total


def in_token_order(place_ref, refs, store, start):
    rows = refs[0].shape[0]
    for relative, ref in enumerate(refs):
        block = jnp.bitwise_xor(place_ref[0], relative)
        store[pl.ds(pl.multiple_of(start + block * rows, 16), rows), :] = ref[...]


def attend_kernel(pieces, place_ref, mask_ref, *refs):
    ins, outs, (all_in, all_out) = refs[:pieces], refs[pieces : 2 * pieces], refs[2 * pieces :]
    count, width = all_out.shape
    all_in[:REACH, :] = jnp.zeros((REACH, 3 * width), jnp.bfloat16)
    all_in[REACH + count :, :] = jnp.zeros((REACH, 3 * width), jnp.bfloat16)
    in_token_order(place_ref, ins, all_in, REACH)
    scaled = [lane.astype(jnp.bfloat16) for lane in head_lanes(QUERIES, width, HD ** (-0.5))]
    plain = head_lanes(QUERIES, width, 1.0)

    @pl.loop(0, count // QUERIES)
    def _(block):
        base = pl.multiple_of(block * QUERIES, QUERIES)
        query = all_in[pl.ds(base + REACH, QUERIES), :width]
        keys_in = all_in[pl.ds(base, WINDOW), width : 2 * width]
        values_in = all_in[pl.ds(base, WINDOW), 2 * width :]
        query_wide = jnp.concatenate([query * lane for lane in scaled], axis=0)
        shares = block_shares(query_wide, keys_in, mask_ref[pl.ds(base, QUERIES), :])
        wide = dot(shares.astype(jnp.bfloat16), values_in)
        all_out[pl.ds(base, QUERIES), :] = fold_heads(wide, plain).astype(jnp.bfloat16)

    rows = outs[0].shape[0]
    for relative, out in enumerate(outs):
        block = jnp.bitwise_xor(place_ref[0], relative)
        out[...] = all_out[pl.ds(pl.multiple_of(block * rows, 16), rows), :]


def attend_back_kernel(pieces, place_ref, mask_ref, *refs):
    ins, grads, outs = refs[:pieces], refs[pieces : 2 * pieces], refs[2 * pieces : 3 * pieces]
    all_in, all_grad, query_sum, key_sum, value_sum = refs[3 * pieces :]
    count, width = all_grad.shape
    all_in[:REACH, :] = jnp.zeros((REACH, 3 * width), jnp.bfloat16)
    all_in[REACH + count :, :] = jnp.zeros((REACH, 3 * width), jnp.bfloat16)
    in_token_order(place_ref, ins, all_in, REACH)
    in_token_order(place_ref, grads, all_grad, 0)
    key_sum[...] = jnp.zeros_like(key_sum)
    value_sum[...] = jnp.zeros_like(value_sum)
    scaled = [lane.astype(jnp.bfloat16) for lane in head_lanes(QUERIES, width, HD ** (-0.5))]
    plain_low = [lane.astype(jnp.bfloat16) for lane in head_lanes(QUERIES, width, 1.0)]
    scaled_wide = head_lanes(QUERIES, width, HD ** (-0.5))

    @pl.loop(0, count // QUERIES)
    def _(block):
        base = pl.multiple_of(block * QUERIES, QUERIES)
        query = all_in[pl.ds(base + REACH, QUERIES), :width]
        keys_in = all_in[pl.ds(base, WINDOW), width : 2 * width]
        values_in = all_in[pl.ds(base, WINDOW), 2 * width :]
        grad = all_grad[pl.ds(base, QUERIES), :]
        query_wide = jnp.concatenate([query * lane for lane in scaled], axis=0)
        grad_wide = jnp.concatenate([grad * lane for lane in plain_low], axis=0)
        shares = block_shares(query_wide, keys_in, mask_ref[pl.ds(base, QUERIES), :])
        grad_shares = dot(grad_wide, values_in, NT)
        inner = jnp.sum(grad_shares * shares, axis=-1, keepdims=True)
        grad_scores = (shares * (grad_shares - inner)).astype(jnp.bfloat16)
        query_sum[pl.ds(base, QUERIES), :] = fold_heads(dot(grad_scores, keys_in), scaled_wide)
        key_sum[pl.ds(base, WINDOW), :] += dot(grad_scores, query_wide, TN)
        value_sum[pl.ds(base, WINDOW), :] += dot(shares.astype(jnp.bfloat16), grad_wide, TN)

    rows = outs[0].shape[0]
    for relative, out in enumerate(outs):
        block = jnp.bitwise_xor(place_ref[0], relative)
        start = pl.multiple_of(block * rows, 16)
        out[:, :width] = query_sum[pl.ds(start, rows), :].astype(jnp.bfloat16)
        out[:, width : 2 * width] = key_sum[pl.ds(start + REACH, rows), :].astype(jnp.bfloat16)
        out[:, 2 * width :] = value_sum[pl.ds(start + REACH, rows), :].astype(jnp.bfloat16)


VMEM_SPEC = pl.BlockSpec(memory_space=pltpu.VMEM)
SMEM_SPEC = pl.BlockSpec(memory_space=pltpu.SMEM)


def attend(place, mask, projected):
    pieces = len(projected)
    rows, width = projected[0].shape[0], projected[0].shape[1] // 3
    count = rows * pieces
    return pl.pallas_call(
        functools.partial(attend_kernel, pieces),
        out_shape=[jax.ShapeDtypeStruct((rows, width), jnp.bfloat16)] * pieces,
        in_specs=[SMEM_SPEC] + [VMEM_SPEC] * (1 + pieces),
        out_specs=[VMEM_SPEC] * pieces,
        scratch_shapes=[
            pltpu.VMEM((count + 2 * REACH, 3 * width), jnp.bfloat16),
            pltpu.VMEM((count, width), jnp.bfloat16),
        ],
        compiler_params=pltpu.CompilerParams(vmem_limit_bytes=32 << 20),
        cost_estimate=pl.CostEstimate(
            flops=4 * count * WINDOW * width * width // HD,
            bytes_accessed=count * width * 8 + count * WINDOW * 4,
            transcendentals=count * WINDOW * width // HD,
        ),
        name="attend",
    )(place, mask, *projected)


def attend_back(place, mask, projected, grads):
    pieces = len(projected)
    rows, width = projected[0].shape[0], projected[0].shape[1] // 3
    count = rows * pieces
    return pl.pallas_call(
        functools.partial(attend_back_kernel, pieces),
        out_shape=[jax.ShapeDtypeStruct((rows, 3 * width), jnp.bfloat16)] * pieces,
        in_specs=[SMEM_SPEC] + [VMEM_SPEC] * (1 + 2 * pieces),
        out_specs=[VMEM_SPEC] * pieces,
        scratch_shapes=[
            pltpu.VMEM((count + 2 * REACH, 3 * width), jnp.bfloat16),
            pltpu.VMEM((count, width), jnp.bfloat16),
            pltpu.VMEM((count, width), jnp.float32),
            pltpu.VMEM((count + 2 * REACH, width), jnp.float32),
            pltpu.VMEM((count + 2 * REACH, width), jnp.float32),
        ],
        compiler_params=pltpu.CompilerParams(vmem_limit_bytes=40 << 20),
        cost_estimate=pl.CostEstimate(
            flops=10 * count * WINDOW * width * width // HD,
            bytes_accessed=count * width * 14 + count * WINDOW * 4,
            transcendentals=count * WINDOW * width // HD,
        ),
        name="attend_back",
    )(place, mask, *projected, *grads)


def crop_mask(segments):
    blocks = segments.shape[0] // QUERIES
    edge = jnp.full((REACH,), -1, segments.dtype)
    padded = jnp.concatenate([edge, segments, edge])
    keys_of = jnp.stack([padded[b * QUERIES : b * QUERIES + WINDOW] for b in range(blocks)])
    same = segments.reshape(blocks, QUERIES)[:, :, None] == keys_of[:, None, :]
    return same.astype(jnp.float32).reshape(blocks * QUERIES, WINDOW)


def move_columns(wide, order, back):
    rows, width = wide.shape
    blocks = order.shape[0]
    block = width // blocks
    if block % 128:
        if back:
            order = jnp.argsort(order)
        columns = (order[:, None] * block + jnp.arange(block)[None, :]).reshape(-1)
        return jnp.take(wide, columns, axis=1)

    def copy(order_ref, in_ref, out_ref):
        out_ref[...] = in_ref[...]

    there = lambda t, order_ref: (0, order_ref[t])
    here = lambda t, order_ref: (0, t)
    return pl.pallas_call(
        copy,
        out_shape=jax.ShapeDtypeStruct(wide.shape, wide.dtype),
        grid_spec=pltpu.PrefetchScalarGridSpec(
            num_scalar_prefetch=1,
            grid=(blocks,),
            in_specs=[pl.BlockSpec((rows, block), here if back else there)],
            out_specs=pl.BlockSpec((rows, block), there if back else here),
        ),
        cost_estimate=pl.CostEstimate(
            flops=0, bytes_accessed=2 * wide.size * wide.dtype.itemsize, transcendentals=0
        ),
        name="move_columns",
    )(order, wide)


def digits_of(size):
    sizes = []
    while size > 1:
        digit = 4 if size % 4 == 0 else (2 if size % 2 == 0 else size)
        sizes.append(digit)
        size //= digit
    return sizes


def strides_of(sizes):
    strides, stride = [], 1
    for size in reversed(sizes):
        strides.append(stride)
        stride *= size
    return strides[::-1]


def shift_pairs(total, size, stride, shift):
    pairs = []
    for source in range(total):
        digit = source // stride % size
        pairs.append((source, source + ((digit + shift) % size - digit) * stride))
    return pairs


class Rows:
    def __init__(self, total):
        self.total = total
        self.sizes = digits_of(total)
        self.strides = strides_of(self.sizes)

    def order(self):
        me = lax.axis_index("dp")
        places = jnp.zeros((1,), jnp.int32)
        for size, stride in zip(self.sizes, self.strides):
            digit = me // stride % size
            there = (digit + size - jnp.arange(size)) % size * stride
            places = (there[:, None] + places[None, :]).reshape(-1)
        return places.astype(jnp.int32)

    def gather(self, block):
        for size, stride in zip(self.sizes, self.strides):
            parts = [block] + [
                lax.ppermute(block, "dp", shift_pairs(self.total, size, stride, shift))
                for shift in range(1, size)
            ]
            block = jnp.concatenate(parts, axis=0)
        return block

    def reduce(self, parts):
        for level in reversed(range(len(self.sizes))):
            size, stride = self.sizes[level], self.strides[level]
            total = parts[0].astype(jnp.float32)
            for shift in range(1, size):
                total += lax.ppermute(
                    parts[shift], "dp", shift_pairs(self.total, size, stride, -shift)
                ).astype(jnp.float32)
            if level == 0:
                return total
            low = total.astype(jnp.bfloat16)
            inner = self.sizes[level - 1]
            step = low.shape[0] // inner
            parts = [low[s * step : (s + 1) * step] for s in range(inner)]


def core_swap(values_in):
    return lax.ppermute(values_in, "mp", [(0, 1), (1, 0), (2, 3), (3, 2)])


def chip_swap(values_in):
    return lax.ppermute(values_in, "mp", [(0, 2), (2, 0), (1, 3), (3, 1)])


def spread(mine):
    beyond = chip_swap(mine)
    return [mine, core_swap(mine), beyond, core_swap(beyond)]


def collect(parts):
    half = (parts[2].astype(jnp.float32) + core_swap(parts[3]).astype(jnp.float32)).astype(
        jnp.bfloat16
    )
    near = parts[0].astype(jnp.float32) + core_swap(parts[1]).astype(jnp.float32)
    return near + chip_swap(half).astype(jnp.float32)


def total_everywhere(value, rows_total):
    value = value + core_swap(value)
    value = value + chip_swap(value)
    stride = 1
    while stride < rows_total:
        value = value + lax.ppermute(
            value, "dp", [(source, source ^ stride) for source in range(rows_total)]
        )
        stride *= 2
    return value


def shards(
    rows_total,
    tokens,
    cotangent,
    segments,
    attention_weights,
    attention_first,
    attention_second,
    dense_weights,
    dense_first,
    dense_second,
    norm_params,
    norm_first,
    norm_second,
):
    layers = attention_weights.shape[0]
    width = attention_weights.shape[3]
    rows = Rows(rows_total)
    order = rows.order()
    place = lax.axis_index("mp").astype(jnp.int32).reshape(1)
    mask = crop_mask(segments)
    mixer_low = attention_weights.astype(jnp.bfloat16)
    dense_low = dense_weights.astype(jnp.bfloat16)
    copies = []
    for current in range(layers):
        inputs_own = jnp.concatenate([mixer_low[current, s] for s in range(3)], axis=1)
        copies.append(
            (
                rows.gather(inputs_own),
                rows.gather(mixer_low[current, 3]),
                rows.gather(dense_low[current, 0]),
                rows.gather(dense_low[current, 1]),
            )
        )
    stream = move_columns(tokens, order, False)
    stream_grad = move_columns(cotangent, order, False)
    params_here = move_columns(norm_params.reshape(layers * 4, D), order, False)
    params_here = params_here.reshape(layers, 4, D)
    saved_forward = []
    for current in range(layers):
        inputs_map, output_map, up_map, down_map = copies[current]
        params = params_here[current]
        normed = spread(layer_norm(stream, params[0], params[1]).astype(jnp.bfloat16))
        projected = [dot(piece, inputs_map).astype(jnp.bfloat16) for piece in normed]
        attended = attend(place, mask, projected)
        middle = stream + collect(
            [dot(piece, output_map, NT).astype(jnp.bfloat16) for piece in attended]
        )
        normed_two = spread(layer_norm(middle, params[2], params[3]).astype(jnp.bfloat16))
        active, slope, parts = [], [], []
        for piece in normed_two:
            hidden = dot(piece, up_map)
            below = 0.5 * (1.0 + lax.erf(hidden * (0.5**0.5)))
            density = jnp.exp(-0.5 * hidden * hidden) * 0.3989422804014327
            active.append((hidden * below).astype(jnp.bfloat16))
            slope.append((below + hidden * density).astype(jnp.bfloat16))
            parts.append(dot(active[-1], down_map, NT).astype(jnp.bfloat16))
        after_dense = middle + collect(parts)
        saved_forward.append((stream, normed, projected, attended, middle, normed_two, active, slope))
        stream = after_dense
    outcome = move_columns(stream, order, True)

    states = [None] * layers
    squares_list = [None] * layers
    vector_list = [None] * layers

    def weight_grad(left, right):
        left, right = jnp.concatenate(left, axis=0), jnp.concatenate(right, axis=0)
        groups = rows.sizes[-1]
        step = left.shape[1] // groups
        return rows.reduce(
            [
                dot(left[:, g * step : (g + 1) * step], right, TN).astype(jnp.bfloat16)
                for g in range(groups)
            ]
        )

    for current in reversed(range(layers)):
        stream_in, normed, projected, attended, middle, normed_two, active, slope = saved_forward[
            current
        ]
        inputs_map, output_map, up_map, down_map = copies[current]
        params = params_here[current]
        back_rows = spread(stream_grad.astype(jnp.bfloat16))
        grad_hidden = [
            (dot(piece, down_map) * bend.astype(jnp.float32)).astype(jnp.bfloat16)
            for piece, bend in zip(back_rows, slope)
        ]
        grad_normed_two = collect(
            [dot(piece, up_map, NT).astype(jnp.bfloat16) for piece in grad_hidden]
        )
        grad_down = weight_grad(back_rows, active)
        grad_up = weight_grad(normed_two, grad_hidden)
        _, norm_pull = jax.vjp(layer_norm, middle, params[2], params[3])
        grad_middle, grad_gain_two, grad_shift_two = norm_pull(grad_normed_two)
        stream_grad = stream_grad + grad_middle
        back_rows_two = spread(stream_grad.astype(jnp.bfloat16))
        grad_attended = [dot(piece, output_map).astype(jnp.bfloat16) for piece in back_rows_two]
        grad_projected = attend_back(place, mask, projected, grad_attended)
        grad_normed = collect(
            [dot(piece, inputs_map, NT).astype(jnp.bfloat16) for piece in grad_projected]
        )
        grad_output_map = weight_grad(back_rows_two, attended)
        grad_inputs_map = weight_grad(normed, grad_projected)
        _, norm_pull_one = jax.vjp(layer_norm, stream_in, params[0], params[1])
        grad_inner, grad_gain_one, grad_shift_one = norm_pull_one(grad_normed)
        stream_grad = stream_grad + grad_inner
        mixer_grad = jnp.stack(
            [grad_inputs_map[:, s * width : (s + 1) * width] for s in range(3)] + [grad_output_map]
        )
        dense_grad = jnp.stack([grad_up, grad_down], axis=0)
        mixer_first, mixer_second, mixer_step = adam_part(
            mixer_grad,
            attention_weights[current],
            attention_first[current],
            attention_second[current],
            WEIGHT_DECAY,
        )
        dense_first_new, dense_second_new, dense_step = adam_part(
            dense_grad,
            dense_weights[current],
            dense_first[current],
            dense_second[current],
            WEIGHT_DECAY,
        )
        weight_squares = jnp.concatenate(
            [
                jnp.sum(attention_weights[current] * attention_weights[current], axis=(1, 2)),
                jnp.sum(dense_weights[current] * dense_weights[current], axis=(1, 2)),
            ]
        )
        step_squares = jnp.concatenate(
            [
                jnp.sum(mixer_step * mixer_step, axis=(1, 2)),
                jnp.sum(dense_step * dense_step, axis=(1, 2)),
            ]
        )
        squares_list[current] = jnp.stack([weight_squares, step_squares], axis=-1)
        vector_list[current] = jnp.stack(
            [grad_gain_one, grad_shift_one, grad_gain_two, grad_shift_two], axis=0
        )
        states[current] = (
            mixer_first,
            mixer_second,
            mixer_step,
            dense_first_new,
            dense_second_new,
            dense_step,
        )
    grad_tokens = move_columns(stream_grad, order, True)
    vectors = move_columns(jnp.concatenate(vector_list, axis=0), order, True)
    total_vectors = total_everywhere(vectors, rows_total).reshape(layers, 4, D)
    total_squares = total_everywhere(jnp.stack(squares_list), rows_total)
    sizes_all = jnp.sqrt(total_squares[:, :, 0])
    moves_all = jnp.sqrt(total_squares[:, :, 1])
    trust_all = sizes_all / moves_all
    mixer_new = jnp.stack(
        [
            attention_weights[current]
            - LEARN_RATE * trust_all[current, :4, None, None] * states[current][2]
            for current in range(layers)
        ]
    )
    dense_new = jnp.stack(
        [
            dense_weights[current]
            - LEARN_RATE * trust_all[current, 4:, None, None] * states[current][5]
            for current in range(layers)
        ]
    )
    mixer_first_all = jnp.stack([states[current][0] for current in range(layers)])
    mixer_second_all = jnp.stack([states[current][1] for current in range(layers)])
    dense_first_all = jnp.stack([states[current][3] for current in range(layers)])
    dense_second_all = jnp.stack([states[current][4] for current in range(layers)])
    params_first, params_second, params_step = adam_part(
        total_vectors, norm_params, norm_first, norm_second, 0.0
    )
    params_size = jnp.sqrt(jnp.sum(norm_params * norm_params, axis=-1))
    params_move = jnp.sqrt(jnp.sum(params_step * params_step, axis=-1))
    params_new = norm_params - LEARN_RATE * (params_size / params_move)[:, :, None] * params_step
    mixer_entries = float(D * HEADS * HD) ** 0.5
    dense_entries = float(D * FF) ** 0.5
    entry_roots = jnp.array([mixer_entries] * 4 + [dense_entries] * 2, jnp.float32)
    norms = jnp.stack([sizes_all / entry_roots[None, :], moves_all / entry_roots[None, :]], axis=-1)
    second_norm_grad = total_vectors[:, 2:4]
    return (
        outcome,
        grad_tokens,
        mixer_new,
        mixer_first_all,
        mixer_second_all,
        mixer_new.astype(jnp.bfloat16),
        dense_new,
        dense_first_all,
        dense_second_all,
        dense_new.astype(jnp.bfloat16),
        params_new,
        params_first,
        params_second,
        norms,
        second_norm_grad,
    )


def solution(mesh):
    rows_spec = P(("dp", "mp"), None)
    weight_spec = P(None, None, "dp", "mp")
    in_specs = (rows_spec, rows_spec, P("dp")) + (weight_spec,) * 6 + (P(),) * 3
    out_specs = (rows_spec,) * 2 + (weight_spec,) * 8 + (P(),) * 5
    return jax.shard_map(
        functools.partial(shards, mesh.shape["dp"]),
        mesh=mesh,
        in_specs=in_specs,
        out_specs=out_specs,
        check_vma=False,
    )
```

```python
import functools

import jax
import jax.numpy as jnp
from jax import lax
from jax.experimental import pallas as pl
from jax.experimental.pallas import tpu as pltpu
from jax.sharding import PartitionSpec as P

D = 1024
HEADS = 16
HD = 64
FF = 4096
STEP = 10


EPS_NORM = 1e-06
BETA_ONE = 0.9
BETA_TWO = 0.999
ADAM_EPS = 1e-06
WEIGHT_DECAY = 0.01
LEARN_RATE = 0.5
MASKED = -1000000000.0

QUERIES = 128
REACH = 64
WINDOW = QUERIES + 2 * REACH

NT = (((1,), (1,)), ((), ()))
TN = (((0,), (0,)), ((), ()))


VMEM_SPEC = pl.BlockSpec(memory_space=pltpu.VMEM)
SMEM_SPEC = pl.BlockSpec(memory_space=pltpu.SMEM)
ANY_SPEC = pl.BlockSpec(memory_space=pl.ANY)


def struct(shape, kind=jnp.bfloat16):
    return jax.ShapeDtypeStruct(shape, kind)


class Order:
    def __init__(self):
        self.earlier = []

    def settle(self, value):
        self.earlier = self.earlier + [value]
        return value

    def __call__(
        self, name, body, ins, outs, room, in_specs=None, out_specs=None, grid_spec=None, scratch=(), aliases=None
    ):
        extra = list(self.earlier)
        scalars = 0 if grid_spec is None else grid_spec[0]

        def wrapped(*refs):
            return body(*refs[: len(ins)], *refs[len(ins) + len(extra) :])

        in_specs = (in_specs or [VMEM_SPEC] * len(ins)) + [ANY_SPEC] * len(extra)
        out_specs = out_specs or [VMEM_SPEC] * len(outs)
        size = sum(array.size * jnp.dtype(array.dtype).itemsize for array in (*ins, *outs))
        places = dict(out_shape=outs, in_specs=in_specs, out_specs=out_specs, scratch_shapes=scratch)
        if grid_spec is not None:
            del places["in_specs"], places["out_specs"], places["scratch_shapes"]
            places["grid_spec"] = pltpu.PrefetchScalarGridSpec(
                num_scalar_prefetch=scalars,
                grid=grid_spec[1],
                in_specs=in_specs,
                out_specs=out_specs,
            )
        result = pl.pallas_call(
            wrapped,
            **places,
            input_output_aliases=aliases or {},
            cost_estimate=pl.CostEstimate(flops=size, bytes_accessed=size, transcendentals=0),
            compiler_params=pltpu.CompilerParams(vmem_limit_bytes=room << 20),
            name=name,
        )(*ins, *extra)
        self.earlier = [result[-1]]
        return result


def add_kernel(here, far, out):
    out[...] = (here[...].astype(jnp.float32) + far[...].astype(jnp.float32)).astype(out.dtype)


def add(run, here, far, kind):
    return run("add", add_kernel, [here, far], [struct(here.shape, kind)], 4)[0]


def cast_kernel(*refs):
    out, begin = refs[-1], 0
    for ref in refs[:-1]:
        out[:, begin : begin + ref.shape[1]] = ref[...].astype(out.dtype)
        begin += ref.shape[1]


def cast(run, *parts):
    across = sum(part.shape[1] for part in parts)
    return run("cast", cast_kernel, parts, [struct((parts[0].shape[0], across))], 6)[0]


def join_kernel(here, far, *outs):
    rows, begin = here.shape[0], 0
    for out in outs:
        columns = slice(begin, begin + out.shape[1])
        out[:rows, :] = here[:, columns]
        out[rows:, :] = far[:, columns]
        begin += out.shape[1]


def join(run, here, far, spans):
    outs = [struct((2 * here.shape[0], span)) for span in spans]
    return run("join", join_kernel, [here, far], outs, 10)


def adam_part(gradient, weight, first, second, decay):
    first_new = BETA_ONE * first + (1.0 - BETA_ONE) * gradient
    second_new = BETA_TWO * second + (1.0 - BETA_TWO) * gradient * gradient
    step_dir = (
        first_new
        / (1.0 - BETA_ONE**STEP)
        / (jnp.sqrt(second_new / (1.0 - BETA_TWO**STEP)) + ADAM_EPS)
        + decay * weight
    )
    return (first_new, second_new, step_dir)


def dot(left, right, dims=(((1,), (0,)), ((), ()))):
    return lax.dot_general(left, right, dims, preferred_element_type=jnp.float32)


def head_lanes(rows, width, value):
    lane_head = lax.broadcasted_iota(jnp.int32, (rows, width), 1) // HD
    return [
        jnp.where(lane_head == head, value, 0.0).astype(jnp.float32) for head in range(width // HD)
    ]


def block_shares(query_wide, keys_in, mask):
    heads_here = query_wide.shape[0] // QUERIES
    scores = dot(query_wide, keys_in, NT).reshape(heads_here, QUERIES, WINDOW)
    scores = jnp.where((mask > 0.5)[None], scores, MASKED)
    powered = jnp.exp(scores - jnp.max(scores, axis=-1, keepdims=True))
    shares = powered * (1.0 / jnp.sum(powered, axis=-1, keepdims=True))
    return shares.reshape(heads_here * QUERIES, WINDOW)


def fold_heads(wide, lanes):
    total = wide[:QUERIES] * lanes[0]
    for head in range(1, len(lanes)):
        total += wide[head * QUERIES : (head + 1) * QUERIES] * lanes[head]
    return total


def places_of(place_ref, pieces, rows):
    half = rows // 2
    found = []
    for piece in range(pieces):
        chip, stream = divmod(piece, 2)
        for core in range(2):
            block = jnp.bitwise_xor(place_ref[0], 2 * chip + core)
            found.append((piece, core * half, pl.multiple_of(block * rows + stream * half, 32)))
    return found


def in_token_order(place_ref, refs, store, start):
    rows = refs[0].shape[0]
    for piece, row, token in places_of(place_ref, len(refs), rows):
        store[pl.ds(token + start, rows // 2), :] = refs[piece][pl.ds(row, rows // 2), :]


def attend_kernel(pieces, place_ref, mask_ref, *refs):
    ins, outs, (all_in, all_out) = refs[:pieces], refs[pieces : 2 * pieces], refs[2 * pieces :]
    count, width = all_out.shape
    all_in[:REACH, :] = jnp.zeros((REACH, 3 * width), jnp.bfloat16)
    all_in[REACH + count :, :] = jnp.zeros((REACH, 3 * width), jnp.bfloat16)
    in_token_order(place_ref, ins, all_in, REACH)
    scaled = [lane.astype(jnp.bfloat16) for lane in head_lanes(QUERIES, width, HD ** (-0.5))]
    plain = head_lanes(QUERIES, width, 1.0)

    @pl.loop(0, count // QUERIES, unroll=count // QUERIES)
    def _(block):
        base = pl.multiple_of(block * QUERIES, QUERIES)
        query = all_in[pl.ds(base + REACH, QUERIES), :width]
        keys_in = all_in[pl.ds(base, WINDOW), width : 2 * width]
        values_in = all_in[pl.ds(base, WINDOW), 2 * width :]
        query_wide = jnp.concatenate([query * lane for lane in scaled], axis=0)
        shares = block_shares(query_wide, keys_in, mask_ref[pl.ds(base, QUERIES), :])
        wide = dot(shares.astype(jnp.bfloat16), values_in)
        all_out[pl.ds(base, QUERIES), :] = fold_heads(wide, plain).astype(jnp.bfloat16)

    rows = outs[0].shape[0]
    for piece, row, token in places_of(place_ref, pieces, rows):
        outs[piece][pl.ds(row, rows // 2), :] = all_out[pl.ds(token, rows // 2), :]


def attend_back_kernel(pieces, place_ref, mask_ref, *refs):
    ins, grads, outs = refs[:pieces], refs[pieces : 2 * pieces], refs[2 * pieces : 3 * pieces]
    all_in, all_grad, query_sum, key_sum, value_sum = refs[3 * pieces :]
    count, width = all_grad.shape
    all_in[:REACH, :] = jnp.zeros((REACH, 3 * width), jnp.bfloat16)
    all_in[REACH + count :, :] = jnp.zeros((REACH, 3 * width), jnp.bfloat16)
    in_token_order(place_ref, ins, all_in, REACH)
    in_token_order(place_ref, grads, all_grad, 0)
    key_sum[...] = jnp.zeros_like(key_sum)
    value_sum[...] = jnp.zeros_like(value_sum)
    scaled = [lane.astype(jnp.bfloat16) for lane in head_lanes(QUERIES, width, HD ** (-0.5))]
    plain_low = [lane.astype(jnp.bfloat16) for lane in head_lanes(QUERIES, width, 1.0)]
    scaled_wide = head_lanes(QUERIES, width, HD ** (-0.5))

    @pl.loop(0, count // QUERIES, unroll=count // QUERIES)
    def _(block):
        base = pl.multiple_of(block * QUERIES, QUERIES)
        query = all_in[pl.ds(base + REACH, QUERIES), :width]
        keys_in = all_in[pl.ds(base, WINDOW), width : 2 * width]
        values_in = all_in[pl.ds(base, WINDOW), 2 * width :]
        grad = all_grad[pl.ds(base, QUERIES), :]
        query_wide = jnp.concatenate([query * lane for lane in scaled], axis=0)
        grad_wide = jnp.concatenate([grad * lane for lane in plain_low], axis=0)
        shares = block_shares(query_wide, keys_in, mask_ref[pl.ds(base, QUERIES), :])
        grad_shares = dot(grad_wide, values_in, NT)
        inner = jnp.sum(grad_shares * shares, axis=-1, keepdims=True)
        grad_scores = (shares * (grad_shares - inner)).astype(jnp.bfloat16)
        query_sum[pl.ds(base, QUERIES), :] = fold_heads(dot(grad_scores, keys_in), scaled_wide)
        key_sum[pl.ds(base, WINDOW), :] += dot(grad_scores, query_wide, TN)
        value_sum[pl.ds(base, WINDOW), :] += dot(shares.astype(jnp.bfloat16), grad_wide, TN)

    rows = outs[0].shape[0]
    for piece, row, token in places_of(place_ref, pieces, rows):
        here, there = pl.ds(row, rows // 2), pl.ds(token + REACH, rows // 2)
        out = outs[piece]
        out[here, :width] = query_sum[pl.ds(token, rows // 2), :].astype(jnp.bfloat16)
        out[here, width : 2 * width] = key_sum[there, :].astype(jnp.bfloat16)
        out[here, 2 * width :] = value_sum[there, :].astype(jnp.bfloat16)


def attend(run, place, mask, projected):
    pieces = len(projected)
    rows, width = projected[0].shape[0], projected[0].shape[1] // 3
    count = rows * pieces
    return run(
        "attend",
        functools.partial(attend_kernel, pieces),
        [place, mask, *projected],
        [struct((rows, width))] * pieces,
        12,
        in_specs=[SMEM_SPEC] + [VMEM_SPEC] * (1 + pieces),
        scratch=[
            pltpu.VMEM((count + 2 * REACH, 3 * width), jnp.bfloat16),
            pltpu.VMEM((count, width), jnp.bfloat16),
        ],
    )


def attend_back(run, place, mask, projected, grads):
    pieces = len(projected)
    rows, width = projected[0].shape[0], projected[0].shape[1] // 3
    count = rows * pieces
    return run(
        "attend_back",
        functools.partial(attend_back_kernel, pieces),
        [place, mask, *projected, *grads],
        [struct((rows, 3 * width))] * pieces,
        20,
        in_specs=[SMEM_SPEC] + [VMEM_SPEC] * (1 + 2 * pieces),
        scratch=[
            pltpu.VMEM((count + 2 * REACH, 3 * width), jnp.bfloat16),
            pltpu.VMEM((count, width), jnp.bfloat16),
            pltpu.VMEM((count, width), jnp.float32),
            pltpu.VMEM((count + 2 * REACH, width), jnp.float32),
            pltpu.VMEM((count + 2 * REACH, width), jnp.float32),
        ],
    )


def crop_mask(segments):
    blocks = segments.shape[0] // QUERIES
    edge = jnp.full((REACH,), -1, segments.dtype)
    padded = jnp.concatenate([edge, segments, edge])
    keys_of = jnp.stack([padded[b * QUERIES : b * QUERIES + WINDOW] for b in range(blocks)])
    same = segments.reshape(blocks, QUERIES)[:, :, None] == keys_of[:, None, :]
    return same.astype(jnp.float32).reshape(blocks * QUERIES, WINDOW)


def row_step(count):
    return 32 if count % 32 == 0 else count


def normalised(value):
    centre = value - jnp.mean(value, axis=-1, keepdims=True)
    spread_of = jnp.mean(centre * centre, axis=-1, keepdims=True)
    scale = lax.rsqrt(spread_of + EPS_NORM)
    return centre * scale, scale


def norm_kernel(row, terms, params_ref, value_ref, *refs):
    *term_refs, out_ref, low_ref = refs if terms else (None, *refs)
    step = row_step(value_ref.shape[0])

    @pl.loop(0, value_ref.shape[0] // step, unroll=value_ref.shape[0] // step)
    def _(index):
        here = pl.ds(pl.multiple_of(index * step, step), step)
        value = value_ref[here, :]
        if terms:
            for ref in term_refs:
                value = value + ref[here, :].astype(jnp.float32)
            out_ref[here, :] = value
        gain, shift = params_ref[row : row + 1, :], params_ref[row + 1 : row + 2, :]
        low_ref[here, :] = (normalised(value)[0] * gain + shift).astype(jnp.bfloat16)


def norm(run, params, row, value, *terms):
    wide = [struct(value.shape, jnp.float32)] if terms else []
    result = run(
        "norm",
        functools.partial(norm_kernel, row, len(terms)),
        [params, value, *terms],
        wide + [struct(value.shape)],
        6,
    )
    return result if terms else result[0]


def norm_back_kernel(
    row, params_ref, stream_ref, value_ref, first, second, sums_ref, out_ref, low_ref
):
    step = row_step(value_ref.shape[0])
    width = value_ref.shape[1]
    sums_ref[...] = jnp.zeros_like(sums_ref)

    @pl.loop(0, value_ref.shape[0] // step, unroll=value_ref.shape[0] // step)
    def _(index):
        here = pl.ds(pl.multiple_of(index * step, step), step)
        grad = first[here, :].astype(jnp.float32) + second[here, :].astype(jnp.float32)
        unit, scale = normalised(value_ref[here, :])
        along = grad * unit
        sums_ref[:8, :] += jnp.sum(along.reshape(step // 8, 8, width), axis=0)
        sums_ref[8:, :] += jnp.sum(grad.reshape(step // 8, 8, width), axis=0)
        gain = params_ref[row : row + 1, :]
        pushed = grad * gain
        inner = jnp.mean(pushed * unit, axis=-1, keepdims=True)
        term = scale * (pushed - jnp.mean(pushed, axis=-1, keepdims=True) - unit * inner)
        total = stream_ref[here, :] + term
        out_ref[here, :] = total
        low_ref[here, :] = total.astype(jnp.bfloat16)


def norm_back(run, params, row, stream_grad, value, *terms):
    return run(
        "norm_back",
        functools.partial(norm_back_kernel, row),
        [params, stream_grad, value, *terms],
        [
            struct((16, value.shape[1]), jnp.float32),
            struct(value.shape, jnp.float32),
            struct(value.shape),
        ],
        8,
    )


COLUMNS = 256


def two_halves(both, weights, here):
    first, second = weights
    half = first.shape[0]
    return dot(both[:, :half], first[:, here]) + dot(both[:, half:], second[:, here])


def project_kernel(begin, mine, facing, first, second, out):
    both = jnp.concatenate([mine[...], facing[...]], axis=0)
    for start in range(0, out.shape[1], COLUMNS):
        here = slice(begin + start, begin + start + COLUMNS)
        out[:, start : start + COLUMNS] = two_halves(both, (first, second), here).astype(
            jnp.bfloat16
        )


def project(run, mine, facing, first, second, begin, width):
    outs = [struct((2 * mine.shape[0], width))]
    body = functools.partial(project_kernel, begin)
    return run("project", body, [mine, facing, first, second], outs, 10)[0]


def widen_kernel(mine, facing, first, second, active, slope):
    both = jnp.concatenate([mine[...], facing[...]], axis=0)
    for start in range(0, active.shape[1], COLUMNS):
        here = slice(start, start + COLUMNS)
        hidden = two_halves(both, (first, second), here)
        below = 0.5 + 0.5 * lax.erf(hidden * (0.5**0.5))
        density = jnp.exp(-0.5 * hidden * hidden) * 0.3989422804014327
        active[:, here] = (hidden * below).astype(jnp.bfloat16)
        slope[:, here] = (below + hidden * density).astype(jnp.bfloat16)


def widen(run, mine, facing, first, second):
    outs = [struct((2 * mine.shape[0], first.shape[1]))] * 2
    return run("widen", widen_kernel, [mine, facing, first, second], outs, 10)


def bend_kernel(mine, facing, first, second, slope, out):
    both = jnp.concatenate([mine[...], facing[...]], axis=0)
    for start in range(0, out.shape[1], COLUMNS):
        here = slice(start, start + COLUMNS)
        grad = two_halves(both, (first, second), here)
        out[:, here] = (grad * slope[:, here].astype(jnp.float32)).astype(jnp.bfloat16)


def bend_back(run, mine, facing, first, second, slope):
    return run("bend_back", bend_kernel, [mine, facing, first, second, slope], [struct(slope.shape)], 10)[0]


def narrow_kernel(begin, piece, first, second, kept, sent):
    half = kept.shape[0]
    columns = slice(begin, begin + piece.shape[1])
    for index, weights in enumerate((first, second)):
        for start in range(0, weights.shape[0], COLUMNS):
            there = index * weights.shape[0] + start
            here = slice(there, there + COLUMNS)
            rows = weights[start : start + COLUMNS, columns]
            both = dot(piece[...], rows, NT).astype(jnp.bfloat16)
            kept[:, here] = both[:half]
            sent[:, here] = both[half:]


def narrow(run, piece, first, second, begin):
    outs = [struct((piece.shape[0] // 2, 2 * first.shape[0]))] * 2
    return run("narrow", functools.partial(narrow_kernel, begin), [piece, first, second], outs, 10)


def weight_terms_kernel(counts, columns, *refs):
    ins = refs[: sum(map(sum, counts))]
    kept, sent, all_left, all_right = refs[len(ins) :]
    begin = 0
    for lefts, rights in counts:
        left, right, ins = ins[:lefts], ins[lefts : lefts + rights], ins[lefts + rights :]
        for store, parts in ((all_left, left), (all_right, right)):
            row = 0
            for part in parts:
                store[row : row + part.shape[0], : part.shape[1]] = part[...]
                row += part.shape[0]
        wide = right[0].shape[1]
        for out, spans in zip((sent, kept), columns[::-1]):
            row = 0
            for first, last in spans:
                for start in range(0, wide, COLUMNS):
                    out[row : row + last - first, begin + start : begin + start + COLUMNS] = dot(
                        all_left[:, first:last], all_right[:, start : start + COLUMNS], TN
                    ).astype(jnp.bfloat16)
                row += last - first
        begin += wide


def weight_terms(run, pairs, columns):
    counts = tuple((len(left), len(right)) for left, right in pairs)
    flat = [array for left, right in pairs for array in (*left, *right)]
    total = sum(array.shape[0] for array in pairs[0][0])
    across = sum(right[0].shape[1] for _, right in pairs)
    return run(
        "weight_terms",
        functools.partial(weight_terms_kernel, counts, columns),
        flat,
        [struct((sum(last - first for first, last in spans), across)) for spans in columns],
        24,
        scratch=[
            pltpu.VMEM((total, pairs[0][0][0].shape[1]), jnp.bfloat16),
            pltpu.VMEM((total, max(right[0].shape[1] for _, right in pairs)), jnp.bfloat16),
        ],
    )


def fold_kernel(many, *refs):
    heres, fars, (kept, sent) = refs[:many], refs[many : 2 * many], refs[2 * many :]
    rows = kept.shape[0]
    begin = 0
    for here, far in zip(heres, fars):
        columns = slice(begin, begin + here.shape[1])
        for out, part in ((sent, slice(rows, None)), (kept, slice(0, rows))):
            out[:, columns] = (
                here[part, :].astype(jnp.float32) + far[part, :].astype(jnp.float32)
            ).astype(jnp.bfloat16)
        begin += here.shape[1]


def fold(run, heres, fars):
    across = sum(array.shape[1] for array in heres)
    outs = [struct((heres[0].shape[0] // 2, across))] * 2
    return run("fold", functools.partial(fold_kernel, len(heres)), [*heres, *fars], outs, 12)


def moments_kernel(at, kept, far, weights, first, second, *refs):
    first_new, second_new, step_out, squares = refs[-4:]
    grad = kept[...].astype(jnp.float32) + far[...].astype(jnp.float32)
    weight = weights[...].reshape(grad.shape)
    new_first, new_second, step = adam_part(
        grad, weight, first[...].reshape(grad.shape), second[...].reshape(grad.shape), WEIGHT_DECAY
    )
    for out, value in ((first_new, new_first), (second_new, new_second), (step_out, step)):
        out[...] = value.reshape(out.shape)
    for place, value in enumerate((weight, step)):
        squares[0, place : place + 1, :] = jnp.sum(value * value, axis=0, keepdims=True)


def moments(run, names, layer, kept, far, weights, first, second, before):
    rows, wide = weights.shape[2:]
    spec = pl.BlockSpec((1, 1, rows, wide), lambda n, at: (layer, at[n], 0, 0))
    grad_spec = pl.BlockSpec((rows, wide), lambda n, at: (0, n))
    before = list(before or [])
    return run(
        "moments",
        moments_kernel,
        [jnp.array(names, jnp.int32), kept, far, weights, first, second, *before],
        [struct(weights.shape, jnp.float32)] * 3 + [struct((len(names), 2, wide), jnp.float32)],
        12,
        in_specs=[grad_spec, grad_spec, spec, spec, spec] + [ANY_SPEC] * len(before),
        out_specs=[spec, spec, spec, pl.BlockSpec((1, 2, wide), lambda n, at: (n, 0, 0))],
        grid_spec=(1, (len(names),)),
        aliases={6 + i: i for i in range(len(before))},
    )


def apply_kernel(trust, weights, step, new, low):
    layer, name = pl.program_id(0), pl.program_id(1)
    value = weights[...] - LEARN_RATE * trust[layer, name] * step[...]
    new[...] = value
    low[...] = value.astype(jnp.bfloat16)


def apply(run, trust, weights, step):
    layers, names, rows, wide = weights.shape
    spec = pl.BlockSpec((1, 1, rows, wide), lambda layer, name: (layer, name, 0, 0))
    return run(
        "apply",
        apply_kernel,
        [trust, weights, step],
        [struct(weights.shape, jnp.float32), struct(weights.shape)],
        8,
        in_specs=[SMEM_SPEC, spec, spec],
        out_specs=[spec, spec],
        grid_spec=(0, (layers, names)),
    )


def move_columns(run, wides, order, out_rows, back):
    width, kind = wides[0].shape[1], wides[0].dtype
    blocks = order.shape[0]
    block = width // blocks
    if block % 128:
        if back:
            order = jnp.argsort(order)
        columns = (order[:, None] * block + jnp.arange(block)[None, :]).reshape(-1)
        moved = jnp.take(jnp.concatenate(wides, axis=0), columns, axis=1)
        starts = [sum(out_rows[:i]) for i in range(len(out_rows))]
        return [moved[start : start + rows] for start, rows in zip(starts, out_rows)]

    def copy(order_ref, *refs):
        ins, outs = refs[: len(wides)], refs[len(wides) :]
        step = min(ref.shape[0] for ref in refs)
        for row in range(0, sum(out_rows), step):
            source, target, from_row, to_row = ins, outs, row, row
            index = 0
            while from_row >= source[index].shape[0]:
                from_row -= source[index].shape[0]
                index += 1
            source, index = source[index], 0
            while to_row >= target[index].shape[0]:
                to_row -= target[index].shape[0]
                index += 1
            target = target[index]
            for place in range(blocks):
                there = pl.ds(pl.multiple_of(order_ref[place] * block, 128), block)
                here = pl.ds(place * block, block)
                from_columns, to_columns = (here, there) if back else (there, here)
                target[pl.ds(to_row, step), to_columns] = source[pl.ds(from_row, step), from_columns]

    return run(
        "move_columns",
        copy,
        [order, *wides],
        [struct((rows, width), kind) for rows in out_rows],
        6,
        in_specs=[SMEM_SPEC] + [VMEM_SPEC] * len(wides),
    )


class Rows:
    def __init__(self, total, run):
        self.total, self.run = total, run
        self.strides = [1 << bit for bit in reversed(range(total.bit_length() - 1))]

    def offsets(self):
        places = [0]
        for stride in self.strides:
            places = places + [place ^ stride for place in places]
        return places

    def order(self):
        return jnp.bitwise_xor(
            jnp.array(self.offsets(), jnp.int32), lax.axis_index("dp").astype(jnp.int32)
        )

    def swap(self, values, stride):
        return lax.ppermute(
            values, "dp", [(source, source ^ stride) for source in range(self.total)]
        )

class Gather:
    def __init__(self, rows, spans, *maps):
        self.rows, self.run, self.spans = rows, rows.run, spans
        self.block = cast(self.run, *maps)
        self.there, self.wholes = None, [None] * len(spans)

    def send(self):
        self.there = self.rows.swap(self.block, self.rows.strides[0])

    def take(self):
        for stride in self.rows.strides[1:-1]:
            (self.block,) = join(self.run, self.block, self.there, [self.block.shape[1]])
            if stride == self.rows.strides[-2]:
                return
            self.there = self.rows.swap(self.block, stride)

    def send_near(self):
        self.there = self.rows.swap(self.block, self.rows.strides[-2])

    def take_near(self):
        self.block = join(self.run, self.block, self.there, self.spans)

    def send_last(self, span=0):
        self.wholes[span] = (
            self.block[span],
            self.rows.swap(self.block[span], self.rows.strides[-1]),
        )

    def take_last(self, span=0):
        here, there = self.wholes[span]
        self.wholes[span] = (here, self.run.settle(there))
        return self.wholes[span]


class Reduce:
    def __init__(self, rows):
        self.rows, self.run = rows, rows.run
        self.kept, self.there = [], []

    def send(self, pairs):
        width = pairs[0][0][0].shape[1]
        columns = (((0, width // 2),), ((width // 2, width),))
        keep, away = weight_terms(self.run, pairs, columns)
        self.kept.append(keep)
        self.there.append(self.rows.swap(away, self.rows.strides[-1]))

    def settle(self, group=0):
        self.there[group] = self.run.settle(self.there[group])

    def pass_on(self, level):
        stride = self.rows.strides[-1 - level]
        keep, away = fold(self.run, self.kept, self.there)
        self.kept, self.there = [keep], [self.rows.swap(away, stride)]

    def finish(self):
        for level in range(3, len(self.rows.strides)):
            self.pass_on(level)
        return self.kept[0], self.there[0]


def core_swap(values_in):
    return lax.ppermute(values_in, "mp", [(0, 1), (1, 0), (2, 3), (3, 2)])


def chip_swap(values_in):
    return lax.ppermute(values_in, "mp", [(0, 2), (2, 0), (1, 3), (3, 1)])


def total_everywhere(value, rows_total):
    value = value + core_swap(value)
    value = value + chip_swap(value)
    stride = 1
    while stride < rows_total:
        value = value + lax.ppermute(
            value, "dp", [(source, source ^ stride) for source in range(rows_total)]
        )
        stride *= 2
    return value


def shards(
    rows_total,
    tokens,
    cotangent,
    segments,
    attention_weights,
    attention_first,
    attention_second,
    dense_weights,
    dense_first,
    dense_second,
    norm_params,
    norm_first,
    norm_second,
):
    layers = attention_weights.shape[0]
    width = attention_weights.shape[3]
    run = Order()
    rows = Rows(rows_total, run)
    order = rows.order()
    place = lax.axis_index("mp").astype(jnp.int32).reshape(1)
    count = tokens.shape[0]
    half = count // 2
    both = range(2)

    wide = dense_weights.shape[3]
    settle = run.settle

    def mixer(current, first, last):
        return [attention_weights[current, s] for s in range(first, last)]

    class Exchange:
        def __init__(self):
            self.mine, self.facing = [None, None], [None, None]
            self.beyond, self.beyond_facing = [None, None], [None, None]

        def send(self, part, value):
            self.mine[part] = value
            self.beyond[part] = chip_swap(value)
            self.facing[part] = core_swap(value)

        def near(self, part):
            self.facing[part] = settle(self.facing[part])
            return self.mine[part], self.facing[part]

        def far(self, part):
            self.beyond[part] = settle(self.beyond[part])
            self.beyond_facing[part] = core_swap(self.beyond[part])

        def pieces(self):
            return [
                array
                for near, far in ((self.mine, self.facing), (self.beyond, self.beyond_facing))
                for part in both
                for array in (near[part], far[part])
            ]

    class Collect:
        def __init__(self, weights, begin):
            self.weights, self.begin = weights, begin
            self.near, self.there = [None, None], [None, None]

        def send(self, part, far_piece, near_piece):
            terms = []
            for piece in (far_piece, near_piece):
                kept, sent = narrow(run, piece, *self.weights, self.begin)
                terms.append((kept, core_swap(sent)))
            self.there[part] = chip_swap(add(run, *terms[0], jnp.bfloat16))
            self.near[part] = add(run, *terms[1], jnp.float32)

        def terms(self, part):
            return self.near[part], self.there[part]

    inputs_way = Gather(rows, [3 * width], *mixer(0, 0, 3))
    inputs_way.send()
    output_way = Gather(rows, [width], *mixer(0, 3, 4))
    (params_here,) = move_columns(
        run, [norm_params.reshape(layers * 4, D)], order, [layers * 4], False
    )
    stream = move_columns(run, [tokens], order, [half, half], False)
    normed = Exchange()
    for part in both:
        normed.send(part, norm(run, params_here, 0, stream[part]))
    inputs_way.take()
    inputs_way.send_near()
    output_way.send()
    up_way = Gather(rows, [wide], dense_weights[0, 0])
    down_way = Gather(rows, [wide], dense_weights[0, 1])
    for part in both:
        normed.near(part)
    normed.far(0)
    inputs_way.take_near()
    inputs_way.send_last()
    output_way.take()
    output_way.send_near()
    up_way.send()
    normed.far(1)
    stream_grad = list(move_columns(run, [cotangent], order, [half, half], False))
    back = Exchange()
    back.send(0, cast(run, stream_grad[0]))
    output_way.take_near()
    output_way.send_last()
    mask = crop_mask(segments)
    back.near(0)
    up_way.take()
    up_way.send_near()
    down_way.send()
    back.far(0)
    back.send(1, cast(run, stream_grad[1]))
    inputs_map, inputs_begin = inputs_way.take_last(), 0
    back.near(1)

    mixer_way = Gather(rows, [4 * width], *mixer(1, 0, 4)) if layers > 1 else None
    dense_way = (
        Gather(rows, [wide, wide], dense_weights[1, 0], dense_weights[1, 1]) if layers > 1 else None
    )
    saved_forward, copies = [], []
    for current in range(layers):
        row = 4 * current
        first = current == 0
        projected = [None] * 4

        def project_inputs(*values):
            return project(run, *values, inputs_begin, 3 * width)

        for part in both:
            projected[part] = project_inputs(*normed.near(part), *inputs_map)
        for part in both:
            if not first:
                normed.far(part)
            projected[2 + part] = project_inputs(
                normed.beyond[part], normed.beyond_facing[part], *inputs_map
            )
        if not first:
            dense_way.take_near()
            dense_way.send_last(0)
        attended = attend(run, place, mask, projected)
        if first:
            back.far(1)
            output_map, output_begin = output_way.take_last(), 0
            up_way.take_near()
            up_way.send_last()
            down_way.take()
            down_way.send_near()
        mixed = Collect(output_map, output_begin)
        for part in both:
            mixed.send(part, attended[2 + part], attended[part])
        if first:
            mixer_way.send()
            down_way.take_near()
        middle, normed_two = [None] * 2, Exchange()
        active, slope = [None] * 4, [None] * 4
        for part in both:
            middle[part], low = norm(run, params_here, row + 2, stream[part], *mixed.terms(part))
            normed_two.send(part, low)
            normed_two.near(part)
        if first:
            mixer_way.take()
            mixer_way.send_near()
            up_map = up_way.take_last()
            down_way.send_last()
        else:
            up_map = dense_way.take_last(0)
            dense_way.send_last(1)
        for part in both:
            active[part], slope[part] = widen(run, *normed_two.near(part), *up_map)
        for part in both:
            normed_two.far(part)
            if first and part == 0:
                mixer_way.take_near()
                dense_way.send()
            active[2 + part], slope[2 + part] = widen(
                run, normed_two.beyond[part], normed_two.beyond_facing[part], *up_map
            )
        if first:
            down_map = down_way.take_last()
            mixer_way.send_last()
        else:
            down_map = dense_way.take_last(1)
        saved_forward.append((stream, normed, projected, attended, middle, normed_two, active, slope))
        copies.append((inputs_map, inputs_begin, output_map, output_begin, up_map, down_map))
        if current + 1 < layers:
            widened = Collect(down_map, 0)
            for part in both:
                widened.send(part, active[2 + part], active[part])
            dense_way.take()
            dense_way.send_near()
            stream, normed = [None, None], Exchange()
            for part in both:
                stream[part], low = norm(
                    run, params_here, row + 4, middle[part], *widened.terms(part)
                )
                normed.send(part, low)
                normed.near(part)
            inputs_map = mixer_way.take_last()
            output_map, inputs_begin, output_begin = inputs_map, 0, 3 * width

    dense_grads, mixer_grads = [None] * layers, [None] * layers
    vector_list = [[None, None] for _ in range(layers)]
    mixer_state, dense_state = None, None
    squares_list = [[None] * 6 for _ in range(layers)]

    def dense_moments(current, names, reduced):
        nonlocal dense_state
        *dense_state, squares = moments(
            run, names, current, *reduced.finish(),
            dense_weights, dense_first, dense_second, dense_state,
        )
        for place, name in enumerate(names):
            squares_list[current][4 + name] = squares[place]

    def mixer_moments(current, reduced):
        nonlocal mixer_state
        *mixer_state, squares = moments(
            run, (0, 1, 2, 3), current, *reduced.finish(),
            attention_weights, attention_first, attention_second, mixer_state,
        )
        for name in range(4):
            squares_list[current][name] = squares[name]

    def eight_rows(vectors):
        total = vectors[0] + vectors[1]
        return jnp.sum(total.reshape(2, 8, D), axis=1)

    for current in reversed(range(layers)):
        row = 4 * current
        newest = current == layers - 1
        stream_in, normed, projected, attended, middle, normed_two, active, slope = saved_forward[
            current
        ]
        inputs_map, inputs_begin, output_map, output_begin, up_map, down_map = copies[current]
        grad_hidden = [None] * 4
        for part in both:
            grad_hidden[part] = bend_back(run, *back.near(part), *down_map, slope[part])
        if not newest:
            mixer_grads[current + 1].settle()
            mixer_grads[current + 1].pass_on(1)
        for part in both:
            if not newest:
                back.far(part)
            grad_hidden[2 + part] = bend_back(
                run, back.beyond[part], back.beyond_facing[part], *down_map, slope[2 + part],
            )
        raised = Collect(up_map, 0)
        for part in both:
            raised.send(part, grad_hidden[2 + part], grad_hidden[part])
        if not newest:
            dense_grads[current + 1].pass_on(2)
        dense_grads[current] = [Reduce(rows), Reduce(rows)]
        dense_grads[current][0].send([(back.pieces(), active)])
        vectors = [None, None]
        turned = Exchange()
        for part in both:
            vectors[part], stream_grad[part], low = norm_back(
                run,
                params_here,
                row + 2,
                stream_grad[part],
                middle[part],
                *raised.terms(part),
            )
            turned.send(part, low)
            turned.near(part)
            if part == 0:
                if newest:
                    dense_grads[current][0].send([(normed_two.pieces(), grad_hidden)])
                else:
                    mixer_grads[current + 1].pass_on(2)
        if not newest:
            dense_grads[current][1].send([(normed_two.pieces(), grad_hidden)])
        vector_list[current][1] = eight_rows(vectors)
        grad_attended = [None] * 4

        def project_back(*values):
            return project(run, *values, output_begin, width)

        for part in both:
            grad_attended[part] = project_back(*turned.near(part), *output_map)
        for part in both:
            turned.far(part)
            grad_attended[2 + part] = project_back(
                turned.beyond[part], turned.beyond_facing[part], *output_map
            )
        if newest:
            dense_grads[current][0].settle(0)
        else:
            dense_moments(current + 1, (1, 0), dense_grads[current + 1])
            dense_grads[current][0].pass_on(1)
        grad_projected = attend_back(run, place, mask, projected, grad_attended)
        lowered = Collect(inputs_map, inputs_begin)
        for part in both:
            lowered.send(part, grad_projected[2 + part], grad_projected[part])
        if newest:
            dense_grads[current] = dense_grads[current][0]
            dense_grads[current].settle(1)
            dense_grads[current].pass_on(1)
        else:
            mixer_moments(current + 1, mixer_grads[current + 1])
            dense_grads[current][0].pass_on(2)
        mixer_grads[current] = Reduce(rows)
        mixer_grads[current].send([(normed.pieces(), grad_projected), (turned.pieces(), attended)])
        back = Exchange()
        for part in both:
            vectors[part], stream_grad[part], low = norm_back(
                run,
                params_here,
                row,
                stream_grad[part],
                stream_in[part],
                *lowered.terms(part),
            )
            if current:
                back.send(part, low)
                back.near(part)
        vector_list[current][0] = eight_rows(vectors)

    dense_grads[0][1].pass_on(1)
    dense_moments(0, (1,), dense_grads[0][0])
    widened = Collect(copies[-1][5], 0)
    active, middle = saved_forward[-1][6], saved_forward[-1][4]
    for part in both:
        widened.send(part, active[2 + part], active[part])
    (grad_tokens,) = move_columns(run, stream_grad, order, [count], True)
    vector_rows = [pair for entry in vector_list for pair in entry]
    (vectors,) = move_columns(
        run, [jnp.concatenate(vector_rows)], order, [layers * 4], True
    )
    dense_grads[0][1].pass_on(2)
    mixer_grads[0].settle()
    mixer_grads[0].pass_on(1)

    def finish(*values):
        parts = [
            values[i] + (values[i + 1] + values[i + 2].astype(jnp.float32)) for i in (0, 3)
        ]
        return move_columns(run, parts, order, [count], True)

    (outcome,) = finish(middle[0], *widened.terms(0), middle[1], *widened.terms(1))
    mixer_grads[0].pass_on(2)
    dense_moments(0, (0,), dense_grads[0][1])
    total_vectors = total_everywhere(vectors, rows_total).reshape(layers, 4, D)
    mixer_moments(0, mixer_grads[0])
    total_squares = total_everywhere(
        jnp.stack(
            [jnp.sum(value, axis=1) for entry in squares_list for value in entry]
        ).reshape(layers, 6, 2),
        rows_total,
    )
    sizes_all = jnp.sqrt(total_squares[:, :, 0])
    moves_all = jnp.sqrt(total_squares[:, :, 1])
    trust_all = sizes_all / moves_all
    mixer_new, mixer_copy = apply(run, trust_all[:, :4], attention_weights, mixer_state[2])
    dense_new, dense_copy = apply(run, trust_all[:, 4:], dense_weights, dense_state[2])
    params_first, params_second, params_step = adam_part(
        total_vectors, norm_params, norm_first, norm_second, 0.0
    )
    params_size = jnp.sqrt(jnp.sum(norm_params * norm_params, axis=-1))
    params_move = jnp.sqrt(jnp.sum(params_step * params_step, axis=-1))
    params_new = norm_params - LEARN_RATE * (params_size / params_move)[:, :, None] * params_step
    mixer_entries = float(D * HEADS * HD) ** 0.5
    dense_entries = float(D * FF) ** 0.5
    entry_roots = jnp.array([mixer_entries] * 4 + [dense_entries] * 2, jnp.float32)
    norms = jnp.stack([sizes_all / entry_roots[None, :], moves_all / entry_roots[None, :]], axis=-1)
    second_norm_grad = total_vectors[:, 2:4]
    return (
        outcome,
        grad_tokens,
        mixer_new,
        mixer_state[0],
        mixer_state[1],
        mixer_copy,
        dense_new,
        dense_state[0],
        dense_state[1],
        dense_copy,
        params_new,
        params_first,
        params_second,
        norms,
        second_norm_grad,
    )


def solution(mesh):
    rows_spec = P(("dp", "mp"), None)
    weight_spec = P(None, None, "dp", "mp")
    in_specs = (rows_spec, rows_spec, P("dp")) + (weight_spec,) * 6 + (P(),) * 3
    out_specs = (rows_spec,) * 2 + (weight_spec,) * 8 + (P(),) * 5
    return jax.shard_map(
        functools.partial(shards, mesh.shape["dp"]),
        mesh=mesh,
        in_specs=in_specs,
        out_specs=out_specs,
        check_vma=False,
    )
```

```python
import functools

import jax
import jax.numpy as jnp
from jax import lax
from jax.experimental import pallas as pl
from jax.experimental.pallas import tpu as pltpu
from jax.sharding import PartitionSpec as P

D = 1024
HEADS = 16
HD = 64
FF = 4096
STEP = 10


EPS_NORM = 1e-06
BETA_ONE = 0.9
BETA_TWO = 0.999
ADAM_EPS = 1e-06
WEIGHT_DECAY = 0.01
LEARN_RATE = 0.5
MASKED = -1000000000.0

QUERIES = 128
REACH = 64
WINDOW = QUERIES + 2 * REACH

NT = (((1,), (1,)), ((), ()))
TN = (((0,), (0,)), ((), ()))


VMEM_SPEC = pl.BlockSpec(memory_space=pltpu.VMEM)
SMEM_SPEC = pl.BlockSpec(memory_space=pltpu.SMEM)
ANY_SPEC = pl.BlockSpec(memory_space=pl.ANY)


def struct(shape, kind=jnp.bfloat16):
    return jax.ShapeDtypeStruct(shape, kind)


TOKEN = struct((8, 128), jnp.float32)


class Order:
    def __init__(self):
        self.token, self.earlier = None, []

    def settle(self, value):
        self.earlier = self.earlier + [value]
        return value

    def mark(self):
        self("mark", lambda: None, [], [], 2)

    def __call__(
        self, name, body, ins, outs, room, in_specs=None, out_specs=None, grid_spec=None, scratch=(), aliases=None
    ):
        before = [] if self.token is None else [self.token]
        extra = before + list(self.earlier)
        scalars = 0 if grid_spec is None else grid_spec[0]

        def wrapped(*refs):
            token = refs[len(ins) + len(extra) + len(outs)]
            token[...] = jnp.zeros(TOKEN.shape, TOKEN.dtype)
            refs = refs[: len(ins)] + refs[len(ins) + len(extra) :]
            return body(*refs[: len(ins) + len(outs)], *refs[len(ins) + len(outs) + 1 :])

        if grid_spec is None:
            token_spec = VMEM_SPEC
        else:
            token_spec = pl.BlockSpec(TOKEN.shape, lambda *grid: (0, 0))
        in_specs = (in_specs or [VMEM_SPEC] * len(ins)) + [token_spec] * len(before)
        in_specs = in_specs + [ANY_SPEC] * len(self.earlier)
        out_specs = (out_specs or [VMEM_SPEC] * len(outs)) + [token_spec]
        if grid_spec is None:
            places = dict(in_specs=in_specs, out_specs=out_specs, scratch_shapes=scratch)
        else:
            places = dict(
                grid_spec=pltpu.PrefetchScalarGridSpec(
                    num_scalar_prefetch=scalars,
                    grid=grid_spec[1],
                    in_specs=in_specs,
                    out_specs=out_specs,
                )
            )
        *result, self.token = pl.pallas_call(
            wrapped,
            out_shape=[*outs, TOKEN],
            **places,
            input_output_aliases=aliases or {},
            cost_estimate=pl.CostEstimate(flops=1, bytes_accessed=1, transcendentals=0),
            compiler_params=pltpu.CompilerParams(vmem_limit_bytes=room << 20),
            name=name,
        )(*ins, *extra)
        self.earlier = []
        return result


def add(run, here, far, kind, *more):
    body = functools.partial(sum_kernel, 2 + len(more))
    return run("add", body, [here, far, *more], [struct(here.shape, kind)], 4)[0]


def sum_kernel(count, *refs):
    total = refs[0][...].astype(jnp.float32)
    for ref in refs[1:count]:
        total = total + ref[...].astype(jnp.float32)
    refs[-1][...] = total.astype(refs[-1].dtype)


def add_halves_kernel(kept, first, second, out):
    half = first.shape[0]
    for here, part in ((slice(0, half), first), (slice(half, None), second)):
        total = kept[here, :].astype(jnp.float32) + part[...].astype(jnp.float32)
        out[here, :] = total.astype(out.dtype)


def add_halves(run, kept, parts, kind):
    return run("add", add_halves_kernel, [kept, *parts], [struct(kept.shape, kind)], 6)[0]


def cast_kernel(ref, out, first, second):
    low = ref[...].astype(out.dtype)
    out[...] = low
    first[...] = low[: first.shape[0]]
    second[...] = low[first.shape[0] :]


def cast(run, wide):
    rows, width = wide.shape
    outs = [struct((rows, width)), *[struct((rows // 2, width))] * 2]
    low, *parts = run("cast", cast_kernel, [wide], outs, 6)
    return low, parts


def block_kernel(ref, out):
    out[...] = ref[...].reshape(out.shape).astype(out.dtype)


def cast_blocks(run, weights, layer, first, last):
    rows, wide = weights.shape[2:]
    return run(
        "cast",
        block_kernel,
        [weights],
        [struct((rows, (last - first) * wide))],
        6,
        in_specs=[pl.BlockSpec((1, 1, rows, wide), lambda n: (layer, first + n, 0, 0))],
        out_specs=[pl.BlockSpec((rows, wide), lambda n: (0, n))],
        grid_spec=(0, (last - first,)),
    )[0]


def join_kernel(begin, here, far, out):
    rows = here.shape[0]
    columns = slice(begin, begin + out.shape[1])
    out[:rows, :] = here[:, columns]
    out[rows:, :] = far[:, columns]


def join(run, here, far, begin, width):
    outs = [struct((2 * here.shape[0], width))]
    return run("join", functools.partial(join_kernel, begin), [here, far], outs, 10)[0]


def adam_part(gradient, weight, first, second, decay):
    first_new = BETA_ONE * first + (1.0 - BETA_ONE) * gradient
    second_new = BETA_TWO * second + (1.0 - BETA_TWO) * gradient * gradient
    step_dir = (
        first_new
        / (1.0 - BETA_ONE**STEP)
        / (jnp.sqrt(second_new / (1.0 - BETA_TWO**STEP)) + ADAM_EPS)
        + decay * weight
    )
    return (first_new, second_new, step_dir)


def dot(left, right, dims=(((1,), (0,)), ((), ()))):
    return lax.dot_general(left, right, dims, preferred_element_type=jnp.float32)


def head_lanes(rows, width, value):
    lane_head = lax.broadcasted_iota(jnp.int32, (rows, width), 1) // HD
    return [
        jnp.where(lane_head == head, value, 0.0).astype(jnp.float32) for head in range(width // HD)
    ]


def block_shares(query_wide, keys_in, mask):
    heads_here = query_wide.shape[0] // QUERIES
    scores = dot(query_wide, keys_in, NT).reshape(heads_here, QUERIES, WINDOW)
    scores = jnp.where((mask > 0.5)[None], scores, MASKED)
    powered = jnp.exp(scores - jnp.max(scores, axis=-1, keepdims=True))
    shares = powered * (1.0 / jnp.sum(powered, axis=-1, keepdims=True))
    return shares.reshape(heads_here * QUERIES, WINDOW)


def fold_heads(wide, lanes):
    total = wide[:QUERIES] * lanes[0]
    for head in range(1, len(lanes)):
        total += wide[head * QUERIES : (head + 1) * QUERIES] * lanes[head]
    return total


def places_of(place_ref, pieces, rows):
    half = rows // 2
    found = []
    for piece in range(pieces):
        for core in range(2):
            block = jnp.bitwise_xor(place_ref[0], 2 * piece + core)
            found.append((piece, core * half, pl.multiple_of(block * half, 32)))
    return found


def in_token_order(place_ref, refs, store, start):
    rows = refs[0].shape[0]
    for piece, row, token in places_of(place_ref, len(refs), rows):
        store[pl.ds(token + start, rows // 2), :] = refs[piece][pl.ds(row, rows // 2), :]


def attend_kernel(pieces, place_ref, mask_ref, *refs):
    ins, outs, (all_in, all_out) = refs[:pieces], refs[pieces : 2 * pieces], refs[2 * pieces :]
    count, width = all_out.shape
    all_in[:REACH, :] = jnp.zeros((REACH, 3 * width), jnp.bfloat16)
    all_in[REACH + count :, :] = jnp.zeros((REACH, 3 * width), jnp.bfloat16)
    in_token_order(place_ref, ins, all_in, REACH)
    scaled = [lane.astype(jnp.bfloat16) for lane in head_lanes(QUERIES, width, HD ** (-0.5))]
    plain = head_lanes(QUERIES, width, 1.0)

    @pl.loop(0, count // QUERIES, unroll=count // QUERIES)
    def _(block):
        base = pl.multiple_of(block * QUERIES, QUERIES)
        query = all_in[pl.ds(base + REACH, QUERIES), :width]
        keys_in = all_in[pl.ds(base, WINDOW), width : 2 * width]
        values_in = all_in[pl.ds(base, WINDOW), 2 * width :]
        query_wide = jnp.concatenate([query * lane for lane in scaled], axis=0)
        shares = block_shares(query_wide, keys_in, mask_ref[pl.ds(base, QUERIES), :])
        wide = dot(shares.astype(jnp.bfloat16), values_in)
        all_out[pl.ds(base, QUERIES), :] = fold_heads(wide, plain).astype(jnp.bfloat16)

    rows = outs[0].shape[0]
    for piece, row, token in places_of(place_ref, pieces, rows):
        outs[piece][pl.ds(row, rows // 2), :] = all_out[pl.ds(token, rows // 2), :]


def attend_back_kernel(pieces, place_ref, mask_ref, *refs):
    ins, grads, outs = refs[:pieces], refs[pieces : 2 * pieces], refs[2 * pieces : 3 * pieces]
    all_in, all_grad, query_sum, key_sum, value_sum = refs[3 * pieces :]
    count, width = all_grad.shape
    all_in[:REACH, :] = jnp.zeros((REACH, 3 * width), jnp.bfloat16)
    all_in[REACH + count :, :] = jnp.zeros((REACH, 3 * width), jnp.bfloat16)
    in_token_order(place_ref, ins, all_in, REACH)
    in_token_order(place_ref, grads, all_grad, 0)
    key_sum[...] = jnp.zeros_like(key_sum)
    value_sum[...] = jnp.zeros_like(value_sum)
    scaled = [lane.astype(jnp.bfloat16) for lane in head_lanes(QUERIES, width, HD ** (-0.5))]
    plain_low = [lane.astype(jnp.bfloat16) for lane in head_lanes(QUERIES, width, 1.0)]
    scaled_wide = head_lanes(QUERIES, width, HD ** (-0.5))

    @pl.loop(0, count // QUERIES, unroll=count // QUERIES)
    def _(block):
        base = pl.multiple_of(block * QUERIES, QUERIES)
        query = all_in[pl.ds(base + REACH, QUERIES), :width]
        keys_in = all_in[pl.ds(base, WINDOW), width : 2 * width]
        values_in = all_in[pl.ds(base, WINDOW), 2 * width :]
        grad = all_grad[pl.ds(base, QUERIES), :]
        query_wide = jnp.concatenate([query * lane for lane in scaled], axis=0)
        grad_wide = jnp.concatenate([grad * lane for lane in plain_low], axis=0)
        shares = block_shares(query_wide, keys_in, mask_ref[pl.ds(base, QUERIES), :])
        grad_shares = dot(grad_wide, values_in, NT)
        inner = jnp.sum(grad_shares * shares, axis=-1, keepdims=True)
        grad_scores = (shares * (grad_shares - inner)).astype(jnp.bfloat16)
        query_sum[pl.ds(base, QUERIES), :] = fold_heads(dot(grad_scores, keys_in), scaled_wide)
        key_sum[pl.ds(base, WINDOW), :] += dot(grad_scores, query_wide, TN)
        value_sum[pl.ds(base, WINDOW), :] += dot(shares.astype(jnp.bfloat16), grad_wide, TN)

    rows = outs[0].shape[0]
    for piece, row, token in places_of(place_ref, pieces, rows):
        here, there = pl.ds(row, rows // 2), pl.ds(token + REACH, rows // 2)
        out = outs[piece]
        out[here, :width] = query_sum[pl.ds(token, rows // 2), :].astype(jnp.bfloat16)
        out[here, width : 2 * width] = key_sum[there, :].astype(jnp.bfloat16)
        out[here, 2 * width :] = value_sum[there, :].astype(jnp.bfloat16)


def attend(run, place, mask, projected):
    pieces = len(projected)
    rows, width = projected[0].shape[0], projected[0].shape[1] // 3
    count = rows * pieces
    return run(
        "attend",
        functools.partial(attend_kernel, pieces),
        [place, mask, *projected],
        [struct((rows, width))] * pieces,
        12,
        in_specs=[SMEM_SPEC] + [VMEM_SPEC] * (1 + pieces),
        scratch=[
            pltpu.VMEM((count + 2 * REACH, 3 * width), jnp.bfloat16),
            pltpu.VMEM((count, width), jnp.bfloat16),
        ],
    )


def attend_back(run, place, mask, projected, grads):
    pieces = len(projected)
    rows, width = projected[0].shape[0], projected[0].shape[1] // 3
    count = rows * pieces
    return run(
        "attend_back",
        functools.partial(attend_back_kernel, pieces),
        [place, mask, *projected, *grads],
        [struct((rows, 3 * width))] * pieces,
        20,
        in_specs=[SMEM_SPEC] + [VMEM_SPEC] * (1 + 2 * pieces),
        scratch=[
            pltpu.VMEM((count + 2 * REACH, 3 * width), jnp.bfloat16),
            pltpu.VMEM((count, width), jnp.bfloat16),
            pltpu.VMEM((count, width), jnp.float32),
            pltpu.VMEM((count + 2 * REACH, width), jnp.float32),
            pltpu.VMEM((count + 2 * REACH, width), jnp.float32),
        ],
    )


def crop_mask(segments):
    blocks = segments.shape[0] // QUERIES
    edge = jnp.full((REACH,), -1, segments.dtype)
    padded = jnp.concatenate([edge, segments, edge])
    keys_of = jnp.stack([padded[b * QUERIES : b * QUERIES + WINDOW] for b in range(blocks)])
    same = segments.reshape(blocks, QUERIES)[:, :, None] == keys_of[:, None, :]
    return same.astype(jnp.float32).reshape(blocks * QUERIES, WINDOW)


def row_step(count):
    return 32 if count % 32 == 0 else count


def normalised(value):
    centre = value - jnp.mean(value, axis=-1, keepdims=True)
    spread_of = jnp.mean(centre * centre, axis=-1, keepdims=True)
    scale = lax.rsqrt(spread_of + EPS_NORM)
    return centre * scale, scale


def norm_kernel(row, terms, params_ref, value_ref, *refs):
    *outs, all_low, first_low, second_low = refs[terms:]
    half = first_low.shape[0]
    step = row_step(half)
    gain, shift = params_ref[row : row + 1, :], params_ref[row + 1 : row + 2, :]
    for start in range(0, 2 * half, step):
        here = slice(start, start + step)
        value = value_ref[here, :]
        if terms:
            value = value + refs[0][here, :].astype(jnp.float32)
            value = value + refs[1][here, :].astype(jnp.float32)
            outs[0][here, :] = value
        low = (normalised(value)[0] * gain + shift).astype(jnp.bfloat16)
        all_low[here, :] = low
        if start < half:
            first_low[here, :] = low
        else:
            second_low[start - half : start - half + step, :] = low


def norm(run, params, row, value, *terms):
    wide = [struct(value.shape, jnp.float32)] if terms else []
    low = [struct(value.shape), *[struct((value.shape[0] // 2, value.shape[1]))] * 2]
    body = functools.partial(norm_kernel, row, len(terms))
    *stream, whole, first, second = run("norm", body, [params, value, *terms], wide + low, 6)
    return (*stream, (whole, [first, second]))


def norm_back_kernel(
    row, params_ref, stream_ref, value_ref, near, far, sums_ref, out_ref, all_low, first_low, second_low
):
    half = first_low.shape[0]
    step = row_step(half)
    width = value_ref.shape[1]
    gain = params_ref[row : row + 1, :]
    sums_ref[...] = jnp.zeros_like(sums_ref)
    for start in range(0, 2 * half, step):
        here = slice(start, start + step)
        grad = near[here, :].astype(jnp.float32) + far[here, :].astype(jnp.float32)
        unit, scale = normalised(value_ref[here, :])
        along = grad * unit
        sums_ref[:8, :] += jnp.sum(along.reshape(step // 8, 8, width), axis=0)
        sums_ref[8:, :] += jnp.sum(grad.reshape(step // 8, 8, width), axis=0)
        pushed = grad * gain
        inner = jnp.mean(pushed * unit, axis=-1, keepdims=True)
        term = scale * (pushed - jnp.mean(pushed, axis=-1, keepdims=True) - unit * inner)
        total = stream_ref[here, :] + term
        out_ref[here, :] = total
        low = total.astype(jnp.bfloat16)
        all_low[here, :] = low
        if start < half:
            first_low[here, :] = low
        else:
            second_low[start - half : start - half + step, :] = low


def norm_back(run, params, row, stream_grad, value, *terms):
    sums, stream, whole, first, second = run(
        "norm_back",
        functools.partial(norm_back_kernel, row),
        [params, stream_grad, value, *terms],
        [
            struct((16, value.shape[1]), jnp.float32),
            struct(value.shape, jnp.float32),
            struct(value.shape),
            *[struct((value.shape[0] // 2, value.shape[1]))] * 2,
        ],
        8,
    )
    return sums, stream, (whole, [first, second])


COLUMNS = 256


def two_halves(both, weights, here):
    first, second = weights
    half = first.shape[0]
    return dot(both[:, :half], first[:, here]) + dot(both[:, half:], second[:, here])


def project_kernel(begin, a, b, c, first, second, out):
    both = jnp.concatenate([a[...], b[...], c[...]], axis=0)
    for start in range(0, out.shape[1], COLUMNS):
        here = slice(begin + start, begin + start + COLUMNS)
        out[:, start : start + COLUMNS] = two_halves(both, (first, second), here).astype(
            jnp.bfloat16
        )


def project(run, piece, first, second, begin, width):
    outs = [struct((sum(part.shape[0] for part in piece), width))]
    body = functools.partial(project_kernel, begin)
    return run("project", body, [*piece, first, second], outs, 14)[0]


def widen_kernel(begin, a, b, c, first, second, active, slope):
    both = jnp.concatenate([a[...], b[...], c[...]], axis=0)
    for start in range(0, active.shape[1], COLUMNS):
        here = slice(start, start + COLUMNS)
        hidden = two_halves(both, (first, second), slice(begin + start, begin + start + COLUMNS))
        below = 0.5 + 0.5 * lax.erf(hidden * (0.5**0.5))
        density = jnp.exp(-0.5 * hidden * hidden) * 0.3989422804014327
        active[:, here] = (hidden * below).astype(jnp.bfloat16)
        slope[:, here] = (below + hidden * density).astype(jnp.bfloat16)


def widen(run, piece, first, second, begin, width):
    outs = [struct((sum(part.shape[0] for part in piece), width))] * 2
    return run("widen", functools.partial(widen_kernel, begin), [*piece, first, second], outs, 14)


def bend_kernel(begin, a, b, c, first, second, slope, out):
    both = jnp.concatenate([a[...], b[...], c[...]], axis=0)
    for start in range(0, out.shape[1], COLUMNS):
        here = slice(start, start + COLUMNS)
        grad = two_halves(both, (first, second), slice(begin + start, begin + start + COLUMNS))
        out[:, here] = (grad * slope[:, here].astype(jnp.float32)).astype(jnp.bfloat16)


def bend_back(run, piece, first, second, begin, slope):
    return run("bend_back", functools.partial(bend_kernel, begin), [*piece, first, second, slope], [struct(slope.shape)], 14)[0]


def narrow_kernel(begin, piece, first, second, kept, sent, sent_more):
    half = kept.shape[0]
    part = sent.shape[0]
    columns = slice(begin, begin + piece.shape[1])
    for index, weights in enumerate((first, second)):
        for start in range(0, weights.shape[0], COLUMNS):
            there = index * weights.shape[0] + start
            here = slice(there, there + COLUMNS)
            rows = weights[start : start + COLUMNS, columns]
            both = dot(piece[...], rows, NT).astype(jnp.bfloat16)
            kept[:, here] = both[:half]
            sent[:, here] = both[half : half + part]
            sent_more[:, here] = both[half + part :]


def narrow(run, piece, first, second, begin):
    rows, width = piece.shape[0] // 2, 2 * first.shape[0]
    outs = [struct((rows, width)), *[struct((rows // 2, width))] * 2]
    kept, *sent = run("narrow", functools.partial(narrow_kernel, begin), [piece, first, second], outs, 14)
    return kept, sent


def weight_terms_kernel(counts, columns, *refs):
    ins = refs[: sum(map(sum, counts))]
    kept, sent, all_left, all_right = refs[len(ins) :]
    begin = 0
    for lefts, rights in counts:
        left, right, ins = ins[:lefts], ins[lefts : lefts + rights], ins[lefts + rights :]
        for store, parts in ((all_left, left), (all_right, right)):
            row = 0
            for part in parts:
                store[row : row + part.shape[0], : part.shape[1]] = part[...]
                row += part.shape[0]
        wide = right[0].shape[1]
        for out, spans in zip((sent, kept), columns[::-1]):
            row = 0
            for first, last in spans:
                for start in range(0, wide, COLUMNS):
                    out[row : row + last - first, begin + start : begin + start + COLUMNS] = dot(
                        all_left[:, first:last], all_right[:, start : start + COLUMNS], TN
                    ).astype(jnp.bfloat16)
                row += last - first
        begin += wide


def weight_terms(run, pairs, columns):
    counts = tuple((len(left), len(right)) for left, right in pairs)
    flat = [array for left, right in pairs for array in (*left, *right)]
    total = sum(array.shape[0] for array in pairs[0][0])
    across = sum(right[0].shape[1] for _, right in pairs)
    return run(
        "weight_terms",
        functools.partial(weight_terms_kernel, counts, columns),
        flat,
        [struct((sum(last - first for first, last in spans), across)) for spans in columns],
        24,
        scratch=[
            pltpu.VMEM((total, pairs[0][0][0].shape[1]), jnp.bfloat16),
            pltpu.VMEM((total, max(right[0].shape[1] for _, right in pairs)), jnp.bfloat16),
        ],
    )


def fold_kernel(many, *refs):
    heres, fars, (kept, sent) = refs[:many], refs[many : 2 * many], refs[2 * many :]
    rows = kept.shape[0]
    begin = 0
    for here, far in zip(heres, fars):
        columns = slice(begin, begin + here.shape[1])
        for out, part in ((sent, slice(rows, None)), (kept, slice(0, rows))):
            out[:, columns] = (
                here[part, :].astype(jnp.float32) + far[part, :].astype(jnp.float32)
            ).astype(jnp.bfloat16)
        begin += here.shape[1]


def fold(run, heres, fars):
    across = sum(array.shape[1] for array in heres)
    outs = [struct((heres[0].shape[0] // 2, across))] * 2
    return run("fold", functools.partial(fold_kernel, len(heres)), [*heres, *fars], outs, 12)


def moments_kernel(at, kept, far, weights, first, second, *refs):
    first_new, second_new, step_out, squares = refs[-4:]
    grad = kept[...].astype(jnp.float32) + far[...].astype(jnp.float32)
    weight = weights[...].reshape(grad.shape)
    new_first, new_second, step = adam_part(
        grad, weight, first[...].reshape(grad.shape), second[...].reshape(grad.shape), WEIGHT_DECAY
    )
    for out, value in ((first_new, new_first), (second_new, new_second), (step_out, step)):
        out[...] = value.reshape(out.shape)
    for place, value in enumerate((weight, step)):
        squares[0, place : place + 1, :] = jnp.sum(value * value, axis=0, keepdims=True)


def moments(run, names, layer, kept, far, weights, first, second, before):
    rows, wide = weights.shape[2:]
    spec = pl.BlockSpec((1, 1, rows, wide), lambda n, at: (layer, at[n], 0, 0))
    grad_spec = pl.BlockSpec((rows, wide), lambda n, at: (0, n))
    before = list(before or [])
    return run(
        "moments",
        moments_kernel,
        [jnp.array(names, jnp.int32), kept, far, weights, first, second, *before],
        [struct(weights.shape, jnp.float32)] * 3 + [struct((len(names), 2, wide), jnp.float32)],
        12,
        in_specs=[grad_spec, grad_spec, spec, spec, spec] + [ANY_SPEC] * len(before),
        out_specs=[spec, spec, spec, pl.BlockSpec((1, 2, wide), lambda n, at: (n, 0, 0))],
        grid_spec=(1, (len(names),)),
        aliases={6 + i: i for i in range(len(before))},
    )


def squares_kernel(places, *refs):
    out = refs[-1]
    for ref, rows in zip(refs[:-1], places):
        for index, row in enumerate(rows):
            sums = jnp.sum(ref[index], axis=-1, keepdims=True)
            out[2 * row : 2 * row + 2, :] = jnp.broadcast_to(sums, (2, out.shape[1]))


def squares_of(run, places, *column_sums):
    rows = 2 * sum(map(len, places))
    body = functools.partial(squares_kernel, places)
    return run("squares_of", body, list(column_sums), [struct((rows, 128), jnp.float32)], 4)[0]


def apply_kernel(begin, total, weights, step, new, low):
    row = 2 * (6 * pl.program_id(0) + begin + pl.program_id(1))
    size, move = jnp.sqrt(total[pl.ds(row, 1), :1]), jnp.sqrt(total[pl.ds(row + 1, 1), :1])
    rate = LEARN_RATE * (size / move)
    value = weights[...].reshape(weights.shape[2:]) - rate * step[...].reshape(step.shape[2:])
    new[...] = value.reshape(new.shape)
    low[...] = value.astype(jnp.bfloat16).reshape(low.shape)


def apply(run, begin, total, weights, step):
    layers, names, rows, wide = weights.shape
    spec = pl.BlockSpec((1, 1, rows, wide), lambda layer, name: (layer, name, 0, 0))
    return run(
        "apply",
        functools.partial(apply_kernel, begin),
        [total, weights, step],
        [struct(weights.shape, jnp.float32), struct(weights.shape)],
        8,
        in_specs=[pl.BlockSpec(total.shape, lambda layer, name: (0, 0)), spec, spec],
        out_specs=[spec, spec],
        grid_spec=(0, (layers, names)),
    )


def move_columns(run, wides, order, out_rows, back):
    width, kind = wides[0].shape[1], wides[0].dtype
    blocks = order.shape[0]
    block = width // blocks
    if block % 128:
        if back:
            order = jnp.argsort(order)
        columns = (order[:, None] * block + jnp.arange(block)[None, :]).reshape(-1)
        moved = jnp.take(jnp.concatenate(wides, axis=0), columns, axis=1)
        starts = [sum(out_rows[:i]) for i in range(len(out_rows))]
        return [moved[start : start + rows] for start, rows in zip(starts, out_rows)]

    def copy(order_ref, *refs):
        ins, outs = refs[: len(wides)], refs[len(wides) :]
        step = min(ref.shape[0] for ref in refs)
        for row in range(0, sum(out_rows), step):
            source, target, from_row, to_row = ins, outs, row, row
            index = 0
            while from_row >= source[index].shape[0]:
                from_row -= source[index].shape[0]
                index += 1
            source, index = source[index], 0
            while to_row >= target[index].shape[0]:
                to_row -= target[index].shape[0]
                index += 1
            target = target[index]
            for place in range(blocks):
                there = pl.ds(pl.multiple_of(order_ref[place] * block, 128), block)
                here = pl.ds(place * block, block)
                from_columns, to_columns = (here, there) if back else (there, here)
                target[pl.ds(to_row, step), to_columns] = source[pl.ds(from_row, step), from_columns]

    return run(
        "move_columns",
        copy,
        [order, *wides],
        [struct((rows, width), kind) for rows in out_rows],
        6,
        in_specs=[SMEM_SPEC] + [VMEM_SPEC] * len(wides),
    )


class Rows:
    def __init__(self, total, run):
        self.total, self.run = total, run
        self.strides = [1 << bit for bit in reversed(range(total.bit_length() - 1))]

    def order(self):
        places = [0]
        for stride in self.strides:
            places = places + [place ^ stride for place in places]
        return jnp.bitwise_xor(
            jnp.array(places, jnp.int32), lax.axis_index("dp").astype(jnp.int32)
        )

    def swap(self, values, stride):
        return lax.ppermute(
            values, "dp", [(source, source ^ stride) for source in range(self.total)]
        )


class Gather:
    def __init__(self, rows, weights, layer, first, last, spans):
        self.rows, self.run, self.spans = rows, rows.run, spans
        self.what = (weights, layer, first, last)
        self.width = sum(spans)
        self.wholes = [None] * len(spans)

    def far(self):
        self.block = cast_blocks(self.run, *self.what)
        self.there = self.rows.swap(self.block, self.rows.strides[0])

    def near(self):
        for stride in self.rows.strides[1:-1]:
            self.run.settle(self.there)
            self.block = join(self.run, self.block, self.there, 0, self.width)
            self.there = self.rows.swap(self.block, stride)

    def last(self, span=0):
        part = join(self.run, self.block, self.there, sum(self.spans[:span]), self.spans[span])
        self.wholes[span] = (part, self.rows.swap(part, self.rows.strides[-1]))

    def take(self, span=0):
        self.run.settle(self.wholes[span][1])
        return self.wholes[span]


def stack_kernel(*refs):
    out, begin = refs[-1], 0
    for here, far in zip(refs[:-1:2], refs[1:-1:2]):
        columns = slice(begin, begin + here.shape[1])
        out[: here.shape[0], columns] = here[...]
        out[here.shape[0] :, columns] = far[...]
        begin += here.shape[1]


def stack(run, *pairs):
    flat = [array for pair in pairs for array in pair]
    across = sum(here.shape[1] for here, _ in pairs)
    return run("stack", stack_kernel, flat, [struct((2 * flat[0].shape[0], across))], 12)[0]


class GatherBoth:
    def __init__(self, rows, weights, layer):
        self.ways = [
            Gather(rows, weights, layer, name, name + 1, [weights.shape[3]]) for name in range(2)
        ]
        self.rows, self.run = rows, rows.run

    def near(self):
        for way in self.ways:
            for stride in self.rows.strides[1:-2]:
                way.block = join(self.run, way.block, way.there, 0, way.width)
                way.there = self.rows.swap(way.block, stride)
        self.block = stack(self.run, *[(way.block, way.there) for way in self.ways])
        self.there = self.rows.swap(self.block, self.rows.strides[-2])

    def last(self):
        self.whole = stack(self.run, (self.block, self.there))
        self.there = self.rows.swap(self.whole, self.rows.strides[-1])

    def take(self):
        self.run.settle(self.there)
        return self.whole, self.there


class Reduce:
    def __init__(self, rows):
        self.rows, self.run = rows, rows.run
        self.kept, self.there = [], []

    def send(self, *pairs):
        columns = (((0, D // 2),), ((D // 2, D),))
        keep, away = weight_terms(self.run, pairs, columns)
        self.kept.append(keep)
        self.there.append(self.rows.swap(away, self.rows.strides[-1]))

    def settle(self, group=0):
        self.run.settle(self.there[group])

    def near(self):
        self.pass_on(self.rows.strides[-2])

    def far(self):
        for stride in reversed(self.rows.strides[:-2]):
            self.pass_on(stride)

    def pass_on(self, stride):
        keep, away = fold(self.run, self.kept, self.there)
        self.kept, self.there = [keep], [self.rows.swap(away, stride)]

    def terms(self):
        return self.kept[0], self.there[0]


def core_swap(values_in):
    return lax.ppermute(values_in, "mp", [(0, 1), (1, 0), (2, 3), (3, 2)])


def chip_swap(values_in):
    return lax.ppermute(values_in, "mp", [(0, 2), (2, 0), (1, 3), (3, 1)])


class Exchange:
    def __init__(self, run, mine):
        self.run, (self.mine, parts) = run, mine
        self.beyond = chip_swap(self.mine)
        self.facing = [core_swap(part) for part in parts]

    def near(self):
        return [self.mine, *self.facing]

    def pass_on(self):
        self.relay, parts = cast(self.run, self.beyond)
        self.beyond_facing = [core_swap(part) for part in parts]

    def far(self):
        return [self.relay, *self.beyond_facing]

    def pieces(self):
        return self.near() + self.far()


def collect(run, near_piece, far_piece, weights, begin):
    far_kept, far_sent = narrow(run, far_piece, *weights, begin)
    far_sent = [core_swap(part) for part in far_sent]
    kept, sent = narrow(run, near_piece, *weights, begin)
    there = chip_swap(add_halves(run, far_kept, far_sent, jnp.bfloat16))
    sent = [core_swap(part) for part in sent]
    return add_halves(run, kept, sent, jnp.float32), there


def shards(
    rows_total,
    tokens,
    cotangent,
    segments,
    attention_weights,
    attention_first,
    attention_second,
    dense_weights,
    dense_first,
    dense_second,
    norm_params,
    norm_first,
    norm_second,
):
    layers = attention_weights.shape[0]
    width, wide = attention_weights.shape[3], dense_weights.shape[3]
    run = Order()
    settle = run.settle
    rows = Rows(rows_total, run)
    order = rows.order()
    place = lax.axis_index("mp").astype(jnp.int32).reshape(1)
    mask = crop_mask(segments)
    count = tokens.shape[0]

    inputs_way = Gather(rows, attention_weights, 0, 0, 3, [3 * width])
    output_way = Gather(rows, attention_weights, 0, 3, 4, [width])
    up_way = Gather(rows, dense_weights, 0, 0, 1, [wide])
    down_way = Gather(rows, dense_weights, 0, 1, 2, [wide])
    mixer_way = Gather(rows, attention_weights, 1, 0, 4, [4 * width])
    dense_way = GatherBoth(rows, dense_weights, 1)

    inputs_way.far()
    (params_here,) = move_columns(
        run, [norm_params.reshape(layers * 4, D)], order, [layers * 4], False
    )
    (stream,) = move_columns(run, [tokens], order, [count], False)
    normed = Exchange(run, *norm(run, params_here, 0, stream))
    inputs_way.near()
    output_way.far()
    inputs_way.last()
    up_way.far()
    output_way.near()
    normed.pass_on()
    (stream_grad,) = move_columns(run, [cotangent], order, [count], False)
    back = Exchange(run, cast(run, stream_grad))
    output_way.last()
    up_way.near()
    inputs_map = inputs_way.take()
    projected = [project(run, normed.near(), *inputs_map, 0, 3 * width)]
    projected.append(project(run, normed.far(), *inputs_map, 0, 3 * width))
    down_way.far()
    attended = attend(run, place, mask, projected)
    back.pass_on()
    up_way.last()
    output_map = output_way.take()

    saved = []
    settle(down_way.there)
    mixed = collect(run, attended[0], attended[1], output_map, 0)
    down_way.near()
    mixer_way.far()
    dense_way.ways[0].far()
    middle, low = norm(run, params_here, 2, stream, *mixed)
    normed_two = Exchange(run, low)
    down_way.last()
    mixer_way.near()
    settle(dense_way.ways[0].there)
    dense_way.ways[1].far()
    up_map = (*up_way.take(), 0)
    active, slope = [None, None], [None, None]
    active[0], slope[0] = widen(run, normed_two.near(), *up_map, wide)
    settle(mixer_way.there)
    settle(dense_way.ways[1].there)
    normed_two.pass_on()
    active[1], slope[1] = widen(run, normed_two.far(), *up_map, wide)
    down_map = (*down_way.take(), 0)
    saved.append((stream, normed, projected, attended, middle, normed_two, active, slope))
    saved[-1] += ((*inputs_map, 0), (*output_map, 0), up_map, down_map)

    widened = collect(run, *active, down_map[:2], down_map[2])
    mixer_way.last()
    dense_way.near()
    stream, low = norm(run, params_here, 4, middle, *widened)
    normed = Exchange(run, low)
    dense_way.last()
    inputs_map = mixer_way.take()
    projected = [project(run, normed.near(), *inputs_map, 0, 3 * width)]
    normed.pass_on()
    projected.append(project(run, normed.far(), *inputs_map, 0, 3 * width))
    attended = attend(run, place, mask, projected)

    mixed = collect(run, attended[0], attended[1], inputs_map, 3 * width)
    middle, low = norm(run, params_here, 6, stream, *mixed)
    normed_two = Exchange(run, low)
    dense_map = dense_way.take()
    up_map, down_map = (*dense_map, 0), (*dense_map, wide)
    active, slope = [None, None], [None, None]
    active[0], slope[0] = widen(run, normed_two.near(), *up_map, wide)
    grad_hidden = [bend_back(run, back.near(), *down_map, slope[0])]
    normed_two.pass_on()
    active[1], slope[1] = widen(run, normed_two.far(), *up_map, wide)
    saved.append((stream, normed, projected, attended, middle, normed_two, active, slope))
    saved[-1] += ((*inputs_map, 0), (*inputs_map, 3 * width), up_map, down_map)

    mixer_state, dense_state = None, None
    squares, places, vectors = [], [], [None] * (2 * layers)

    def dense_moments(layer, names, terms):
        nonlocal dense_state
        *dense_state, sums = moments(
            run, names, layer, *terms, dense_weights, dense_first, dense_second, dense_state
        )
        squares.append(sums)
        places.append([6 * layer + 4 + name for name in names])

    def mixer_moments(layer, terms):
        nonlocal mixer_state
        *mixer_state, sums = moments(
            run, (0, 1, 2, 3), layer, *terms,
            attention_weights, attention_first, attention_second, mixer_state,
        )
        squares.append(sums)
        places.append([6 * layer + name for name in range(4)])

    def weight_grad(*pairs):
        reduced = Reduce(rows)
        reduced.send(*pairs)
        return reduced

    stream_in, normed, projected, attended, middle, normed_two, active, slope = saved[1][:8]
    inputs_map, output_map, up_map, down_map = saved[1][8:]
    grad_hidden.append(bend_back(run, back.far(), *down_map, slope[1]))
    raised = collect(run, *grad_hidden, up_map[:2], up_map[2])
    down_later = weight_grad((back.pieces(), active))
    up_later = weight_grad((normed_two.pieces(), grad_hidden))
    vectors[3], stream_grad, low = norm_back(run, params_here, 6, stream_grad, middle, *raised)
    turned = Exchange(run, low)
    down_later.near()
    grad_attended = [project(run, turned.near(), *output_map, width)]
    turned.pass_on()
    grad_attended.append(project(run, turned.far(), *output_map, width))
    grad_projected = attend_back(run, place, mask, projected, grad_attended)

    down_later.settle()
    lowered = collect(run, *grad_projected, inputs_map[:2], inputs_map[2])
    down_later.far()
    up_later.near()
    mixer_later = weight_grad((normed.pieces(), grad_projected), (turned.pieces(), attended))
    vectors[2], stream_grad, low = norm_back(run, params_here, 4, stream_grad, stream_in, *lowered)
    back = Exchange(run, low)

    stream_in, normed, projected, attended, middle, normed_two, active, slope = saved[0][:8]
    inputs_map, output_map, up_map, down_map = saved[0][8:]
    grad_hidden = [bend_back(run, back.near(), *down_map, slope[0])]
    mixer_later.settle()
    up_later.settle()
    down_later.settle()
    back.pass_on()
    grad_hidden.append(bend_back(run, back.far(), *down_map, slope[1]))
    raised = collect(run, *grad_hidden, up_map[:2], up_map[2])
    mixer_later.near()
    up_later.far()
    down_grad = weight_grad((back.pieces(), active))
    dense_moments(1, (1,), down_later.terms())
    up_later.settle()
    vectors[1], stream_grad, low = norm_back(run, params_here, 2, stream_grad, middle, *raised)
    turned = Exchange(run, low)
    mixer_later.far()
    up_grad = weight_grad((normed_two.pieces(), grad_hidden))
    grad_attended = [project(run, turned.near(), *output_map, width)]
    dense_moments(1, (0,), up_later.terms())
    down_grad.near()
    mixer_later.settle()
    turned.pass_on()
    grad_attended.append(project(run, turned.far(), *output_map, width))
    grad_projected = attend_back(run, place, mask, projected, grad_attended)

    down_grad.settle()
    lowered = collect(run, *grad_projected, inputs_map[:2], inputs_map[2])
    mixer_grad = weight_grad((normed.pieces(), grad_projected), (turned.pieces(), attended))
    down_grad.far()
    up_grad.near()
    mixer_moments(1, mixer_later.terms())
    down_grad.settle()
    vectors[0], stream_grad, low = norm_back(run, params_here, 0, stream_grad, stream_in, *lowered)

    up_grad.far()
    middle, active, down_map = saved[-1][4], saved[-1][6], saved[-1][11]
    widened = collect(run, *active, down_map[:2], down_map[2])
    mixer_grad.near()
    dense_moments(0, (1,), down_grad.terms())
    all_rows = jnp.concatenate([jnp.sum(sums.reshape(2, 8, D), axis=1) for sums in vectors])
    (all_rows,) = move_columns(run, [all_rows], order, [layers * 4], True)
    all_rows = add(run, all_rows, core_swap(all_rows), jnp.float32)
    (grad_tokens,) = move_columns(run, [stream_grad], order, [count], True)
    mixer_grad.far()
    last_stream = add(run, middle, widened[0], jnp.float32, widened[1])
    all_rows = add(run, all_rows, chip_swap(all_rows), jnp.float32)
    for stride in reversed(rows.strides):
        all_rows = add(run, all_rows, rows.swap(all_rows, stride), jnp.float32)
    (outcome,) = move_columns(run, [last_stream], order, [count], True)
    dense_moments(0, (0,), up_grad.terms())
    mixer_moments(0, mixer_grad.terms())
    all_squares = squares_of(run, places, *squares)
    all_squares = add(run, all_squares, core_swap(all_squares), jnp.float32)
    all_squares = add(run, all_squares, chip_swap(all_squares), jnp.float32)
    for stride in reversed(rows.strides):
        all_squares = add(run, all_squares, rows.swap(all_squares, stride), jnp.float32)
    all_vectors = all_rows
    mixer_new, mixer_copy = apply(run, 0, all_squares, attention_weights, mixer_state[2])
    dense_new, dense_copy = apply(run, 4, all_squares, dense_weights, dense_state[2])

    total_squares = all_squares[:, 0].reshape(layers, 6, 2)
    total_vectors = all_vectors.reshape(layers, 4, D)
    sizes_all = jnp.sqrt(total_squares[:, :, 0])
    moves_all = jnp.sqrt(total_squares[:, :, 1])
    params_first, params_second, params_step = adam_part(
        total_vectors, norm_params, norm_first, norm_second, 0.0
    )
    params_size = jnp.sqrt(jnp.sum(norm_params * norm_params, axis=-1))
    params_move = jnp.sqrt(jnp.sum(params_step * params_step, axis=-1))
    params_new = norm_params - LEARN_RATE * (params_size / params_move)[:, :, None] * params_step
    mixer_entries = float(D * HEADS * HD) ** 0.5
    dense_entries = float(D * FF) ** 0.5
    entry_roots = jnp.array([mixer_entries] * 4 + [dense_entries] * 2, jnp.float32)
    norms = jnp.stack([sizes_all / entry_roots[None, :], moves_all / entry_roots[None, :]], axis=-1)
    second_norm_grad = total_vectors[:, 2:4]
    return (
        outcome,
        grad_tokens,
        mixer_new,
        mixer_state[0],
        mixer_state[1],
        mixer_copy,
        dense_new,
        dense_state[0],
        dense_state[1],
        dense_copy,
        params_new,
        params_first,
        params_second,
        norms,
        second_norm_grad,
    )


def solution(mesh):
    rows_spec = P(("dp", "mp"), None)
    weight_spec = P(None, None, "dp", "mp")
    in_specs = (rows_spec, rows_spec, P("dp")) + (weight_spec,) * 6 + (P(),) * 3
    out_specs = (rows_spec,) * 2 + (weight_spec,) * 8 + (P(),) * 5
    return jax.shard_map(
        functools.partial(shards, mesh.shape["dp"]),
        mesh=mesh,
        in_specs=in_specs,
        out_specs=out_specs,
        check_vma=False,
    )
```

```python
import functools

import jax
import jax.numpy as jnp
from jax import lax
from jax.experimental import pallas as pl
from jax.experimental.pallas import tpu as pltpu
from jax.sharding import PartitionSpec as P

D = 1024
HEADS = 16
HD = 64
FF = 4096
STEP = 10


EPS_NORM = 1e-06
BETA_ONE = 0.9
BETA_TWO = 0.999
ADAM_EPS = 1e-06
WEIGHT_DECAY = 0.01
LEARN_RATE = 0.5
MASKED = -1000000000.0

QUERIES = 128
REACH = 64
WINDOW = QUERIES + 2 * REACH

NT = (((1,), (1,)), ((), ()))
TN = (((0,), (0,)), ((), ()))


VMEM_SPEC = pl.BlockSpec(memory_space=pltpu.VMEM)
SMEM_SPEC = pl.BlockSpec(memory_space=pltpu.SMEM)
ANY_SPEC = pl.BlockSpec(memory_space=pl.ANY)


def struct(shape, kind=jnp.bfloat16):
    return jax.ShapeDtypeStruct(shape, kind)


TOKEN = struct((8, 128), jnp.float32)


class Order:
    def __init__(self):
        self.token, self.earlier = None, []

    def settle(self, value):
        self.earlier = self.earlier + [value]
        return value

    def mark(self):
        self("mark", lambda: None, [], [], 2)

    def __call__(
        self, name, body, ins, outs, room, in_specs=None, out_specs=None, grid_spec=None, scratch=(), aliases=None
    ):
        before = [] if self.token is None else [self.token]
        extra = before + list(self.earlier)
        scalars = 0 if grid_spec is None else grid_spec[0]

        def wrapped(*refs):
            token = refs[len(ins) + len(extra) + len(outs)]
            token[...] = jnp.zeros(TOKEN.shape, TOKEN.dtype)
            refs = refs[: len(ins)] + refs[len(ins) + len(extra) :]
            return body(*refs[: len(ins) + len(outs)], *refs[len(ins) + len(outs) + 1 :])

        if grid_spec is None:
            token_spec = VMEM_SPEC
        else:
            token_spec = pl.BlockSpec(TOKEN.shape, lambda *grid: (0, 0))
        in_specs = (in_specs or [VMEM_SPEC] * len(ins)) + [token_spec] * len(before)
        in_specs = in_specs + [ANY_SPEC] * len(self.earlier)
        out_specs = (out_specs or [VMEM_SPEC] * len(outs)) + [token_spec]
        if grid_spec is None:
            places = dict(in_specs=in_specs, out_specs=out_specs, scratch_shapes=scratch)
        else:
            places = dict(
                grid_spec=pltpu.PrefetchScalarGridSpec(
                    num_scalar_prefetch=scalars,
                    grid=grid_spec[1],
                    in_specs=in_specs,
                    out_specs=out_specs,
                )
            )
        *result, self.token = pl.pallas_call(
            wrapped,
            out_shape=[*outs, TOKEN],
            **places,
            input_output_aliases=aliases or {},
            cost_estimate=pl.CostEstimate(flops=1, bytes_accessed=1, transcendentals=0),
            compiler_params=pltpu.CompilerParams(vmem_limit_bytes=room << 20),
            name=name,
        )(*ins, *extra)
        self.earlier = []
        return result


def add(run, here, far, kind, *more):
    body = functools.partial(sum_kernel, 2 + len(more))
    return run("add", body, [here, far, *more], [struct(here.shape, kind)], 4)[0]


def sum_kernel(count, *refs):
    total = refs[0][...].astype(jnp.float32)
    for ref in refs[1:count]:
        total = total + ref[...].astype(jnp.float32)
    refs[-1][...] = total.astype(refs[-1].dtype)


def add_halves_kernel(kept, first, second, out):
    half = first.shape[0]
    for here, part in ((slice(0, half), first), (slice(half, None), second)):
        total = kept[here, :].astype(jnp.float32) + part[...].astype(jnp.float32)
        out[here, :] = total.astype(out.dtype)


def add_halves(run, kept, parts, kind):
    return run("add", add_halves_kernel, [kept, *parts], [struct(kept.shape, kind)], 6)[0]


def cast_kernel(ref, out, first, second):
    low = ref[...].astype(out.dtype)
    out[...] = low
    first[...] = low[: first.shape[0]]
    second[...] = low[first.shape[0] :]


def cast(run, wide):
    rows, width = wide.shape
    outs = [struct((rows, width)), *[struct((rows // 2, width))] * 2]
    low, *parts = run("cast", cast_kernel, [wide], outs, 6)
    return low, parts


def block_kernel(ref, out):
    out[...] = ref[...].reshape(out.shape).astype(out.dtype)


def cast_blocks(run, weights, layer, first, last):
    rows, wide = weights.shape[2:]
    return run(
        "cast",
        block_kernel,
        [weights],
        [struct((rows, (last - first) * wide))],
        6,
        in_specs=[pl.BlockSpec((1, 1, rows, wide), lambda n: (layer, first + n, 0, 0))],
        out_specs=[pl.BlockSpec((rows, wide), lambda n: (0, n))],
        grid_spec=(0, (last - first,)),
    )[0]


def join_kernel(begin, here, far, out):
    rows = here.shape[0]
    columns = slice(begin, begin + out.shape[1])
    out[:rows, :] = here[:, columns]
    out[rows:, :] = far[:, columns]


def join(run, here, far, begin, width):
    outs = [struct((2 * here.shape[0], width))]
    return run("join", functools.partial(join_kernel, begin), [here, far], outs, 10)[0]


def adam_part(gradient, weight, first, second, decay):
    first_new = BETA_ONE * first + (1.0 - BETA_ONE) * gradient
    second_new = BETA_TWO * second + (1.0 - BETA_TWO) * gradient * gradient
    step_dir = (
        first_new
        / (1.0 - BETA_ONE**STEP)
        / (jnp.sqrt(second_new / (1.0 - BETA_TWO**STEP)) + ADAM_EPS)
        + decay * weight
    )
    return (first_new, second_new, step_dir)


def dot(left, right, dims=(((1,), (0,)), ((), ()))):
    return lax.dot_general(left, right, dims, preferred_element_type=jnp.float32)


def head_lanes(rows, width, value):
    lane_head = lax.broadcasted_iota(jnp.int32, (rows, width), 1) // HD
    return [
        jnp.where(lane_head == head, value, 0.0).astype(jnp.float32) for head in range(width // HD)
    ]


def block_shares(query_wide, keys_in, mask):
    heads_here = query_wide.shape[0] // QUERIES
    scores = dot(query_wide, keys_in, NT).reshape(heads_here, QUERIES, WINDOW)
    scores = jnp.where((mask > 0.5)[None], scores, MASKED)
    powered = jnp.exp(scores - jnp.max(scores, axis=-1, keepdims=True))
    shares = powered * (1.0 / jnp.sum(powered, axis=-1, keepdims=True))
    return shares.reshape(heads_here * QUERIES, WINDOW)


def fold_heads(wide, lanes):
    total = wide[:QUERIES] * lanes[0]
    for head in range(1, len(lanes)):
        total += wide[head * QUERIES : (head + 1) * QUERIES] * lanes[head]
    return total


def places_of(place_ref, pieces, rows):
    half = rows // 2
    found = []
    for piece in range(pieces):
        for core in range(2):
            block = jnp.bitwise_xor(place_ref[0], 2 * piece + core)
            found.append((piece, core * half, pl.multiple_of(block * half, 32)))
    return found


def in_token_order(place_ref, refs, store, start):
    rows = refs[0].shape[0]
    for piece, row, token in places_of(place_ref, len(refs), rows):
        store[pl.ds(token + start, rows // 2), :] = refs[piece][pl.ds(row, rows // 2), :]


def attend_kernel(pieces, place_ref, mask_ref, *refs):
    ins, outs, (all_in, all_out) = refs[:pieces], refs[pieces : 2 * pieces], refs[2 * pieces :]
    count, width = all_out.shape
    all_in[:REACH, :] = jnp.zeros((REACH, 3 * width), jnp.bfloat16)
    all_in[REACH + count :, :] = jnp.zeros((REACH, 3 * width), jnp.bfloat16)
    in_token_order(place_ref, ins, all_in, REACH)
    scaled = [lane.astype(jnp.bfloat16) for lane in head_lanes(QUERIES, width, HD ** (-0.5))]
    plain = head_lanes(QUERIES, width, 1.0)

    @pl.loop(0, count // QUERIES, unroll=count // QUERIES)
    def _(block):
        base = pl.multiple_of(block * QUERIES, QUERIES)
        query = all_in[pl.ds(base + REACH, QUERIES), :width]
        keys_in = all_in[pl.ds(base, WINDOW), width : 2 * width]
        values_in = all_in[pl.ds(base, WINDOW), 2 * width :]
        query_wide = jnp.concatenate([query * lane for lane in scaled], axis=0)
        shares = block_shares(query_wide, keys_in, mask_ref[pl.ds(base, QUERIES), :])
        wide = dot(shares.astype(jnp.bfloat16), values_in)
        all_out[pl.ds(base, QUERIES), :] = fold_heads(wide, plain).astype(jnp.bfloat16)

    rows = outs[0].shape[0]
    for piece, row, token in places_of(place_ref, pieces, rows):
        outs[piece][pl.ds(row, rows // 2), :] = all_out[pl.ds(token, rows // 2), :]


def attend_back_kernel(pieces, place_ref, mask_ref, *refs):
    ins, grads, outs = refs[:pieces], refs[pieces : 2 * pieces], refs[2 * pieces : 3 * pieces]
    all_in, all_grad, query_sum, key_sum, value_sum = refs[3 * pieces :]
    count, width = all_grad.shape
    all_in[:REACH, :] = jnp.zeros((REACH, 3 * width), jnp.bfloat16)
    all_in[REACH + count :, :] = jnp.zeros((REACH, 3 * width), jnp.bfloat16)
    in_token_order(place_ref, ins, all_in, REACH)
    in_token_order(place_ref, grads, all_grad, 0)
    key_sum[...] = jnp.zeros_like(key_sum)
    value_sum[...] = jnp.zeros_like(value_sum)
    scaled = [lane.astype(jnp.bfloat16) for lane in head_lanes(QUERIES, width, HD ** (-0.5))]
    plain_low = [lane.astype(jnp.bfloat16) for lane in head_lanes(QUERIES, width, 1.0)]
    scaled_wide = head_lanes(QUERIES, width, HD ** (-0.5))

    @pl.loop(0, count // QUERIES, unroll=count // QUERIES)
    def _(block):
        base = pl.multiple_of(block * QUERIES, QUERIES)
        query = all_in[pl.ds(base + REACH, QUERIES), :width]
        keys_in = all_in[pl.ds(base, WINDOW), width : 2 * width]
        values_in = all_in[pl.ds(base, WINDOW), 2 * width :]
        grad = all_grad[pl.ds(base, QUERIES), :]
        query_wide = jnp.concatenate([query * lane for lane in scaled], axis=0)
        grad_wide = jnp.concatenate([grad * lane for lane in plain_low], axis=0)
        shares = block_shares(query_wide, keys_in, mask_ref[pl.ds(base, QUERIES), :])
        grad_shares = dot(grad_wide, values_in, NT)
        inner = jnp.sum(grad_shares * shares, axis=-1, keepdims=True)
        grad_scores = (shares * (grad_shares - inner)).astype(jnp.bfloat16)
        query_sum[pl.ds(base, QUERIES), :] = fold_heads(dot(grad_scores, keys_in), scaled_wide)
        key_sum[pl.ds(base, WINDOW), :] += dot(grad_scores, query_wide, TN)
        value_sum[pl.ds(base, WINDOW), :] += dot(shares.astype(jnp.bfloat16), grad_wide, TN)

    rows = outs[0].shape[0]
    for piece, row, token in places_of(place_ref, pieces, rows):
        here, there = pl.ds(row, rows // 2), pl.ds(token + REACH, rows // 2)
        out = outs[piece]
        out[here, :width] = query_sum[pl.ds(token, rows // 2), :].astype(jnp.bfloat16)
        out[here, width : 2 * width] = key_sum[there, :].astype(jnp.bfloat16)
        out[here, 2 * width :] = value_sum[there, :].astype(jnp.bfloat16)


def attend(run, place, mask, projected):
    pieces = len(projected)
    rows, width = projected[0].shape[0], projected[0].shape[1] // 3
    count = rows * pieces
    return run(
        "attend",
        functools.partial(attend_kernel, pieces),
        [place, mask, *projected],
        [struct((rows, width))] * pieces,
        12,
        in_specs=[SMEM_SPEC] + [VMEM_SPEC] * (1 + pieces),
        scratch=[
            pltpu.VMEM((count + 2 * REACH, 3 * width), jnp.bfloat16),
            pltpu.VMEM((count, width), jnp.bfloat16),
        ],
    )


def attend_back(run, place, mask, projected, grads):
    pieces = len(projected)
    rows, width = projected[0].shape[0], projected[0].shape[1] // 3
    count = rows * pieces
    return run(
        "attend_back",
        functools.partial(attend_back_kernel, pieces),
        [place, mask, *projected, *grads],
        [struct((rows, 3 * width))] * pieces,
        20,
        in_specs=[SMEM_SPEC] + [VMEM_SPEC] * (1 + 2 * pieces),
        scratch=[
            pltpu.VMEM((count + 2 * REACH, 3 * width), jnp.bfloat16),
            pltpu.VMEM((count, width), jnp.bfloat16),
            pltpu.VMEM((count, width), jnp.float32),
            pltpu.VMEM((count + 2 * REACH, width), jnp.float32),
            pltpu.VMEM((count + 2 * REACH, width), jnp.float32),
        ],
    )


def crop_mask(segments):
    blocks = segments.shape[0] // QUERIES
    edge = jnp.full((REACH,), -1, segments.dtype)
    padded = jnp.concatenate([edge, segments, edge])
    keys_of = jnp.stack([padded[b * QUERIES : b * QUERIES + WINDOW] for b in range(blocks)])
    same = segments.reshape(blocks, QUERIES)[:, :, None] == keys_of[:, None, :]
    return same.astype(jnp.float32).reshape(blocks * QUERIES, WINDOW)


def row_step(count):
    return 32 if count % 32 == 0 else count


def normalised(value):
    centre = value - jnp.mean(value, axis=-1, keepdims=True)
    spread_of = jnp.mean(centre * centre, axis=-1, keepdims=True)
    scale = lax.rsqrt(spread_of + EPS_NORM)
    return centre * scale, scale


def norm_kernel(row, terms, params_ref, value_ref, *refs):
    *outs, all_low, first_low, second_low = refs[terms:]
    half = first_low.shape[0]
    step = row_step(half)
    gain, shift = params_ref[row : row + 1, :], params_ref[row + 1 : row + 2, :]
    for start in range(0, 2 * half, step):
        here = slice(start, start + step)
        value = value_ref[here, :]
        if terms:
            value = value + refs[0][here, :].astype(jnp.float32)
            value = value + refs[1][here, :].astype(jnp.float32)
            outs[0][here, :] = value
        low = (normalised(value)[0] * gain + shift).astype(jnp.bfloat16)
        all_low[here, :] = low
        if start < half:
            first_low[here, :] = low
        else:
            second_low[start - half : start - half + step, :] = low


def norm(run, params, row, value, *terms):
    wide = [struct(value.shape, jnp.float32)] if terms else []
    low = [struct(value.shape), *[struct((value.shape[0] // 2, value.shape[1]))] * 2]
    body = functools.partial(norm_kernel, row, len(terms))
    *stream, whole, first, second = run("norm", body, [params, value, *terms], wide + low, 6)
    return (*stream, (whole, [first, second]))


def norm_back_kernel(
    row, params_ref, stream_ref, value_ref, near, far, sums_ref, out_ref, all_low, first_low, second_low
):
    half = first_low.shape[0]
    step = row_step(half)
    width = value_ref.shape[1]
    gain = params_ref[row : row + 1, :]
    sums_ref[...] = jnp.zeros_like(sums_ref)
    for start in range(0, 2 * half, step):
        here = slice(start, start + step)
        grad = near[here, :].astype(jnp.float32) + far[here, :].astype(jnp.float32)
        unit, scale = normalised(value_ref[here, :])
        along = grad * unit
        sums_ref[:8, :] += jnp.sum(along.reshape(step // 8, 8, width), axis=0)
        sums_ref[8:, :] += jnp.sum(grad.reshape(step // 8, 8, width), axis=0)
        pushed = grad * gain
        inner = jnp.mean(pushed * unit, axis=-1, keepdims=True)
        term = scale * (pushed - jnp.mean(pushed, axis=-1, keepdims=True) - unit * inner)
        total = stream_ref[here, :] + term
        out_ref[here, :] = total
        low = total.astype(jnp.bfloat16)
        all_low[here, :] = low
        if start < half:
            first_low[here, :] = low
        else:
            second_low[start - half : start - half + step, :] = low


def norm_back(run, params, row, stream_grad, value, *terms):
    sums, stream, whole, first, second = run(
        "norm_back",
        functools.partial(norm_back_kernel, row),
        [params, stream_grad, value, *terms],
        [
            struct((16, value.shape[1]), jnp.float32),
            struct(value.shape, jnp.float32),
            struct(value.shape),
            *[struct((value.shape[0] // 2, value.shape[1]))] * 2,
        ],
        8,
    )
    return sums, stream, (whole, [first, second])


COLUMNS = 256


def by_parts(both, weights, here):
    total, row = 0.0, 0
    for part in weights:
        total = total + dot(both[:, row : row + part.shape[0]], part[:, here])
        row += part.shape[0]
    return total


def project_kernel(begin, many, a, b, c, *refs):
    weights, (out,) = refs[:many], refs[many:]
    both = jnp.concatenate([a[...], b[...], c[...]], axis=0)
    for start in range(0, out.shape[1], COLUMNS):
        here = slice(begin + start, begin + start + COLUMNS)
        out[:, start : start + COLUMNS] = by_parts(both, weights, here).astype(
            jnp.bfloat16
        )


def project(run, piece, *rest):
    *weights, begin, width = rest
    outs = [struct((sum(part.shape[0] for part in piece), width))]
    body = functools.partial(project_kernel, begin, len(weights))
    return run("project", body, [*piece, *weights], outs, 14)[0]


def widen_kernel(begin, many, a, b, c, *refs):
    weights, (active, slope) = refs[:many], refs[many:]
    both = jnp.concatenate([a[...], b[...], c[...]], axis=0)
    for start in range(0, active.shape[1], COLUMNS):
        here = slice(start, start + COLUMNS)
        hidden = by_parts(both, weights, slice(begin + start, begin + start + COLUMNS))
        below = 0.5 + 0.5 * lax.erf(hidden * (0.5**0.5))
        density = jnp.exp(-0.5 * hidden * hidden) * 0.3989422804014327
        active[:, here] = (hidden * below).astype(jnp.bfloat16)
        slope[:, here] = (below + hidden * density).astype(jnp.bfloat16)


def widen(run, piece, *rest):
    *weights, begin, width = rest
    outs = [struct((sum(part.shape[0] for part in piece), width))] * 2
    body = functools.partial(widen_kernel, begin, len(weights))
    return run("widen", body, [*piece, *weights], outs, 14)


def bend_kernel(begin, many, a, b, c, *refs):
    weights, (slope, out) = refs[:many], refs[many:]
    both = jnp.concatenate([a[...], b[...], c[...]], axis=0)
    for start in range(0, out.shape[1], COLUMNS):
        here = slice(start, start + COLUMNS)
        grad = by_parts(both, weights, slice(begin + start, begin + start + COLUMNS))
        out[:, here] = (grad * slope[:, here].astype(jnp.float32)).astype(jnp.bfloat16)


def bend_back(run, piece, *rest):
    *weights, begin, slope = rest
    body = functools.partial(bend_kernel, begin, len(weights))
    return run("bend_back", body, [*piece, *weights, slope], [struct(slope.shape)], 14)[0]


def narrow_kernel(begin, many, piece, *refs):
    weights_parts, (kept, sent, sent_more) = refs[:many], refs[many:]
    half = kept.shape[0]
    part = sent.shape[0]
    columns = slice(begin, begin + piece.shape[1])
    for index, weights in enumerate(weights_parts):
        for start in range(0, weights.shape[0], COLUMNS):
            there = index * weights.shape[0] + start
            here = slice(there, there + COLUMNS)
            rows = weights[start : start + COLUMNS, columns]
            both = dot(piece[...], rows, NT).astype(jnp.bfloat16)
            kept[:, here] = both[:half]
            sent[:, here] = both[half : half + part]
            sent_more[:, here] = both[half + part :]


def narrow(run, piece, *rest):
    *weights, begin = rest
    rows, width = piece.shape[0] // 2, sum(part.shape[0] for part in weights)
    outs = [struct((rows, width)), *[struct((rows // 2, width))] * 2]
    body = functools.partial(narrow_kernel, begin, len(weights))
    kept, *sent = run("narrow", body, [piece, *weights], outs, 14)
    return kept, sent


def weight_terms_kernel(counts, columns, *refs):
    ins = refs[: sum(map(sum, counts))]
    kept, sent, all_left, all_right = refs[len(ins) :]
    begin = 0
    for lefts, rights in counts:
        left, right, ins = ins[:lefts], ins[lefts : lefts + rights], ins[lefts + rights :]
        for store, parts in ((all_left, left), (all_right, right)):
            row = 0
            for part in parts:
                store[row : row + part.shape[0], : part.shape[1]] = part[...]
                row += part.shape[0]
        wide = right[0].shape[1]
        for out, spans in zip((sent, kept), columns[::-1]):
            row = 0
            for first, last in spans:
                for start in range(0, wide, COLUMNS):
                    out[row : row + last - first, begin + start : begin + start + COLUMNS] = dot(
                        all_left[:, first:last], all_right[:, start : start + COLUMNS], TN
                    ).astype(jnp.bfloat16)
                row += last - first
        begin += wide


def weight_terms(run, pairs, columns):
    counts = tuple((len(left), len(right)) for left, right in pairs)
    flat = [array for left, right in pairs for array in (*left, *right)]
    total = sum(array.shape[0] for array in pairs[0][0])
    across = sum(right[0].shape[1] for _, right in pairs)
    return run(
        "weight_terms",
        functools.partial(weight_terms_kernel, counts, columns),
        flat,
        [struct((sum(last - first for first, last in spans), across)) for spans in columns],
        24,
        scratch=[
            pltpu.VMEM((total, pairs[0][0][0].shape[1]), jnp.bfloat16),
            pltpu.VMEM((total, max(right[0].shape[1] for _, right in pairs)), jnp.bfloat16),
        ],
    )


def fold_kernel(many, *refs):
    heres, fars, (kept, sent) = refs[:many], refs[many : 2 * many], refs[2 * many :]
    rows = kept.shape[0]
    begin = 0
    for here, far in zip(heres, fars):
        columns = slice(begin, begin + here.shape[1])
        for out, part in ((sent, slice(rows, None)), (kept, slice(0, rows))):
            out[:, columns] = (
                here[part, :].astype(jnp.float32) + far[part, :].astype(jnp.float32)
            ).astype(jnp.bfloat16)
        begin += here.shape[1]


def fold(run, heres, fars):
    across = sum(array.shape[1] for array in heres)
    outs = [struct((heres[0].shape[0] // 2, across))] * 2
    return run("fold", functools.partial(fold_kernel, len(heres)), [*heres, *fars], outs, 12)


def moments_kernel(at, kept, far, weights, first, second, *refs):
    first_new, second_new, step_out, squares = refs[-4:]
    grad = kept[...].astype(jnp.float32) + far[...].astype(jnp.float32)
    weight = weights[...].reshape(grad.shape)
    new_first, new_second, step = adam_part(
        grad, weight, first[...].reshape(grad.shape), second[...].reshape(grad.shape), WEIGHT_DECAY
    )
    for out, value in ((first_new, new_first), (second_new, new_second), (step_out, step)):
        out[...] = value.reshape(out.shape)
    for place, value in enumerate((weight, step)):
        squares[0, place : place + 1, :] = jnp.sum(value * value, axis=0, keepdims=True)


def moments(run, names, layer, kept, far, weights, first, second, before):
    rows, wide = weights.shape[2:]
    spec = pl.BlockSpec((1, 1, rows, wide), lambda n, at: (layer, at[n], 0, 0))
    grad_spec = pl.BlockSpec((rows, wide), lambda n, at: (0, n))
    before = list(before or [])
    return run(
        "moments",
        moments_kernel,
        [jnp.array(names, jnp.int32), kept, far, weights, first, second, *before],
        [struct(weights.shape, jnp.float32)] * 3 + [struct((len(names), 2, wide), jnp.float32)],
        12,
        in_specs=[grad_spec, grad_spec, spec, spec, spec] + [ANY_SPEC] * len(before),
        out_specs=[spec, spec, spec, pl.BlockSpec((1, 2, wide), lambda n, at: (n, 0, 0))],
        grid_spec=(1, (len(names),)),
        aliases={6 + i: i for i in range(len(before))},
    )


def squares_place(index):
    return 8 + index // 8, index % 8 * 128


def squares_kernel(places, vectors, *refs):
    out = refs[-1]
    out[:8, :] = vectors[...]
    out[8:, :] = jnp.zeros_like(out[8:, :])
    for ref, names in zip(refs[:-1], places):
        for index, name in enumerate(names):
            sums = jnp.sum(ref[index], axis=-1, keepdims=True)
            for part in range(2):
                row, lane = squares_place(2 * name + part)
                out[row : row + 1, lane : lane + 128] = jnp.broadcast_to(
                    sums[part : part + 1], (1, 128)
                )


def sums_of(run, places, vectors, *column_sums):
    body = functools.partial(squares_kernel, places)
    return run("sums_of", body, [vectors, *column_sums], [struct((16, D), jnp.float32)], 4)[0]


def apply_kernel(begin, total, weights, step, new, low):
    index = 2 * (6 * pl.program_id(0) + begin + pl.program_id(1))

    numbers = total[8:, :]
    here_row = lax.broadcasted_iota(jnp.int32, numbers.shape, 0) + 8
    here_lane = lax.broadcasted_iota(jnp.int32, numbers.shape, 1)

    def root(at):
        row, lane = squares_place(at)
        chosen = jnp.where((here_row == row) & (here_lane == lane), numbers, 0.0)
        return jnp.sqrt(jnp.sum(jnp.sum(chosen, axis=0, keepdims=True), axis=1, keepdims=True))

    rate = LEARN_RATE * (root(index) / root(index + 1))
    value = weights[...].reshape(weights.shape[2:]) - rate * step[...].reshape(step.shape[2:])
    new[...] = value.reshape(new.shape)
    low[...] = value.astype(jnp.bfloat16).reshape(low.shape)


def apply(run, begin, total, weights, step):
    layers, names, rows, wide = weights.shape
    spec = pl.BlockSpec((1, 1, rows, wide), lambda layer, name: (layer, name, 0, 0))
    return run(
        "apply",
        functools.partial(apply_kernel, begin),
        [total, weights, step],
        [struct(weights.shape, jnp.float32), struct(weights.shape)],
        8,
        in_specs=[pl.BlockSpec(total.shape, lambda layer, name: (0, 0)), spec, spec],
        out_specs=[spec, spec],
        grid_spec=(0, (layers, names)),
    )


def move_columns(run, wides, order, out_rows, back):
    width, kind = wides[0].shape[1], wides[0].dtype
    blocks = order.shape[0]
    block = width // blocks
    if block % 128:
        if back:
            order = jnp.argsort(order)
        columns = (order[:, None] * block + jnp.arange(block)[None, :]).reshape(-1)
        moved = jnp.take(jnp.concatenate(wides, axis=0), columns, axis=1)
        starts = [sum(out_rows[:i]) for i in range(len(out_rows))]
        return [moved[start : start + rows] for start, rows in zip(starts, out_rows)]

    def copy(order_ref, *refs):
        ins, outs = refs[: len(wides)], refs[len(wides) :]
        step = min(ref.shape[0] for ref in refs)
        for row in range(0, sum(out_rows), step):
            source, target, from_row, to_row = ins, outs, row, row
            index = 0
            while from_row >= source[index].shape[0]:
                from_row -= source[index].shape[0]
                index += 1
            source, index = source[index], 0
            while to_row >= target[index].shape[0]:
                to_row -= target[index].shape[0]
                index += 1
            target = target[index]
            for place in range(blocks):
                there = pl.ds(pl.multiple_of(order_ref[place] * block, 128), block)
                here = pl.ds(place * block, block)
                from_columns, to_columns = (here, there) if back else (there, here)
                target[pl.ds(to_row, step), to_columns] = source[pl.ds(from_row, step), from_columns]

    return run(
        "move_columns",
        copy,
        [order, *wides],
        [struct((rows, width), kind) for rows in out_rows],
        6,
        in_specs=[SMEM_SPEC] + [VMEM_SPEC] * len(wides),
    )


class Rows:
    def __init__(self, total, run):
        self.total, self.run = total, run
        self.strides = [1 << bit for bit in reversed(range(total.bit_length() - 1))]

    def order(self):
        places = [0]
        for stride in self.strides:
            places = places + [place ^ stride for place in places]
        return jnp.bitwise_xor(
            jnp.array(places, jnp.int32), lax.axis_index("dp").astype(jnp.int32)
        )

    def swap(self, values, stride):
        return lax.ppermute(
            values, "dp", [(source, source ^ stride) for source in range(self.total)]
        )


class Gather:
    def __init__(self, rows, weights, layer, first, last, spans):
        self.rows, self.run, self.spans = rows, rows.run, spans
        self.what = (weights, layer, first, last)
        self.width = sum(spans)
        self.wholes = [None] * len(spans)

    def far(self):
        self.block = cast_blocks(self.run, *self.what)
        self.there = self.rows.swap(self.block, self.rows.strides[0])

    def near(self):
        for stride in self.rows.strides[1:-1]:
            self.run.settle(self.there)
            self.block = join(self.run, self.block, self.there, 0, self.width)
            self.there = self.rows.swap(self.block, stride)

    def last(self, span=0):
        part = join(self.run, self.block, self.there, sum(self.spans[:span]), self.spans[span])
        self.wholes[span] = (part, self.rows.swap(part, self.rows.strides[-1]))

    def take(self, span=0):
        self.run.settle(self.wholes[span][1])
        return self.wholes[span]

    def early(self):
        self.ahead = self.rows.swap(self.block, self.rows.strides[-1])

    def late(self):
        shape = struct(self.there.shape)
        (self.behind,) = self.run("copy", block_kernel, [self.there], [shape], 6)
        self.behind_there = self.rows.swap(self.behind, self.rows.strides[-1])

    def take_parts(self):
        self.run.settle(self.ahead)
        self.run.settle(self.behind_there)
        return self.block, self.behind, self.ahead, self.behind_there


def stack_kernel(*refs):
    out, begin = refs[-1], 0
    for here, far in zip(refs[:-1:2], refs[1:-1:2]):
        columns = slice(begin, begin + here.shape[1])
        out[: here.shape[0], columns] = here[...]
        out[here.shape[0] :, columns] = far[...]
        begin += here.shape[1]


def stack(run, *pairs):
    flat = [array for pair in pairs for array in pair]
    across = sum(here.shape[1] for here, _ in pairs)
    return run("stack", stack_kernel, flat, [struct((2 * flat[0].shape[0], across))], 12)[0]


class GatherBoth:
    def __init__(self, rows, weights, layer):
        self.ways = [
            Gather(rows, weights, layer, name, name + 1, [weights.shape[3]]) for name in range(2)
        ]
        self.rows, self.run = rows, rows.run

    def near(self):
        for way in self.ways:
            for stride in self.rows.strides[1:-2]:
                way.block = join(self.run, way.block, way.there, 0, way.width)
                way.there = self.rows.swap(way.block, stride)
        self.block = stack(self.run, *[(way.block, way.there) for way in self.ways])
        self.there = self.rows.swap(self.block, self.rows.strides[-2])

    def last(self):
        self.whole = stack(self.run, (self.block, self.there))
        self.there = self.rows.swap(self.whole, self.rows.strides[-1])

    def take(self):
        self.run.settle(self.there)
        return self.whole, self.there


class Reduce:
    def __init__(self, rows):
        self.rows, self.run = rows, rows.run
        self.kept, self.there = [], []

    def send(self, *pairs):
        columns = (((0, D // 2),), ((D // 2, D),))
        keep, away = weight_terms(self.run, pairs, columns)
        self.kept.append(keep)
        self.there.append(self.rows.swap(away, self.rows.strides[-1]))

    def settle(self, group=0):
        self.run.settle(self.there[group])

    def near(self):
        self.pass_on(self.rows.strides[-2])

    def far(self):
        for stride in reversed(self.rows.strides[:-2]):
            self.pass_on(stride)

    def pass_on(self, stride):
        keep, away = fold(self.run, self.kept, self.there)
        self.kept, self.there = [keep], [self.rows.swap(away, stride)]

    def terms(self):
        return self.kept[0], self.there[0]


def core_swap(values_in):
    return lax.ppermute(values_in, "mp", [(0, 1), (1, 0), (2, 3), (3, 2)])


def chip_swap(values_in):
    return lax.ppermute(values_in, "mp", [(0, 2), (2, 0), (1, 3), (3, 1)])


class Exchange:
    def __init__(self, run, mine):
        self.run, (self.mine, parts) = run, mine
        self.beyond = chip_swap(self.mine)
        self.facing = [core_swap(part) for part in parts]

    def near(self):
        return [self.mine, *self.facing]

    def pass_on(self):
        self.relay, parts = cast(self.run, self.beyond)
        self.beyond_facing = [core_swap(part) for part in parts]

    def far(self):
        return [self.relay, *self.beyond_facing]

    def pieces(self):
        return self.near() + self.far()


def collect(run, near_piece, far_piece, weights, begin):
    far_kept, far_sent = narrow(run, far_piece, *weights, begin)
    far_sent = [core_swap(part) for part in far_sent]
    kept, sent = narrow(run, near_piece, *weights, begin)
    there = chip_swap(add_halves(run, far_kept, far_sent, jnp.bfloat16))
    sent = [core_swap(part) for part in sent]
    return add_halves(run, kept, sent, jnp.float32), there


def shards(
    rows_total,
    tokens,
    cotangent,
    segments,
    attention_weights,
    attention_first,
    attention_second,
    dense_weights,
    dense_first,
    dense_second,
    norm_params,
    norm_first,
    norm_second,
):
    layers = attention_weights.shape[0]
    width, wide = attention_weights.shape[3], dense_weights.shape[3]
    run = Order()
    settle = run.settle
    rows = Rows(rows_total, run)
    order = rows.order()
    place = lax.axis_index("mp").astype(jnp.int32).reshape(1)
    mask = crop_mask(segments)
    count = tokens.shape[0]

    inputs_way = Gather(rows, attention_weights, 0, 0, 3, [3 * width])
    output_way = Gather(rows, attention_weights, 0, 3, 4, [width])
    up_way = Gather(rows, dense_weights, 0, 0, 1, [wide])
    down_way = Gather(rows, dense_weights, 0, 1, 2, [wide])
    mixer_way = Gather(rows, attention_weights, 1, 0, 4, [4 * width])
    dense_way = GatherBoth(rows, dense_weights, 1)

    inputs_way.far()
    (params_here,) = move_columns(
        run, [norm_params.reshape(layers * 4, D)], order, [layers * 4], False
    )
    (stream,) = move_columns(run, [tokens], order, [count], False)
    normed = Exchange(run, *norm(run, params_here, 0, stream))
    inputs_way.near()
    output_way.far()
    inputs_way.last()
    up_way.far()
    normed.pass_on()
    (stream_grad,) = move_columns(run, [cotangent], order, [count], False)
    back = Exchange(run, cast(run, stream_grad))
    output_way.near()
    up_way.near()
    output_way.last()
    inputs_map = inputs_way.take()
    projected = [project(run, normed.near(), *inputs_map, 0, 3 * width)]
    projected.append(project(run, normed.far(), *inputs_map, 0, 3 * width))
    down_way.far()
    attended = attend(run, place, mask, projected)
    back.pass_on()
    up_way.last()
    output_map = output_way.take()

    saved = []
    settle(down_way.there)
    mixed = collect(run, attended[0], attended[1], output_map, 0)
    down_way.near()
    down_way.early()
    mixer_way.far()
    dense_way.ways[0].far()
    middle, low = norm(run, params_here, 2, stream, *mixed)
    normed_two = Exchange(run, low)
    down_way.late()
    mixer_way.near()
    settle(dense_way.ways[0].there)
    dense_way.ways[1].far()
    up_map = (*up_way.take(), 0)
    active, slope = [None, None], [None, None]
    active[0], slope[0] = widen(run, normed_two.near(), *up_map, wide)
    settle(mixer_way.there)
    settle(dense_way.ways[1].there)
    settle(down_way.ahead)
    normed_two.pass_on()
    mixer_way.last()
    dense_way.near()
    active[1], slope[1] = widen(run, normed_two.far(), *up_map, wide)
    down_map = (*down_way.take_parts(), 0)
    saved.append((stream, normed, projected, attended, middle, normed_two, active, slope))
    saved[-1] += ((*inputs_map, 0), (*output_map, 0), up_map, down_map)

    widened = collect(run, *active, down_map[:-1], down_map[-1])
    settle(dense_way.there)
    inputs_map = mixer_way.take()
    stream, low = norm(run, params_here, 4, middle, *widened)
    normed = Exchange(run, low)
    dense_way.last()
    projected = [project(run, normed.near(), *inputs_map, 0, 3 * width)]
    normed.pass_on()
    projected.append(project(run, normed.far(), *inputs_map, 0, 3 * width))
    attended = attend(run, place, mask, projected)

    mixed = collect(run, attended[0], attended[1], inputs_map, 3 * width)
    middle, low = norm(run, params_here, 6, stream, *mixed)
    normed_two = Exchange(run, low)
    dense_map = dense_way.take()
    up_map, down_map = (*dense_map, 0), (*dense_map, wide)
    active, slope = [None, None], [None, None]
    active[0], slope[0] = widen(run, normed_two.near(), *up_map, wide)
    grad_hidden = [bend_back(run, back.near(), *down_map, slope[0])]
    normed_two.pass_on()
    active[1], slope[1] = widen(run, normed_two.far(), *up_map, wide)
    saved.append((stream, normed, projected, attended, middle, normed_two, active, slope))
    saved[-1] += ((*inputs_map, 0), (*inputs_map, 3 * width), up_map, down_map)

    mixer_state, dense_state = None, None
    squares, places, vectors = [], [], [None] * (2 * layers)

    def dense_moments(layer, names, terms):
        nonlocal dense_state
        *dense_state, sums = moments(
            run, names, layer, *terms, dense_weights, dense_first, dense_second, dense_state
        )
        squares.append(sums)
        places.append([6 * layer + 4 + name for name in names])

    def mixer_moments(layer, terms):
        nonlocal mixer_state
        *mixer_state, sums = moments(
            run, (0, 1, 2, 3), layer, *terms,
            attention_weights, attention_first, attention_second, mixer_state,
        )
        squares.append(sums)
        places.append([6 * layer + name for name in range(4)])

    def weight_grad(*pairs):
        reduced = Reduce(rows)
        reduced.send(*pairs)
        return reduced

    stream_in, normed, projected, attended, middle, normed_two, active, slope = saved[1][:8]
    inputs_map, output_map, up_map, down_map = saved[1][8:]
    grad_hidden.append(bend_back(run, back.far(), *down_map, slope[1]))
    raised = collect(run, *grad_hidden, up_map[:-1], up_map[-1])
    down_later = weight_grad((back.pieces(), active))
    up_later = weight_grad((normed_two.pieces(), grad_hidden))
    vectors[3], stream_grad, low = norm_back(run, params_here, 6, stream_grad, middle, *raised)
    turned = Exchange(run, low)
    down_later.near()
    grad_attended = [project(run, turned.near(), *output_map, width)]
    turned.pass_on()
    grad_attended.append(project(run, turned.far(), *output_map, width))
    grad_projected = attend_back(run, place, mask, projected, grad_attended)

    down_later.settle()
    lowered = collect(run, *grad_projected, inputs_map[:-1], inputs_map[-1])
    down_later.far()
    up_later.near()
    mixer_later = weight_grad((normed.pieces(), grad_projected), (turned.pieces(), attended))
    vectors[2], stream_grad, low = norm_back(run, params_here, 4, stream_grad, stream_in, *lowered)
    back = Exchange(run, low)

    stream_in, normed, projected, attended, middle, normed_two, active, slope = saved[0][:8]
    inputs_map, output_map, up_map, down_map = saved[0][8:]
    grad_hidden = [bend_back(run, back.near(), *down_map, slope[0])]
    mixer_later.settle()
    up_later.settle()
    down_later.settle()
    back.pass_on()
    grad_hidden.append(bend_back(run, back.far(), *down_map, slope[1]))
    raised = collect(run, *grad_hidden, up_map[:-1], up_map[-1])
    mixer_later.near()
    up_later.far()
    down_grad = weight_grad((back.pieces(), active))
    dense_moments(1, (1,), down_later.terms())
    up_later.settle()
    vectors[1], stream_grad, low = norm_back(run, params_here, 2, stream_grad, middle, *raised)
    turned = Exchange(run, low)
    mixer_later.far()
    up_grad = weight_grad((normed_two.pieces(), grad_hidden))
    grad_attended = [project(run, turned.near(), *output_map, width)]
    dense_moments(1, (0,), up_later.terms())
    down_grad.near()
    mixer_later.settle()
    turned.pass_on()
    grad_attended.append(project(run, turned.far(), *output_map, width))
    grad_projected = attend_back(run, place, mask, projected, grad_attended)

    mixer_grad = weight_grad((normed.pieces(), grad_projected), (turned.pieces(), attended))
    down_grad.settle()
    lowered = collect(run, *grad_projected, inputs_map[:-1], inputs_map[-1])
    down_grad.far()
    up_grad.near()
    mixer_moments(1, mixer_later.terms())
    down_grad.settle()
    vectors[0], stream_grad, low = norm_back(run, params_here, 0, stream_grad, stream_in, *lowered)

    up_grad.far()
    mixer_grad.near()
    all_rows = jnp.concatenate([jnp.sum(sums.reshape(2, 8, D), axis=1) for sums in vectors])
    (all_rows,) = move_columns(run, [all_rows], order, [layers * 4], True)
    dense_moments(0, (1,), down_grad.terms())
    (grad_tokens,) = move_columns(run, [stream_grad], order, [count], True)
    middle, active, down_map = saved[-1][4], saved[-1][6], saved[-1][11]
    widened = collect(run, *active, down_map[:-1], down_map[-1])
    mixer_grad.far()
    dense_moments(0, (0,), up_grad.terms())
    last_stream = add(run, middle, widened[0], jnp.float32, widened[1])
    (outcome,) = move_columns(run, [last_stream], order, [count], True)
    mixer_moments(0, mixer_grad.terms())
    total = sums_of(run, places, all_rows, *squares)
    total = add(run, total, core_swap(total), jnp.float32)
    total = add(run, total, chip_swap(total), jnp.float32)
    for stride in reversed(rows.strides):
        total = add(run, total, rows.swap(total, stride), jnp.float32)
    mixer_new, mixer_copy = apply(run, 0, total, attention_weights, mixer_state[2])
    dense_new, dense_copy = apply(run, 4, total, dense_weights, dense_state[2])

    total_vectors = total[: 4 * layers].reshape(layers, 4, D)
    total_squares = total[8 : 8 + 3].reshape(24, 128)[:, 0].reshape(layers, 6, 2)
    sizes_all = jnp.sqrt(total_squares[:, :, 0])
    moves_all = jnp.sqrt(total_squares[:, :, 1])
    params_first, params_second, params_step = adam_part(
        total_vectors, norm_params, norm_first, norm_second, 0.0
    )
    params_size = jnp.sqrt(jnp.sum(norm_params * norm_params, axis=-1))
    params_move = jnp.sqrt(jnp.sum(params_step * params_step, axis=-1))
    params_new = norm_params - LEARN_RATE * (params_size / params_move)[:, :, None] * params_step
    mixer_entries = float(D * HEADS * HD) ** 0.5
    dense_entries = float(D * FF) ** 0.5
    entry_roots = jnp.array([mixer_entries] * 4 + [dense_entries] * 2, jnp.float32)
    norms = jnp.stack([sizes_all / entry_roots[None, :], moves_all / entry_roots[None, :]], axis=-1)
    second_norm_grad = total_vectors[:, 2:4]
    return (
        outcome,
        grad_tokens,
        mixer_new,
        mixer_state[0],
        mixer_state[1],
        mixer_copy,
        dense_new,
        dense_state[0],
        dense_state[1],
        dense_copy,
        params_new,
        params_first,
        params_second,
        norms,
        second_norm_grad,
    )


def solution(mesh):
    rows_spec = P(("dp", "mp"), None)
    weight_spec = P(None, None, "dp", "mp")
    in_specs = (rows_spec, rows_spec, P("dp")) + (weight_spec,) * 6 + (P(),) * 3
    out_specs = (rows_spec,) * 2 + (weight_spec,) * 8 + (P(),) * 5
    return jax.shard_map(
        functools.partial(shards, mesh.shape["dp"]),
        mesh=mesh,
        in_specs=in_specs,
        out_specs=out_specs,
        check_vma=False,
    )
```

```python
import functools

import jax
import jax.numpy as jnp
from jax import lax
from jax.experimental import pallas as pl
from jax.experimental.pallas import tpu as pltpu
from jax.sharding import PartitionSpec as P

D = 1024
HEADS = 16
HD = 64
FF = 4096
STEP = 10


EPS_NORM = 1e-06
BETA_ONE = 0.9
BETA_TWO = 0.999
ADAM_EPS = 1e-06
WEIGHT_DECAY = 0.01
LEARN_RATE = 0.5
MASKED = -1000000000.0

QUERIES = 128
REACH = 64
WINDOW = QUERIES + 2 * REACH

NT = (((1,), (1,)), ((), ()))
TN = (((0,), (0,)), ((), ()))


VMEM_SPEC = pl.BlockSpec(memory_space=pltpu.VMEM)
SMEM_SPEC = pl.BlockSpec(memory_space=pltpu.SMEM)
ANY_SPEC = pl.BlockSpec(memory_space=pl.ANY)


def struct(shape, kind=jnp.bfloat16):
    return jax.ShapeDtypeStruct(shape, kind)


TOKEN = struct((8, 128), jnp.float32)


class Order:
    def __init__(self):
        self.token, self.earlier = None, []

    def settle(self, value):
        self.earlier = self.earlier + [value]
        return value

    def mark(self):
        self("mark", lambda: None, [], [], 2)

    def __call__(
        self, name, body, ins, outs, room, in_specs=None, out_specs=None, grid_spec=None, scratch=(), aliases=None
    ):
        before = [] if self.token is None else [self.token]
        extra = before + list(self.earlier)
        scalars = 0 if grid_spec is None else grid_spec[0]

        def wrapped(*refs):
            token = refs[len(ins) + len(extra) + len(outs)]
            token[...] = jnp.zeros(TOKEN.shape, TOKEN.dtype)
            refs = refs[: len(ins)] + refs[len(ins) + len(extra) :]
            return body(*refs[: len(ins) + len(outs)], *refs[len(ins) + len(outs) + 1 :])

        if grid_spec is None:
            token_spec = VMEM_SPEC
        else:
            token_spec = pl.BlockSpec(TOKEN.shape, lambda *grid: (0, 0))
        in_specs = (in_specs or [VMEM_SPEC] * len(ins)) + [token_spec] * len(before)
        in_specs = in_specs + [ANY_SPEC] * len(self.earlier)
        out_specs = (out_specs or [VMEM_SPEC] * len(outs)) + [token_spec]
        if grid_spec is None:
            places = dict(in_specs=in_specs, out_specs=out_specs, scratch_shapes=scratch)
        else:
            places = dict(
                grid_spec=pltpu.PrefetchScalarGridSpec(
                    num_scalar_prefetch=scalars,
                    grid=grid_spec[1],
                    in_specs=in_specs,
                    out_specs=out_specs,
                )
            )
        *result, self.token = pl.pallas_call(
            wrapped,
            out_shape=[*outs, TOKEN],
            **places,
            input_output_aliases=aliases or {},
            cost_estimate=pl.CostEstimate(flops=1, bytes_accessed=1, transcendentals=0),
            compiler_params=pltpu.CompilerParams(vmem_limit_bytes=room << 20),
            name=name,
        )(*ins, *extra)
        self.earlier = []
        return result


def add(run, here, far, kind, *more):
    body = functools.partial(sum_kernel, 2 + len(more))
    return run("add", body, [here, far, *more], [struct(here.shape, kind)], 4)[0]


def sum_kernel(count, *refs):
    total = refs[0][...].astype(jnp.float32)
    for ref in refs[1:count]:
        total = total + ref[...].astype(jnp.float32)
    refs[-1][...] = total.astype(refs[-1].dtype)


def add_halves_kernel(kept, first, second, out):
    half = first.shape[0]
    for here, part in ((slice(0, half), first), (slice(half, None), second)):
        total = kept[here, :].astype(jnp.float32) + part[...].astype(jnp.float32)
        out[here, :] = total.astype(out.dtype)


def add_halves(run, kept, parts, kind):
    return run("add", add_halves_kernel, [kept, *parts], [struct(kept.shape, kind)], 6)[0]


def cast_kernel(ref, out, first, second):
    low = ref[...].astype(out.dtype)
    out[...] = low
    first[...] = low[: first.shape[0]]
    second[...] = low[first.shape[0] :]


def cast(run, wide):
    rows, width = wide.shape
    outs = [struct((rows, width)), *[struct((rows // 2, width))] * 2]
    low, *parts = run("cast", cast_kernel, [wide], outs, 6)
    return low, parts


def block_kernel(ref, out):
    out[...] = ref[...].reshape(out.shape).astype(out.dtype)


def cast_blocks(run, weights, layer, first, last):
    rows, wide = weights.shape[2:]
    return run(
        "cast",
        block_kernel,
        [weights],
        [struct((rows, (last - first) * wide))],
        6,
        in_specs=[pl.BlockSpec((1, 1, rows, wide), lambda n: (layer, first + n, 0, 0))],
        out_specs=[pl.BlockSpec((rows, wide), lambda n: (0, n))],
        grid_spec=(0, (last - first,)),
    )[0]


def join_kernel(begin, here, far, out):
    rows = here.shape[0]
    columns = slice(begin, begin + out.shape[1])
    out[:rows, :] = here[:, columns]
    out[rows:, :] = far[:, columns]


def join(run, here, far, begin, width):
    outs = [struct((2 * here.shape[0], width))]
    return run("join", functools.partial(join_kernel, begin), [here, far], outs, 10)[0]


def adam_part(gradient, weight, first, second, decay):
    first_new = BETA_ONE * first + (1.0 - BETA_ONE) * gradient
    second_new = BETA_TWO * second + (1.0 - BETA_TWO) * gradient * gradient
    step_dir = (
        first_new
        / (1.0 - BETA_ONE**STEP)
        / (jnp.sqrt(second_new / (1.0 - BETA_TWO**STEP)) + ADAM_EPS)
        + decay * weight
    )
    return (first_new, second_new, step_dir)


def dot(left, right, dims=(((1,), (0,)), ((), ()))):
    return lax.dot_general(left, right, dims, preferred_element_type=jnp.float32)


def head_lanes(rows, width, value):
    lane_head = lax.broadcasted_iota(jnp.int32, (rows, width), 1) // HD
    return [
        jnp.where(lane_head == head, value, 0.0).astype(jnp.float32) for head in range(width // HD)
    ]


def block_shares(query_wide, keys_in, mask):
    heads_here = query_wide.shape[0] // QUERIES
    scores = dot(query_wide, keys_in, NT).reshape(heads_here, QUERIES, WINDOW)
    scores = jnp.where((mask > 0.5)[None], scores, MASKED)
    powered = jnp.exp(scores - jnp.max(scores, axis=-1, keepdims=True))
    shares = powered * (1.0 / jnp.sum(powered, axis=-1, keepdims=True))
    return shares.reshape(heads_here * QUERIES, WINDOW)


def fold_heads(wide, lanes):
    total = wide[:QUERIES] * lanes[0]
    for head in range(1, len(lanes)):
        total += wide[head * QUERIES : (head + 1) * QUERIES] * lanes[head]
    return total


def places_of(place_ref, pieces, rows):
    half = rows // 2
    found = []
    for piece in range(pieces):
        for core in range(2):
            block = jnp.bitwise_xor(place_ref[0], 2 * piece + core)
            found.append((piece, core * half, pl.multiple_of(block * half, 32)))
    return found


def in_token_order(place_ref, refs, store, start):
    rows = refs[0].shape[0]
    for piece, row, token in places_of(place_ref, len(refs), rows):
        store[pl.ds(token + start, rows // 2), :] = refs[piece][pl.ds(row, rows // 2), :]


def attend_kernel(pieces, place_ref, mask_ref, *refs):
    ins, outs, (all_in, all_out) = refs[:pieces], refs[pieces : 2 * pieces], refs[2 * pieces :]
    count, width = all_out.shape
    all_in[:REACH, :] = jnp.zeros((REACH, 3 * width), jnp.bfloat16)
    all_in[REACH + count :, :] = jnp.zeros((REACH, 3 * width), jnp.bfloat16)
    in_token_order(place_ref, ins, all_in, REACH)
    scaled = [lane.astype(jnp.bfloat16) for lane in head_lanes(QUERIES, width, HD ** (-0.5))]
    plain = head_lanes(QUERIES, width, 1.0)

    @pl.loop(0, count // QUERIES, unroll=count // QUERIES)
    def _(block):
        base = pl.multiple_of(block * QUERIES, QUERIES)
        query = all_in[pl.ds(base + REACH, QUERIES), :width]
        keys_in = all_in[pl.ds(base, WINDOW), width : 2 * width]
        values_in = all_in[pl.ds(base, WINDOW), 2 * width :]
        query_wide = jnp.concatenate([query * lane for lane in scaled], axis=0)
        shares = block_shares(query_wide, keys_in, mask_ref[pl.ds(base, QUERIES), :])
        wide = dot(shares.astype(jnp.bfloat16), values_in)
        all_out[pl.ds(base, QUERIES), :] = fold_heads(wide, plain).astype(jnp.bfloat16)

    rows = outs[0].shape[0]
    for piece, row, token in places_of(place_ref, pieces, rows):
        outs[piece][pl.ds(row, rows // 2), :] = all_out[pl.ds(token, rows // 2), :]


def attend_back_kernel(pieces, place_ref, mask_ref, *refs):
    ins, grads, outs = refs[:pieces], refs[pieces : 2 * pieces], refs[2 * pieces : 3 * pieces]
    all_in, all_grad, query_sum, key_sum, value_sum = refs[3 * pieces :]
    count, width = all_grad.shape
    all_in[:REACH, :] = jnp.zeros((REACH, 3 * width), jnp.bfloat16)
    all_in[REACH + count :, :] = jnp.zeros((REACH, 3 * width), jnp.bfloat16)
    in_token_order(place_ref, ins, all_in, REACH)
    in_token_order(place_ref, grads, all_grad, 0)
    key_sum[...] = jnp.zeros_like(key_sum)
    value_sum[...] = jnp.zeros_like(value_sum)
    scaled = [lane.astype(jnp.bfloat16) for lane in head_lanes(QUERIES, width, HD ** (-0.5))]
    plain_low = [lane.astype(jnp.bfloat16) for lane in head_lanes(QUERIES, width, 1.0)]
    scaled_wide = head_lanes(QUERIES, width, HD ** (-0.5))

    @pl.loop(0, count // QUERIES, unroll=count // QUERIES)
    def _(block):
        base = pl.multiple_of(block * QUERIES, QUERIES)
        query = all_in[pl.ds(base + REACH, QUERIES), :width]
        keys_in = all_in[pl.ds(base, WINDOW), width : 2 * width]
        values_in = all_in[pl.ds(base, WINDOW), 2 * width :]
        grad = all_grad[pl.ds(base, QUERIES), :]
        query_wide = jnp.concatenate([query * lane for lane in scaled], axis=0)
        grad_wide = jnp.concatenate([grad * lane for lane in plain_low], axis=0)
        shares = block_shares(query_wide, keys_in, mask_ref[pl.ds(base, QUERIES), :])
        grad_shares = dot(grad_wide, values_in, NT)
        inner = jnp.sum(grad_shares * shares, axis=-1, keepdims=True)
        grad_scores = (shares * (grad_shares - inner)).astype(jnp.bfloat16)
        query_sum[pl.ds(base, QUERIES), :] = fold_heads(dot(grad_scores, keys_in), scaled_wide)
        key_sum[pl.ds(base, WINDOW), :] += dot(grad_scores, query_wide, TN)
        value_sum[pl.ds(base, WINDOW), :] += dot(shares.astype(jnp.bfloat16), grad_wide, TN)

    rows = outs[0].shape[0]
    for piece, row, token in places_of(place_ref, pieces, rows):
        here, there = pl.ds(row, rows // 2), pl.ds(token + REACH, rows // 2)
        out = outs[piece]
        out[here, :width] = query_sum[pl.ds(token, rows // 2), :].astype(jnp.bfloat16)
        out[here, width : 2 * width] = key_sum[there, :].astype(jnp.bfloat16)
        out[here, 2 * width :] = value_sum[there, :].astype(jnp.bfloat16)


def attend(run, place, mask, projected):
    pieces = len(projected)
    rows, width = projected[0].shape[0], projected[0].shape[1] // 3
    count = rows * pieces
    return run(
        "attend",
        functools.partial(attend_kernel, pieces),
        [place, mask, *projected],
        [struct((rows, width))] * pieces,
        12,
        in_specs=[SMEM_SPEC] + [VMEM_SPEC] * (1 + pieces),
        scratch=[
            pltpu.VMEM((count + 2 * REACH, 3 * width), jnp.bfloat16),
            pltpu.VMEM((count, width), jnp.bfloat16),
        ],
    )


def attend_back(run, place, mask, projected, grads):
    pieces = len(projected)
    rows, width = projected[0].shape[0], projected[0].shape[1] // 3
    count = rows * pieces
    return run(
        "attend_back",
        functools.partial(attend_back_kernel, pieces),
        [place, mask, *projected, *grads],
        [struct((rows, 3 * width))] * pieces,
        20,
        in_specs=[SMEM_SPEC] + [VMEM_SPEC] * (1 + 2 * pieces),
        scratch=[
            pltpu.VMEM((count + 2 * REACH, 3 * width), jnp.bfloat16),
            pltpu.VMEM((count, width), jnp.bfloat16),
            pltpu.VMEM((count, width), jnp.float32),
            pltpu.VMEM((count + 2 * REACH, width), jnp.float32),
            pltpu.VMEM((count + 2 * REACH, width), jnp.float32),
        ],
    )


def crop_mask(segments):
    blocks = segments.shape[0] // QUERIES
    edge = jnp.full((REACH,), -1, segments.dtype)
    padded = jnp.concatenate([edge, segments, edge])
    keys_of = jnp.stack([padded[b * QUERIES : b * QUERIES + WINDOW] for b in range(blocks)])
    same = segments.reshape(blocks, QUERIES)[:, :, None] == keys_of[:, None, :]
    return same.astype(jnp.float32).reshape(blocks * QUERIES, WINDOW)


def row_step(count):
    return 32 if count % 32 == 0 else count


def normalised(value):
    centre = value - jnp.mean(value, axis=-1, keepdims=True)
    spread_of = jnp.mean(centre * centre, axis=-1, keepdims=True)
    scale = lax.rsqrt(spread_of + EPS_NORM)
    return centre * scale, scale


def norm_kernel(row, terms, params_ref, value_ref, *refs):
    *outs, all_low, first_low, second_low = refs[terms:]
    half = first_low.shape[0]
    step = row_step(half)
    gain, shift = params_ref[row : row + 1, :], params_ref[row + 1 : row + 2, :]
    for start in range(0, 2 * half, step):
        here = slice(start, start + step)
        value = value_ref[here, :]
        if terms:
            value = value + refs[0][here, :].astype(jnp.float32)
            value = value + refs[1][here, :].astype(jnp.float32)
            outs[0][here, :] = value
        low = (normalised(value)[0] * gain + shift).astype(jnp.bfloat16)
        all_low[here, :] = low
        if start < half:
            first_low[here, :] = low
        else:
            second_low[start - half : start - half + step, :] = low


def norm(run, params, row, value, *terms):
    wide = [struct(value.shape, jnp.float32)] if terms else []
    low = [struct(value.shape), *[struct((value.shape[0] // 2, value.shape[1]))] * 2]
    body = functools.partial(norm_kernel, row, len(terms))
    *stream, whole, first, second = run("norm", body, [params, value, *terms], wide + low, 6)
    return (*stream, (whole, [first, second]))


def norm_back_kernel(
    row, params_ref, stream_ref, value_ref, near, far, sums_ref, out_ref, all_low, first_low, second_low
):
    half = first_low.shape[0]
    step = row_step(half)
    width = value_ref.shape[1]
    gain = params_ref[row : row + 1, :]
    sums_ref[...] = jnp.zeros_like(sums_ref)
    for start in range(0, 2 * half, step):
        here = slice(start, start + step)
        grad = near[here, :].astype(jnp.float32) + far[here, :].astype(jnp.float32)
        unit, scale = normalised(value_ref[here, :])
        along = grad * unit
        sums_ref[:8, :] += jnp.sum(along.reshape(step // 8, 8, width), axis=0)
        sums_ref[8:, :] += jnp.sum(grad.reshape(step // 8, 8, width), axis=0)
        pushed = grad * gain
        inner = jnp.mean(pushed * unit, axis=-1, keepdims=True)
        term = scale * (pushed - jnp.mean(pushed, axis=-1, keepdims=True) - unit * inner)
        total = stream_ref[here, :] + term
        out_ref[here, :] = total
        low = total.astype(jnp.bfloat16)
        all_low[here, :] = low
        if start < half:
            first_low[here, :] = low
        else:
            second_low[start - half : start - half + step, :] = low


def norm_back(run, params, row, stream_grad, value, *terms):
    sums, stream, whole, first, second = run(
        "norm_back",
        functools.partial(norm_back_kernel, row),
        [params, stream_grad, value, *terms],
        [
            struct((16, value.shape[1]), jnp.float32),
            struct(value.shape, jnp.float32),
            struct(value.shape),
            *[struct((value.shape[0] // 2, value.shape[1]))] * 2,
        ],
        8,
    )
    return sums, stream, (whole, [first, second])


COLUMNS = 256


def by_parts(both, weights, here):
    total, row = 0.0, 0
    for part in weights:
        total = total + dot(both[:, row : row + part.shape[0]], part[:, here])
        row += part.shape[0]
    return total


def project_kernel(begin, many, a, b, c, *refs):
    weights, (out,) = refs[:many], refs[many:]
    both = jnp.concatenate([a[...], b[...], c[...]], axis=0)
    for start in range(0, out.shape[1], COLUMNS):
        here = slice(begin + start, begin + start + COLUMNS)
        out[:, start : start + COLUMNS] = by_parts(both, weights, here).astype(
            jnp.bfloat16
        )


def project(run, piece, *rest):
    *weights, begin, width = rest
    outs = [struct((sum(part.shape[0] for part in piece), width))]
    body = functools.partial(project_kernel, begin, len(weights))
    return run("project", body, [*piece, *weights], outs, 14)[0]


def widen_kernel(begin, many, a, b, c, *refs):
    weights, (active, slope) = refs[:many], refs[many:]
    both = jnp.concatenate([a[...], b[...], c[...]], axis=0)
    for start in range(0, active.shape[1], COLUMNS):
        here = slice(start, start + COLUMNS)
        hidden = by_parts(both, weights, slice(begin + start, begin + start + COLUMNS))
        below = 0.5 + 0.5 * lax.erf(hidden * (0.5**0.5))
        density = jnp.exp(-0.5 * hidden * hidden) * 0.3989422804014327
        active[:, here] = (hidden * below).astype(jnp.bfloat16)
        slope[:, here] = (below + hidden * density).astype(jnp.bfloat16)


def widen(run, piece, *rest):
    *weights, begin, width = rest
    outs = [struct((sum(part.shape[0] for part in piece), width))] * 2
    body = functools.partial(widen_kernel, begin, len(weights))
    return run("widen", body, [*piece, *weights], outs, 14)


def bend_kernel(begin, many, a, b, c, *refs):
    weights, (slope, out) = refs[:many], refs[many:]
    both = jnp.concatenate([a[...], b[...], c[...]], axis=0)
    for start in range(0, out.shape[1], COLUMNS):
        here = slice(start, start + COLUMNS)
        grad = by_parts(both, weights, slice(begin + start, begin + start + COLUMNS))
        out[:, here] = (grad * slope[:, here].astype(jnp.float32)).astype(jnp.bfloat16)


def bend_back(run, piece, *rest):
    *weights, begin, slope = rest
    body = functools.partial(bend_kernel, begin, len(weights))
    return run("bend_back", body, [*piece, *weights, slope], [struct(slope.shape)], 14)[0]


def narrow_kernel(begin, many, piece, *refs):
    weights_parts, (kept, sent, sent_more) = refs[:many], refs[many:]
    half = kept.shape[0]
    part = sent.shape[0]
    columns = slice(begin, begin + piece.shape[1])
    for index, weights in enumerate(weights_parts):
        for start in range(0, weights.shape[0], COLUMNS):
            there = index * weights.shape[0] + start
            here = slice(there, there + COLUMNS)
            rows = weights[start : start + COLUMNS, columns]
            both = dot(piece[...], rows, NT).astype(jnp.bfloat16)
            kept[:, here] = both[:half]
            sent[:, here] = both[half : half + part]
            sent_more[:, here] = both[half + part :]


def narrow(run, piece, *rest):
    *weights, begin = rest
    rows, width = piece.shape[0] // 2, sum(part.shape[0] for part in weights)
    outs = [struct((rows, width)), *[struct((rows // 2, width))] * 2]
    body = functools.partial(narrow_kernel, begin, len(weights))
    kept, *sent = run("narrow", body, [piece, *weights], outs, 14)
    return kept, sent


def weight_terms_kernel(counts, columns, *refs):
    ins = refs[: sum(map(sum, counts))]
    kept, sent, all_left, all_right = refs[len(ins) :]
    begin = 0
    for lefts, rights in counts:
        left, right, ins = ins[:lefts], ins[lefts : lefts + rights], ins[lefts + rights :]
        for store, parts in ((all_left, left), (all_right, right)):
            row = 0
            for part in parts:
                store[row : row + part.shape[0], : part.shape[1]] = part[...]
                row += part.shape[0]
        wide = right[0].shape[1]
        for out, spans in zip((sent, kept), columns[::-1]):
            row = 0
            for first, last in spans:
                for start in range(0, wide, COLUMNS):
                    out[row : row + last - first, begin + start : begin + start + COLUMNS] = dot(
                        all_left[:, first:last], all_right[:, start : start + COLUMNS], TN
                    ).astype(jnp.bfloat16)
                row += last - first
        begin += wide


def weight_terms(run, pairs, columns):
    counts = tuple((len(left), len(right)) for left, right in pairs)
    flat = [array for left, right in pairs for array in (*left, *right)]
    total = sum(array.shape[0] for array in pairs[0][0])
    across = sum(right[0].shape[1] for _, right in pairs)
    return run(
        "weight_terms",
        functools.partial(weight_terms_kernel, counts, columns),
        flat,
        [struct((sum(last - first for first, last in spans), across)) for spans in columns],
        24,
        scratch=[
            pltpu.VMEM((total, pairs[0][0][0].shape[1]), jnp.bfloat16),
            pltpu.VMEM((total, max(right[0].shape[1] for _, right in pairs)), jnp.bfloat16),
        ],
    )


def fold_kernel(many, *refs):
    heres, fars, (kept, sent) = refs[:many], refs[many : 2 * many], refs[2 * many :]
    rows = kept.shape[0]
    begin = 0
    for here, far in zip(heres, fars):
        columns = slice(begin, begin + here.shape[1])
        for out, part in ((sent, slice(rows, None)), (kept, slice(0, rows))):
            out[:, columns] = (
                here[part, :].astype(jnp.float32) + far[part, :].astype(jnp.float32)
            ).astype(jnp.bfloat16)
        begin += here.shape[1]


def fold(run, heres, fars):
    across = sum(array.shape[1] for array in heres)
    outs = [struct((heres[0].shape[0] // 2, across))] * 2
    return run("fold", functools.partial(fold_kernel, len(heres)), [*heres, *fars], outs, 12)


def moments_kernel(at, kept, far, weights, first, second, *refs):
    first_new, second_new, step_out, squares = refs[-4:]
    wide = weights.shape[3]
    for name in range(weights.shape[1]):
        here = slice(name * wide, name * wide + wide)
        grad = kept[:, here].astype(jnp.float32) + far[:, here].astype(jnp.float32)
        weight = weights[0, name]
        new_first, new_second, step = adam_part(
            grad, weight, first[0, name], second[0, name], WEIGHT_DECAY
        )
        for out, value in ((first_new, new_first), (second_new, new_second), (step_out, step)):
            out[0, name] = value
        for place, value in enumerate((weight, step)):
            squares[name, place : place + 1, :] = jnp.sum(value * value, axis=0, keepdims=True)


def moments(run, names, layer, kept, far, weights, first, second, before):
    rows, wide = weights.shape[2:]
    many = len(names) if tuple(names) == tuple(range(weights.shape[1])) else 1
    spec = pl.BlockSpec((1, many, rows, wide), lambda n, at: (layer, at[n], 0, 0))
    grad_spec = pl.BlockSpec((rows, many * wide), lambda n, at: (0, n))
    before = list(before or [])
    return run(
        "moments",
        moments_kernel,
        [jnp.array(names, jnp.int32), kept, far, weights, first, second, *before],
        [struct(weights.shape, jnp.float32)] * 3 + [struct((len(names), 2, wide), jnp.float32)],
        12,
        in_specs=[grad_spec, grad_spec, spec, spec, spec] + [ANY_SPEC] * len(before),
        out_specs=[spec, spec, spec, pl.BlockSpec((many, 2, wide), lambda n, at: (n, 0, 0))],
        grid_spec=(1, (len(names) // many,)),
        aliases={6 + i: i for i in range(len(before))},
    )


def squares_place(index):
    return 8 + index // 8, index % 8 * 128


def squares_kernel(places, vectors, *refs):
    out = refs[-1]
    out[:8, :] = vectors[...]
    out[8:, :] = jnp.zeros_like(out[8:, :])
    for ref, names in zip(refs[:-1], places):
        for index, name in enumerate(names):
            sums = jnp.sum(ref[index], axis=-1, keepdims=True)
            for part in range(2):
                row, lane = squares_place(2 * name + part)
                out[row : row + 1, lane : lane + 128] = jnp.broadcast_to(
                    sums[part : part + 1], (1, 128)
                )


def sums_of(run, places, vectors, *column_sums):
    body = functools.partial(squares_kernel, places)
    return run("sums_of", body, [vectors, *column_sums], [struct((16, D), jnp.float32)], 4)[0]


def apply_kernel(begin, total, weights, step, new, low):
    first = 2 * (6 * pl.program_id(0) + begin)

    numbers = total[8:, :]
    here_row = lax.broadcasted_iota(jnp.int32, numbers.shape, 0) + 8
    here_lane = lax.broadcasted_iota(jnp.int32, numbers.shape, 1)

    def root(at):
        row, lane = squares_place(at)
        chosen = jnp.where((here_row == row) & (here_lane == lane), numbers, 0.0)
        return jnp.sqrt(jnp.sum(jnp.sum(chosen, axis=0, keepdims=True), axis=1, keepdims=True))

    for name in range(weights.shape[1]):
        rate = LEARN_RATE * (root(first + 2 * name) / root(first + 2 * name + 1))
        value = weights[0, name] - rate * step[0, name]
        new[0, name] = value
        low[0, name] = value.astype(jnp.bfloat16)


def apply(run, begin, total, weights, step):
    layers, names, rows, wide = weights.shape
    spec = pl.BlockSpec((1, names, rows, wide), lambda layer: (layer, 0, 0, 0))
    return run(
        "apply",
        functools.partial(apply_kernel, begin),
        [total, weights, step],
        [struct(weights.shape, jnp.float32), struct(weights.shape)],
        16,
        in_specs=[pl.BlockSpec(total.shape, lambda layer: (0, 0)), spec, spec],
        out_specs=[spec, spec],
        grid_spec=(0, (layers,)),
    )


def move_columns(run, wides, order, out_rows, back):
    width, kind = wides[0].shape[1], wides[0].dtype
    blocks = order.shape[0]
    block = width // blocks
    if block % 128:
        if back:
            order = jnp.argsort(order)
        columns = (order[:, None] * block + jnp.arange(block)[None, :]).reshape(-1)
        moved = jnp.take(jnp.concatenate(wides, axis=0), columns, axis=1)
        starts = [sum(out_rows[:i]) for i in range(len(out_rows))]
        return [moved[start : start + rows] for start, rows in zip(starts, out_rows)]

    def copy(order_ref, *refs):
        ins, outs = refs[: len(wides)], refs[len(wides) :]
        step = min(ref.shape[0] for ref in refs)
        for row in range(0, sum(out_rows), step):
            source, target, from_row, to_row = ins, outs, row, row
            index = 0
            while from_row >= source[index].shape[0]:
                from_row -= source[index].shape[0]
                index += 1
            source, index = source[index], 0
            while to_row >= target[index].shape[0]:
                to_row -= target[index].shape[0]
                index += 1
            target = target[index]
            for place in range(blocks):
                there = pl.ds(pl.multiple_of(order_ref[place] * block, 128), block)
                here = pl.ds(place * block, block)
                from_columns, to_columns = (here, there) if back else (there, here)
                target[pl.ds(to_row, step), to_columns] = source[pl.ds(from_row, step), from_columns]

    return run(
        "move_columns",
        copy,
        [order, *wides],
        [struct((rows, width), kind) for rows in out_rows],
        6,
        in_specs=[SMEM_SPEC] + [VMEM_SPEC] * len(wides),
    )


class Rows:
    def __init__(self, total, run):
        self.total, self.run = total, run
        self.strides = [1 << bit for bit in reversed(range(total.bit_length() - 1))]

    def order(self):
        places = [0]
        for stride in self.strides:
            places = places + [place ^ stride for place in places]
        return jnp.bitwise_xor(
            jnp.array(places, jnp.int32), lax.axis_index("dp").astype(jnp.int32)
        )

    def swap(self, values, stride):
        return lax.ppermute(
            values, "dp", [(source, source ^ stride) for source in range(self.total)]
        )


class Gather:
    def __init__(self, rows, weights, layer, first, last, spans):
        self.rows, self.run, self.spans = rows, rows.run, spans
        self.what = (weights, layer, first, last)
        self.width = sum(spans)
        self.wholes = [None] * len(spans)

    def far(self):
        self.block = cast_blocks(self.run, *self.what)
        self.there = self.rows.swap(self.block, self.rows.strides[0])

    def near(self):
        for stride in self.rows.strides[1:-1]:
            self.run.settle(self.there)
            self.block = join(self.run, self.block, self.there, 0, self.width)
            self.there = self.rows.swap(self.block, stride)

    def last(self, span=0):
        part = join(self.run, self.block, self.there, sum(self.spans[:span]), self.spans[span])
        self.wholes[span] = (part, self.rows.swap(part, self.rows.strides[-1]))

    def take(self, span=0):
        self.run.settle(self.wholes[span][1])
        return self.wholes[span]

    def early(self):
        self.ahead = self.rows.swap(self.block, self.rows.strides[-1])

    def late(self):
        shape = struct(self.there.shape)
        (self.behind,) = self.run("copy", block_kernel, [self.there], [shape], 6)
        self.behind_there = self.rows.swap(self.behind, self.rows.strides[-1])

    def take_parts(self):
        self.run.settle(self.ahead)
        self.run.settle(self.behind_there)
        return self.block, self.behind, self.ahead, self.behind_there


def stack_kernel(*refs):
    out, begin = refs[-1], 0
    for here, far in zip(refs[:-1:2], refs[1:-1:2]):
        columns = slice(begin, begin + here.shape[1])
        out[: here.shape[0], columns] = here[...]
        out[here.shape[0] :, columns] = far[...]
        begin += here.shape[1]


def stack(run, *pairs):
    flat = [array for pair in pairs for array in pair]
    across = sum(here.shape[1] for here, _ in pairs)
    return run("stack", stack_kernel, flat, [struct((2 * flat[0].shape[0], across))], 12)[0]


class GatherBoth:
    def __init__(self, rows, weights, layer):
        self.ways = [
            Gather(rows, weights, layer, name, name + 1, [weights.shape[3]]) for name in range(2)
        ]
        self.rows, self.run = rows, rows.run

    def near(self):
        for way in self.ways:
            for stride in self.rows.strides[1:-2]:
                way.block = join(self.run, way.block, way.there, 0, way.width)
                way.there = self.rows.swap(way.block, stride)
        self.block = stack(self.run, *[(way.block, way.there) for way in self.ways])
        self.there = self.rows.swap(self.block, self.rows.strides[-2])

    def last(self):
        self.whole = stack(self.run, (self.block, self.there))
        self.there = self.rows.swap(self.whole, self.rows.strides[-1])

    def take(self):
        self.run.settle(self.there)
        return self.whole, self.there


class Reduce:
    def __init__(self, rows):
        self.rows, self.run = rows, rows.run
        self.kept, self.there = [], []

    def send(self, *pairs):
        columns = (((0, D // 2),), ((D // 2, D),))
        keep, away = weight_terms(self.run, pairs, columns)
        self.kept.append(keep)
        self.there.append(self.rows.swap(away, self.rows.strides[-1]))

    def settle(self, group=0):
        self.run.settle(self.there[group])

    def near(self):
        self.pass_on(self.rows.strides[-2])

    def far(self):
        for stride in reversed(self.rows.strides[:-2]):
            self.pass_on(stride)

    def pass_on(self, stride):
        keep, away = fold(self.run, self.kept, self.there)
        self.kept, self.there = [keep], [self.rows.swap(away, stride)]

    def terms(self):
        return self.kept[0], self.there[0]


def core_swap(values_in):
    return lax.ppermute(values_in, "mp", [(0, 1), (1, 0), (2, 3), (3, 2)])


def chip_swap(values_in):
    return lax.ppermute(values_in, "mp", [(0, 2), (2, 0), (1, 3), (3, 1)])


class Exchange:
    def __init__(self, run, mine):
        self.run, (self.mine, parts) = run, mine
        self.beyond = chip_swap(self.mine)
        self.facing = [core_swap(part) for part in parts]

    def near(self):
        return [self.mine, *self.facing]

    def pass_on(self):
        self.relay, parts = cast(self.run, self.beyond)
        self.beyond_facing = [core_swap(part) for part in parts]

    def far(self):
        return [self.relay, *self.beyond_facing]

    def pieces(self):
        return self.near() + self.far()


def collect(run, near_piece, far_piece, weights, begin):
    far_kept, far_sent = narrow(run, far_piece, *weights, begin)
    far_sent = [core_swap(part) for part in far_sent]
    kept, sent = narrow(run, near_piece, *weights, begin)
    there = chip_swap(add_halves(run, far_kept, far_sent, jnp.bfloat16))
    sent = [core_swap(part) for part in sent]
    return add_halves(run, kept, sent, jnp.float32), there


def shards(
    rows_total,
    tokens,
    cotangent,
    segments,
    attention_weights,
    attention_first,
    attention_second,
    dense_weights,
    dense_first,
    dense_second,
    norm_params,
    norm_first,
    norm_second,
):
    layers = attention_weights.shape[0]
    width, wide = attention_weights.shape[3], dense_weights.shape[3]
    run = Order()
    settle = run.settle
    rows = Rows(rows_total, run)
    order = rows.order()
    place = lax.axis_index("mp").astype(jnp.int32).reshape(1)
    mask = crop_mask(segments)
    count = tokens.shape[0]

    inputs_way = Gather(rows, attention_weights, 0, 0, 3, [3 * width])
    output_way = Gather(rows, attention_weights, 0, 3, 4, [width])
    up_way = Gather(rows, dense_weights, 0, 0, 1, [wide])
    down_way = Gather(rows, dense_weights, 0, 1, 2, [wide])
    mixer_way = Gather(rows, attention_weights, 1, 0, 4, [4 * width])
    dense_way = GatherBoth(rows, dense_weights, 1)

    inputs_way.far()
    (params_here,) = move_columns(
        run, [norm_params.reshape(layers * 4, D)], order, [layers * 4], False
    )
    (stream,) = move_columns(run, [tokens], order, [count], False)
    normed = Exchange(run, *norm(run, params_here, 0, stream))
    inputs_way.near()
    output_way.far()
    inputs_way.last()
    up_way.far()
    normed.pass_on()
    (stream_grad,) = move_columns(run, [cotangent], order, [count], False)
    back = Exchange(run, cast(run, stream_grad))
    output_way.near()
    up_way.near()
    output_way.last()
    inputs_map = inputs_way.take()
    projected = [project(run, normed.near(), *inputs_map, 0, 3 * width)]
    projected.append(project(run, normed.far(), *inputs_map, 0, 3 * width))
    down_way.far()
    attended = attend(run, place, mask, projected)
    back.pass_on()
    up_way.last()
    output_map = output_way.take()

    saved = []
    settle(down_way.there)
    mixed = collect(run, attended[0], attended[1], output_map, 0)
    down_way.near()
    down_way.early()
    mixer_way.far()
    dense_way.ways[0].far()
    middle, low = norm(run, params_here, 2, stream, *mixed)
    normed_two = Exchange(run, low)
    down_way.late()
    mixer_way.near()
    settle(dense_way.ways[0].there)
    dense_way.ways[1].far()
    up_map = (*up_way.take(), 0)
    active, slope = [None, None], [None, None]
    active[0], slope[0] = widen(run, normed_two.near(), *up_map, wide)
    settle(mixer_way.there)
    settle(dense_way.ways[1].there)
    settle(down_way.ahead)
    normed_two.pass_on()
    mixer_way.last()
    dense_way.near()
    active[1], slope[1] = widen(run, normed_two.far(), *up_map, wide)
    down_map = (*down_way.take_parts(), 0)
    saved.append((stream, normed, projected, attended, middle, normed_two, active, slope))
    saved[-1] += ((*inputs_map, 0), (*output_map, 0), up_map, down_map)

    widened = collect(run, *active, down_map[:-1], down_map[-1])
    settle(dense_way.there)
    inputs_map = mixer_way.take()
    stream, low = norm(run, params_here, 4, middle, *widened)
    normed = Exchange(run, low)
    dense_way.last()
    projected = [project(run, normed.near(), *inputs_map, 0, 3 * width)]
    normed.pass_on()
    projected.append(project(run, normed.far(), *inputs_map, 0, 3 * width))
    attended = attend(run, place, mask, projected)

    mixed = collect(run, attended[0], attended[1], inputs_map, 3 * width)
    middle, low = norm(run, params_here, 6, stream, *mixed)
    normed_two = Exchange(run, low)
    dense_map = dense_way.take()
    up_map, down_map = (*dense_map, 0), (*dense_map, wide)
    active, slope = [None, None], [None, None]
    active[0], slope[0] = widen(run, normed_two.near(), *up_map, wide)
    grad_hidden = [bend_back(run, back.near(), *down_map, slope[0])]
    normed_two.pass_on()
    active[1], slope[1] = widen(run, normed_two.far(), *up_map, wide)
    saved.append((stream, normed, projected, attended, middle, normed_two, active, slope))
    saved[-1] += ((*inputs_map, 0), (*inputs_map, 3 * width), up_map, down_map)

    mixer_state, dense_state = None, None
    squares, places, vectors = [], [], [None] * (2 * layers)

    def dense_moments(layer, names, terms):
        nonlocal dense_state
        *dense_state, sums = moments(
            run, names, layer, *terms, dense_weights, dense_first, dense_second, dense_state
        )
        squares.append(sums)
        places.append([6 * layer + 4 + name for name in names])

    def mixer_moments(layer, terms):
        nonlocal mixer_state
        *mixer_state, sums = moments(
            run, (0, 1, 2, 3), layer, *terms,
            attention_weights, attention_first, attention_second, mixer_state,
        )
        squares.append(sums)
        places.append([6 * layer + name for name in range(4)])

    def weight_grad(*pairs):
        reduced = Reduce(rows)
        reduced.send(*pairs)
        return reduced

    stream_in, normed, projected, attended, middle, normed_two, active, slope = saved[1][:8]
    inputs_map, output_map, up_map, down_map = saved[1][8:]
    grad_hidden.append(bend_back(run, back.far(), *down_map, slope[1]))
    raised = collect(run, *grad_hidden, up_map[:-1], up_map[-1])
    down_later = weight_grad((back.pieces(), active))
    up_later = weight_grad((normed_two.pieces(), grad_hidden))
    vectors[3], stream_grad, low = norm_back(run, params_here, 6, stream_grad, middle, *raised)
    turned = Exchange(run, low)
    down_later.near()
    grad_attended = [project(run, turned.near(), *output_map, width)]
    turned.pass_on()
    grad_attended.append(project(run, turned.far(), *output_map, width))
    grad_projected = attend_back(run, place, mask, projected, grad_attended)

    down_later.settle()
    lowered = collect(run, *grad_projected, inputs_map[:-1], inputs_map[-1])
    down_later.far()
    up_later.near()
    mixer_later = weight_grad((normed.pieces(), grad_projected), (turned.pieces(), attended))
    vectors[2], stream_grad, low = norm_back(run, params_here, 4, stream_grad, stream_in, *lowered)
    back = Exchange(run, low)

    stream_in, normed, projected, attended, middle, normed_two, active, slope = saved[0][:8]
    inputs_map, output_map, up_map, down_map = saved[0][8:]
    grad_hidden = [bend_back(run, back.near(), *down_map, slope[0])]
    mixer_later.settle()
    up_later.settle()
    down_later.settle()
    back.pass_on()
    grad_hidden.append(bend_back(run, back.far(), *down_map, slope[1]))
    raised = collect(run, *grad_hidden, up_map[:-1], up_map[-1])
    mixer_later.near()
    up_later.far()
    down_grad = weight_grad((back.pieces(), active))
    dense_moments(1, (1,), down_later.terms())
    up_later.settle()
    vectors[1], stream_grad, low = norm_back(run, params_here, 2, stream_grad, middle, *raised)
    turned = Exchange(run, low)
    mixer_later.far()
    up_grad = weight_grad((normed_two.pieces(), grad_hidden))
    grad_attended = [project(run, turned.near(), *output_map, width)]
    dense_moments(1, (0,), up_later.terms())
    down_grad.near()
    mixer_later.settle()
    turned.pass_on()
    grad_attended.append(project(run, turned.far(), *output_map, width))
    grad_projected = attend_back(run, place, mask, projected, grad_attended)

    mixer_grad = weight_grad((normed.pieces(), grad_projected), (turned.pieces(), attended))
    down_grad.settle()
    lowered = collect(run, *grad_projected, inputs_map[:-1], inputs_map[-1])
    down_grad.far()
    up_grad.near()
    mixer_moments(1, mixer_later.terms())
    down_grad.settle()
    vectors[0], stream_grad, low = norm_back(run, params_here, 0, stream_grad, stream_in, *lowered)

    up_grad.far()
    mixer_grad.near()
    all_rows = jnp.concatenate([jnp.sum(sums.reshape(2, 8, D), axis=1) for sums in vectors])
    (all_rows,) = move_columns(run, [all_rows], order, [layers * 4], True)
    dense_moments(0, (1,), down_grad.terms())
    (grad_tokens,) = move_columns(run, [stream_grad], order, [count], True)
    middle, active, down_map = saved[-1][4], saved[-1][6], saved[-1][11]
    widened = collect(run, *active, down_map[:-1], down_map[-1])
    mixer_grad.far()
    dense_moments(0, (0,), up_grad.terms())
    last_stream = add(run, middle, widened[0], jnp.float32, widened[1])
    (outcome,) = move_columns(run, [last_stream], order, [count], True)
    mixer_moments(0, mixer_grad.terms())
    total = sums_of(run, places, all_rows, *squares)
    total = add(run, total, core_swap(total), jnp.float32)
    total = add(run, total, chip_swap(total), jnp.float32)
    for stride in reversed(rows.strides):
        total = add(run, total, rows.swap(total, stride), jnp.float32)
    mixer_new, mixer_copy = apply(run, 0, total, attention_weights, mixer_state[2])
    dense_new, dense_copy = apply(run, 4, total, dense_weights, dense_state[2])

    total_vectors = total[: 4 * layers].reshape(layers, 4, D)
    total_squares = total[8 : 8 + 3].reshape(24, 128)[:, 0].reshape(layers, 6, 2)
    sizes_all = jnp.sqrt(total_squares[:, :, 0])
    moves_all = jnp.sqrt(total_squares[:, :, 1])
    params_first, params_second, params_step = adam_part(
        total_vectors, norm_params, norm_first, norm_second, 0.0
    )
    params_size = jnp.sqrt(jnp.sum(norm_params * norm_params, axis=-1))
    params_move = jnp.sqrt(jnp.sum(params_step * params_step, axis=-1))
    params_new = norm_params - LEARN_RATE * (params_size / params_move)[:, :, None] * params_step
    mixer_entries = float(D * HEADS * HD) ** 0.5
    dense_entries = float(D * FF) ** 0.5
    entry_roots = jnp.array([mixer_entries] * 4 + [dense_entries] * 2, jnp.float32)
    norms = jnp.stack([sizes_all / entry_roots[None, :], moves_all / entry_roots[None, :]], axis=-1)
    second_norm_grad = total_vectors[:, 2:4]
    return (
        outcome,
        grad_tokens,
        mixer_new,
        mixer_state[0],
        mixer_state[1],
        mixer_copy,
        dense_new,
        dense_state[0],
        dense_state[1],
        dense_copy,
        params_new,
        params_first,
        params_second,
        norms,
        second_norm_grad,
    )


def solution(mesh):
    rows_spec = P(("dp", "mp"), None)
    weight_spec = P(None, None, "dp", "mp")
    in_specs = (rows_spec, rows_spec, P("dp")) + (weight_spec,) * 6 + (P(),) * 3
    out_specs = (rows_spec,) * 2 + (weight_spec,) * 8 + (P(),) * 5
    return jax.shard_map(
        functools.partial(shards, mesh.shape["dp"]),
        mesh=mesh,
        in_specs=in_specs,
        out_specs=out_specs,
        check_vma=False,
    )
```
